32 devices in a mesh: dp: 16 (over z, y, core), tensor: 2 (over x).
Axes of the slice: x: 2, y: 2, z: 4, core: 2. Of those that a mesh axis runs over, the one named last changes fastest.
Arguments:
- tokens: bfloat16 [81920, 512], P(('dp', 'tensor')), may hold values from -6 to 6
- qkv_weight: bfloat16 [3, 512, 512], P(None, None, 'tensor'), may hold values from -0.25 to 0.25
- qv_bias: bfloat16 [2, 512], P(None, 'tensor'), may hold values from -3 to 3
- out_weight: bfloat16 [512, 512], P('tensor'), may hold values from -1 to 1
- out_bias: float32 [512], replicated, may hold values from -2 to 2
- norm_one_gain: float32 [512], replicated, may hold values from 0.5 to 1.5
- norm_one_shift: float32 [512], replicated, may hold values from -2 to 2
- up_weight: bfloat16 [512, 2048], P(None, 'tensor'), may hold values from -0.25 to 0.25
- up_bias: bfloat16 [2048], P('tensor'), may hold values from -3 to 3
- down_weight: bfloat16 [2048, 512], P('tensor'), may hold values from -0.1875 to 0.1875
- down_bias: float32 [512], replicated, may hold values from -2 to 2
- norm_two_gain: float32 [512], replicated, may hold values from 0.5 to 1.5
- norm_two_shift: float32 [512], replicated, may hold values from -2 to 2
- out_grad: bfloat16 [81920, 512], P(('dp', 'tensor')), may hold values from -6 to 6
- lengths: int32 [512], P('dp'), may hold values from 95 to 160, as said below
Outputs:
- layer_out: bfloat16 [81920, 512], P(('dp', 'tensor'))
- grad_tokens: bfloat16 [81920, 512], P(('dp', 'tensor'))
- grad_qkv_weight: float32 [3, 512, 512], P(None, None, 'tensor')
- grad_qv_bias: float32 [2, 512], P(None, 'tensor')
- grad_out_weight: float32 [512, 512], P('tensor')
- grad_out_bias: float32 [512], replicated
- grad_norm_one_gain: float32 [512], replicated
- grad_norm_one_shift: float32 [512], replicated
- grad_up_weight: float32 [512, 2048], P(None, 'tensor')
- grad_up_bias: float32 [2048], P('tensor')
- grad_down_weight: float32 [2048, 512], P('tensor')
- grad_down_bias: float32 [512], replicated
- grad_norm_two_gain: float32 [512], replicated
- grad_norm_two_shift: float32 [512], replicated
The draws below stay inside these ranges and needn't reach their ends.
Inputs may be any that keep to these rules, and one draw needn't show every extreme that they name: `lengths`: each run of 32 consecutive chains (the chains of one dp index) forms a group; the first chain of every group has exactly 160 residues and the second has the group's fewest.
All inputs are finite; a program needn't handle non-finite values.
Results may differ from the reference program's by a relative error of at most 0.02.
Values may be sent and summed in bfloat16 or wider, within the bound.
A program may use at most 256 MiB of HBM per device.

```python
import math
import jax
import jax.numpy as jnp
from jax import lax

D = 512
HEADS = 8
HDIM = 64
FF = 2048
LMAX = 160
LMIN = 95
SEQ_DEV = 32
CHAINS = 512
TOKENS = 81920


def draw_lengths(key, part):
    groups = CHAINS // SEQ_DEV
    key_low, key_each = jax.random.split(key)
    floors = LMIN + jax.random.randint(key_low, (groups,), 0, (LMAX - LMIN) // 2 + 1)
    floors = floors.at[0].set(LMIN)
    raw = jax.random.randint(key_each, (groups, SEQ_DEV), 0, 1 << 20)
    picked = floors[:, None] + raw % (LMAX + 1 - floors[:, None])
    picked = picked.at[:, 0].set(LMAX)
    picked = picked.at[:, 1].set(floors)
    return picked.reshape(CHAINS).astype(jnp.int32)


def level_of(stream_key, shape, cuts, smallest, largest):
    factor_of = 1.0
    for dim, blocks in cuts:
        steps = jax.random.uniform(jax.random.fold_in(jax.random.fold_in(stream_key, 6), dim), (blocks,), jnp.float32, smallest / len(cuts), largest / len(cuts))
        factor_of = factor_of * jnp.repeat(jnp.exp(steps), shape[dim] // blocks).reshape((-1,) + (1,) * (len(shape) - 1 - dim))
    return factor_of


def centred(stream_key, shape, scale, limit, cuts=(), kind=jnp.bfloat16):
    level = level_of(stream_key, shape, cuts, -0.22, 0.18) if cuts else 1.0
    entries = jax.random.normal(stream_key, shape, jnp.float32) * scale * level
    return jnp.minimum(jnp.maximum(entries, -limit), limit).astype(kind)


def setup_inputs(seed: int = 0) -> dict:
    key_list = jax.random.split(jax.random.key(seed), 16)
    tokens = centred(key_list[0], (TOKENS, D), 1.0, 6.0, ((0, 32),))
    qkv_weight = centred(key_list[1], (3, D, D), D ** -0.5, 0.25, ((2, 2),))
    qv_bias = centred(key_list[2], (2, D), 0.5, 3.0, ((1, 2),))
    out_weight = centred(key_list[3], (D, D), (D // 16) ** -0.5, 1.0, ((0, 2),))
    out_bias = centred(key_list[4], (D,), 0.3, 2.0, (), jnp.float32)
    norm_one_gain = jnp.clip(1.0 + 0.1 * jax.random.normal(key_list[5], (D,), jnp.float32), 0.5, 1.5)
    norm_one_shift = centred(key_list[6], (D,), 0.3, 2.0, (), jnp.float32)
    up_weight = centred(key_list[7], (D, FF), D ** -0.5, 0.25, ((1, 2),))
    up_bias = centred(key_list[8], (FF,), 0.5, 3.0, ((0, 2),))
    down_weight = centred(key_list[9], (FF, D), (FF // 2) ** -0.5, 0.1875, ((0, 2),))
    down_bias = centred(key_list[10], (D,), 0.3, 2.0, (), jnp.float32)
    norm_two_gain = jnp.clip(1.0 + 0.1 * jax.random.normal(key_list[11], (D,), jnp.float32), 0.5, 1.5)
    norm_two_shift = centred(key_list[12], (D,), 0.3, 2.0, (), jnp.float32)
    out_grad = centred(key_list[13], (TOKENS, D), 1.0, 6.0, ((0, 32),))
    lengths = draw_lengths(jax.random.fold_in(key_list[15], 71), 0)
    return {"tokens": tokens, "qkv_weight": qkv_weight, "qv_bias": qv_bias, "out_weight": out_weight, "out_bias": out_bias, "norm_one_gain": norm_one_gain, "norm_one_shift": norm_one_shift, "up_weight": up_weight, "up_bias": up_bias, "down_weight": down_weight, "down_bias": down_bias, "norm_two_gain": norm_two_gain, "norm_two_shift": norm_two_shift, "out_grad": out_grad, "lengths": lengths}


eps_norm = 1e-12
neg_fill = -1e+30
inv_root_two = 1.0 / math.sqrt(2.0)

@jax.custom_vjp
def low(v):
    return lax.optimization_barrier(v.astype(jnp.bfloat16)).astype(jnp.float32)

@jax.custom_vjp
def low_back(v):
    return v

def low_keep(v):
    return (low(v), None)

def low_pass(kept, grad):
    return (grad,)

def back_keep(v):
    return (v, None)

def back_low(kept, grad):
    return (low(grad),)
low.defvjp(low_keep, low_pass)
low_back.defvjp(back_keep, back_low)

def norm_rows(hidden, gain, shift):
    centre = lax.optimization_barrier(jnp.mean(hidden, axis=-1, keepdims=True))
    centered = hidden - centre
    spread = lax.optimization_barrier(jnp.mean(centered * centered, axis=-1, keepdims=True))
    return centered * lax.rsqrt(spread + eps_norm) * gain + shift

def group_forward(x_rows, lens, params):
    qkv_weight, qv_bias, out_weight, out_bias, gain_one, shift_one, up_weight, up_bias, down_weight, down_bias, gain_two, shift_two = params
    highest = lax.Precision.HIGHEST
    projected = jnp.einsum('td,jde->jte', x_rows, qkv_weight, precision=highest)
    bias_three = jnp.stack([qv_bias[0], jnp.zeros_like(qv_bias[0]), qv_bias[1]])
    qkv_low = low(low_back(projected + bias_three[:, None, :]))
    chains = lens.shape[0]
    length = x_rows.shape[0] // chains
    shaped = qkv_low.reshape(3, chains, length, HEADS, HDIM)
    scores = jnp.einsum('cqhd,ckhd->chqk', shaped[0], shaped[1], precision=highest) * (1.0 / math.sqrt(HDIM))
    live_keys = lax.broadcasted_iota(jnp.int32, (chains, 1, 1, length), 3) < lens[:, None, None, None]
    scores = low_back(jnp.where(live_keys, scores, neg_fill))
    probs_low = low(jax.nn.softmax(scores, axis=-1))
    attended = jnp.einsum('chqk,ckhd->cqhd', probs_low, shaped[2], precision=highest)
    attended = low(low_back(attended.reshape(x_rows.shape[0], HEADS * HDIM)))
    first_sum = x_rows + low_back(jnp.dot(attended, out_weight, precision=highest)) + out_bias
    normed_one = norm_rows(first_sum, gain_one, shift_one)
    pre_act = low_back(jnp.dot(low(normed_one), up_weight, precision=highest) + up_bias)
    act_low = low(0.5 * pre_act * (1.0 + lax.erf(pre_act * inv_root_two)))
    second_sum = normed_one + low_back(jnp.dot(act_low, down_weight, precision=highest)) + down_bias
    return norm_rows(second_sum, gain_two, shift_two)

def forward_all(x_all, lens_all, params):
    groups = lens_all.shape[0] // SEQ_DEV
    x_groups = x_all.reshape(groups, SEQ_DEV * LMAX, x_all.shape[1])
    len_groups = lens_all.reshape(groups, SEQ_DEV)
    checked = jax.checkpoint(group_forward)

    def scan_step(carry, item):
        return (carry, checked(item[0], item[1], params))
    _, stacked = lax.scan(scan_step, jnp.zeros((), jnp.float32), (x_groups, len_groups))
    return stacked.reshape(x_all.shape)

def reference(tokens, qkv_weight, qv_bias, out_weight, out_bias, norm_one_gain, norm_one_shift, up_weight, up_bias, down_weight, down_bias, norm_two_gain, norm_two_shift, out_grad, lengths):
    params = tuple((weight_arg.astype(jnp.float32) for weight_arg in (qkv_weight, qv_bias, out_weight, out_bias, norm_one_gain, norm_one_shift, up_weight, up_bias, down_weight, down_bias, norm_two_gain, norm_two_shift)))
    x_all = tokens.astype(jnp.float32)
    positions = jnp.arange(TOKENS, dtype=jnp.int32)
    live = (positions % LMAX < lengths[positions // LMAX]).astype(jnp.float32)

    def whole(x_arg, param_arg):
        return forward_all(x_arg, lengths, param_arg)
    result, pullback = jax.vjp(whole, x_all, params)
    grad_x, grads = pullback(out_grad.astype(jnp.float32) * live[:, None])
    return (result.astype(jnp.bfloat16), grad_x.astype(jnp.bfloat16), grads[0], grads[1], grads[2], grads[3], grads[4], grads[5], grads[6], grads[7], grads[8], grads[9], grads[10], grads[11])
```

```python
import jax, jax.numpy as jnp, math, functools
from jax import lax
from jax.sharding import PartitionSpec as P
from jax.experimental import pallas as pl
from jax.experimental.pallas import tpu as pltpu
F32=jnp.float32; BF=jnp.bfloat16
LMAX=160
EPS=1e-12
def dot(a,b): return lax.dot_general(a,b,(((1,),(0,)),((),())),preferred_element_type=F32)
def dot_nt(a,b): return lax.dot_general(a,b,(((1,),(1,)),((),())),preferred_element_type=F32)
AS_P=0.3275911*math.sqrt(0.5)
AS=[0.254829592,-0.284496736,1.421413741,-1.453152027,1.061405429]
def gelu_parts(v):
    E=jnp.exp(v*v*-0.5)
    t=1.0/(1.0+AS_P*jnp.abs(v))
    q=AS[4]*0.5
    for a in (AS[3],AS[2],AS[1],AS[0]): q=q*t+a*0.5
    q=q*t*E
    phi=jnp.where(v>=0,1.0-q,q)
    return v*phi, phi+v*(E*(1.0/math.sqrt(2*math.pi)))
def rowmean(x): return jnp.sum(x,axis=1,keepdims=True)*(1.0/x.shape[1])
def colsum(x): return jnp.sum(x,axis=0,keepdims=True)
def ffn_kernel(CH,lens_ref,h1_ref,og_ref,wup_ref,wdn_ref,upb_ref,sv_ref,
               out_ref,gone_ref,dwup_o,dwdn_o,dvec_ref,dupb_ref,
               act_s,slope_s,nT_s,gT_s,acc_s,dwup_s,dwdn_s):
    i=pl.program_id(0); n=pl.num_programs(0)
    R,D=h1_ref.shape; FF=wup_ref.shape[1]; NC=FF//CH
    @pl.when(i==0)
    def _():
        dwup_s[...]=jnp.zeros_like(dwup_s); dwdn_s[...]=jnp.zeros_like(dwdn_s)
        dvec_ref[...]=jnp.zeros_like(dvec_ref); dupb_ref[...]=jnp.zeros_like(dupb_ref)
    g1,b1,bd,g2,b2=(sv_ref[k:k+1,:] for k in range(5))
    h=h1_ref[...]
    c=h-rowmean(h); inv1=lax.rsqrt(rowmean(c*c)+EPS)
    n1=c*inv1
    normed=n1*g1+b1
    nlow=normed.astype(BF)
    nT_s[...]=nlow.T
    def up(k):
        return dot(nlow,wup_ref[:,k*CH:(k+1)*CH])+upb_ref[:,k*CH:(k+1)*CH]
    pre=up(0)
    acc=None
    for k in range(NC):
        nxt=up(k+1) if k+1<NC else None
        a,s=gelu_parts(pre)
        a=a.astype(BF)
        act_s[:,k*CH:(k+1)*CH]=a
        slope_s[:,k*CH:(k+1)*CH]=s.astype(slope_s.dtype)
        t=dot(a,wdn_ref[k*CH:(k+1)*CH,:])
        if k==0: acc_s[...]=t
        else: acc_s[...]+=t
        pre=nxt
    h2=normed+acc_s[...]+bd
    c2=h2-rowmean(h2); inv2=lax.rsqrt(rowmean(c2*c2)+EPS)
    n2=c2*inv2
    out_ref[...]=(n2*g2+b2).astype(BF)
    rows=i*R+lax.broadcasted_iota(jnp.int32,(R,1),0)
    live=jnp.zeros((R,1),F32)
    c0=(i*R)//LMAX
    for j in range((R-2)//LMAX+2):
        ch=jnp.minimum(c0+j,lens_ref.shape[0]-1)
        live=jnp.where((rows>=ch*LMAX)&(rows<ch*LMAX+lens_ref[ch]),1.0,live)
    go=og_ref[...].astype(F32)*live
    dvec_ref[4:5,:]+=colsum(go*n2); dvec_ref[5:6,:]+=colsum(go)
    e=go*g2
    gtwo=inv2*(e-rowmean(e)-n2*rowmean(e*n2))
    dvec_ref[3:4,:]+=colsum(gtwo)
    g2low=gtwo.astype(BF)
    gT_s[...]=g2low.T
    def gact(k): return dot_nt(g2low,wdn_ref[k*CH:(k+1)*CH,:])
    ga=gact(0)
    for k in range(NC):
        nxt=gact(k+1) if k+1<NC else None
        sl=slice(k*CH,(k+1)*CH)
        gp=(ga*slope_s[:,sl]).astype(BF)
        dwdn_s[:,sl]+=dot(gT_s[...],act_s[:,sl])
        dwup_s[:,sl]+=dot(nT_s[...],gp)
        dupb_ref[:,sl]+=colsum(gp.astype(F32))
        t=dot_nt(gp,wup_ref[:,sl])
        if k==0: acc_s[...]=t
        else: acc_s[...]+=t
        ga=nxt
    g1in=gtwo+acc_s[...]
    dvec_ref[1:2,:]+=colsum(g1in*n1); dvec_ref[2:3,:]+=colsum(g1in)
    e=g1in*g1
    gone=inv1*(e-rowmean(e)-n1*rowmean(e*n1))
    dvec_ref[0:1,:]+=colsum(gone)
    gone_ref[...]=gone
    @pl.when(i==n-1)
    def _():
        dwup_o[...]=dwup_s[...].astype(BF); dwdn_o[...]=dwdn_s[...].astype(BF)
def ffn(lens,h1,og,wup,wdn,upb,sv,R=512,CH=256,slope_dt=F32):
    rows,D=h1.shape; FF=wup.shape[1]
    one=lambda s: pl.BlockSpec(s,lambda i:tuple(0 for _ in s),pipeline_mode=pl.Buffered(1))
    row=pl.BlockSpec((R,D),lambda i:(i,0))
    return pl.pallas_call(functools.partial(ffn_kernel,CH),grid=(rows//R,),
      in_specs=[pl.BlockSpec(memory_space=pltpu.SMEM),row,row,one((D,FF)),one((FF,D)),one((1,FF)),one(sv.shape)],
      out_specs=[row,row,one((D,FF)),one((D,FF)),one((8,D)),one((1,FF))],
      out_shape=[jax.ShapeDtypeStruct((rows,D),BF),jax.ShapeDtypeStruct((rows,D),F32),
        jax.ShapeDtypeStruct((D,FF),BF),jax.ShapeDtypeStruct((D,FF),BF),
        jax.ShapeDtypeStruct((8,D),F32),jax.ShapeDtypeStruct((1,FF),F32)],
      scratch_shapes=[pltpu.VMEM((R,FF),BF),pltpu.VMEM((R,FF),slope_dt),pltpu.VMEM((D,R),BF),pltpu.VMEM((D,R),BF),
        pltpu.VMEM((R,D),F32),pltpu.VMEM((D,FF),F32),pltpu.VMEM((D,FF),F32)],
      compiler_params=pltpu.CompilerParams(vmem_limit_bytes=60<<20),name="ffn")(lens,h1,og,wup,wdn,upb,sv)
HD=64
def lane_head(w): return lax.broadcasted_iota(jnp.int32,(1,w),1)//HD
def stack_heads(x,nh):
    hd=lane_head(x.shape[1])
    return jnp.concatenate([jnp.where(hd==h,x,jnp.zeros_like(x)) for h in range(nh)],axis=0)
def pick_heads(x,nh):
    r=x.shape[0]//nh; hd=lane_head(x.shape[1])
    o=x[:r]
    for h in range(1,nh): o=jnp.where(hd==h,x[h*r:(h+1)*r],o)
    return o
def attn_fwd_kernel(lens_ref,x_ref,wqkv_ref,wout_ref,qkvb_ref,ob_ref,h1_ref,qkv_ref,att_ref,p_ref,att_s):
    i=pl.program_id(0)
    R,D=x_ref.shape; C=R//LMAX
    x=x_ref[...]
    for j in range(3):
        for g in range(2):
            w=D//2
            t=dot(x,wqkv_ref[j,:,g*w:(g+1)*w])+qkvb_ref[j:j+1,g*w:(g+1)*w]
            t=t.astype(BF)
            if j==0: t=t*jnp.asarray(0.125,BF)
            qkv_ref[j,g]=t
    kpos=lax.broadcasted_iota(jnp.int32,(LMAX,1),0)
    for c in range(C):
        rs=slice(c*LMAX,(c+1)*LMAX)
        ln=lens_ref[i*C+c]
        bias=jnp.where(kpos<ln,0.0,-1e30).astype(F32)
        for g in range(2):
            q=qkv_ref[0,g,rs,:]; k=qkv_ref[1,g,rs,:]; v=qkv_ref[2,g,rs,:]
            qs=stack_heads(q,4)
            st=dot_nt(k,qs)+bias
            m=jnp.max(st,axis=0,keepdims=True)
            e=jnp.exp(st-m)
            l=jnp.sum(e,axis=0,keepdims=True)
            p=(e*(1.0/l)).astype(BF)
            p_ref[c,g]=p
            o=dot(p.T,v)
            att_s[rs,g*256:(g+1)*256]=pick_heads(o,4).astype(BF)
    att_ref[...]=att_s[...]
    h1_ref[...]=x.astype(F32)+dot(att_s[...],wout_ref[...])+ob_ref[...]
def attn_fwd(lens,x,wqkv,wout,qkvb,ob,C=4):
    rows,D=x.shape; R=C*LMAX
    one=lambda s: pl.BlockSpec(s,lambda i:tuple(0 for _ in s),pipeline_mode=pl.Buffered(1))
    row=pl.BlockSpec((R,D),lambda i:(i,0))
    return pl.pallas_call(attn_fwd_kernel,grid=(rows//R,),
      in_specs=[pl.BlockSpec(memory_space=pltpu.SMEM),row,one((3,D,D)),one((D,D)),one((3,D)),one((1,D))],
      out_specs=[row,pl.BlockSpec((3,2,R,D//2),lambda i:(0,0,i,0)),row,pl.BlockSpec((C,2,LMAX,4*LMAX),lambda i:(i,0,0,0))],
      out_shape=[jax.ShapeDtypeStruct((rows,D),F32),jax.ShapeDtypeStruct((3,2,rows,D//2),BF),jax.ShapeDtypeStruct((rows,D),BF),
         jax.ShapeDtypeStruct((rows//LMAX,2,LMAX,4*LMAX),BF)],
      scratch_shapes=[pltpu.VMEM((R,D),BF)],
      compiler_params=pltpu.CompilerParams(vmem_limit_bytes=60<<20),name="attn_fwd")(lens,x,wqkv,wout,qkvb,ob)

def attn_bwd_kernel(lens_ref,gone_ref,x_ref,qkv_ref,p_ref,att_ref,wqkv_ref,wout_ref,
    gx_ref,dwq_o,dwo_o,dqvb_ref,dwq_s,dwo_s,dq_s):
    i=pl.program_id(0); n=pl.num_programs(0)
    R,D=x_ref.shape; C=R//LMAX
    @pl.when(i==0)
    def _():
        dwq_s[...]=jnp.zeros_like(dwq_s); dwo_s[...]=jnp.zeros_like(dwo_s); dqvb_ref[...]=jnp.zeros_like(dqvb_ref)
    gl=gone_ref[...].astype(BF)
    glT=gl.T
    dwo_s[...]+=dot(glT,att_ref[...])
    xT=x_ref[...].T
    gx=gone_ref[...]
    for g in range(2):
        ga=dot_nt(gl,wout_ref[g*256:(g+1)*256,:]).astype(BF)
        for c in range(C):
            rs=slice(c*LMAX,(c+1)*LMAX)
            q=qkv_ref[0,g,rs,:]; k=qkv_ref[1,g,rs,:]; v=qkv_ref[2,g,rs,:]
            go=ga[rs]
            p=p_ref[c,g]
            gs=stack_heads(go,4)
            dp=dot_nt(v,gs)
            pf=p.astype(F32)
            inner=jnp.sum(pf*dp,axis=0,keepdims=True)
            ds=(pf*(dp-inner)).astype(BF)
            dv=dot(p,gs)
            dk=dot(ds,stack_heads(q,4))
            dq=pick_heads(dot(ds.T,k),4)*0.125
            dq_s[rs,0:256]=dq.astype(BF); dq_s[rs,256:512]=dk.astype(BF); dq_s[rs,512:768]=dv.astype(BF)
        dwq_s[:,g*768:(g+1)*768]+=dot(xT,dq_s[...])
        dqvb_ref[0:1,g*256:(g+1)*256]+=colsum(dq_s[:,0:256].astype(F32))
        dqvb_ref[1:2,g*256:(g+1)*256]+=colsum(dq_s[:,512:768].astype(F32))
        for j in range(3):
            gx=gx+dot_nt(dq_s[:,j*256:(j+1)*256],wqkv_ref[j,:,g*256:(g+1)*256])
    gx_ref[...]=gx.astype(BF)
    @pl.when(i==n-1)
    def _():
        dwq_o[...]=dwq_s[...].astype(BF); dwo_o[...]=dwo_s[...].astype(BF)
def attn_bwd(lens,gone,x,qkv,p,att,wqkv,wout,C=4):
    rows,D=x.shape; R=C*LMAX
    one=lambda s: pl.BlockSpec(s,lambda i:tuple(0 for _ in s),pipeline_mode=pl.Buffered(1))
    row=pl.BlockSpec((R,D),lambda i:(i,0))
    return pl.pallas_call(attn_bwd_kernel,grid=(rows//R,),
      in_specs=[pl.BlockSpec(memory_space=pltpu.SMEM),row,row,pl.BlockSpec((3,2,R,D//2),lambda i:(0,0,i,0)),
        pl.BlockSpec((C,2,LMAX,4*LMAX),lambda i:(i,0,0,0)),row,one((3,D,D)),one((D,D))],
      out_specs=[row,one((D,3*D)),one((D,D)),one((8,D))],
      out_shape=[jax.ShapeDtypeStruct((rows,D),BF),jax.ShapeDtypeStruct((D,3*D),BF),jax.ShapeDtypeStruct((D,D),BF),jax.ShapeDtypeStruct((8,D),F32)],
      scratch_shapes=[pltpu.VMEM((D,3*D),F32),pltpu.VMEM((D,D),F32),pltpu.VMEM((R,768),BF)],
      compiler_params=pltpu.CompilerParams(vmem_limit_bytes=60<<20),name="attn_bwd")(lens,gone,x,qkv,p,att,wqkv,wout)

def tile_rows(rows):
    for r in (512, 640, 320):
        if rows % r == 0:
            return r
    return LMAX

def chain_block(chains):
    for c in (4, 2):
        if chains % c == 0:
            return c
    return 1

def on_device(tokens, qkv_weight, qv_bias, out_weight, out_bias, norm_one_gain, norm_one_shift, up_weight, up_bias,
              down_weight, down_bias, norm_two_gain, norm_two_shift, out_grad, lengths):
    rows, D = tokens.shape
    chains = rows // LMAX
    place = lax.axis_index("tensor")
    lens = lax.dynamic_slice_in_dim(lengths, place * chains, chains)
    gather = lambda a, d: lax.all_gather(a, "tensor", axis=d, tiled=True)
    wqkv = gather(qkv_weight, 2)
    wout = gather(out_weight, 0)
    wup = gather(up_weight, 1)
    wdn = gather(down_weight, 0)
    qvb = gather(qv_bias, 1).astype(F32)
    upb = gather(up_bias, 0).astype(F32)[None]
    qkvb = jnp.stack([qvb[0], jnp.zeros_like(qvb[0]), qvb[1]])
    zero = jnp.zeros_like(down_bias)
    sv = jnp.stack([norm_one_gain, norm_one_shift, down_bias, norm_two_gain, norm_two_shift, zero, zero, zero])
    block = chain_block(chains)
    h1, qkv, att, probs = attn_fwd(lens, tokens, wqkv, wout, qkvb, out_bias[None], C=block)
    out, gone, dwup, dwdn, dvec, dupb = ffn(lens, h1, out_grad, wup, wdn, upb, sv, R=tile_rows(rows))
    gx, dwq, dwo, dqvb = attn_bwd(lens, gone, tokens, qkv, probs, att, wqkv, wout, C=block)
    def total(a, dim):
        a = lax.psum_scatter(a.astype(BF), "tensor", scatter_dimension=dim, tiled=True)
        return lax.psum(a, "dp").astype(F32)
    dwq = dwq.reshape(D, 2, 3, D // 2).transpose(2, 0, 1, 3).reshape(3, D, D)
    small = lax.psum(dvec, ("dp", "tensor"))
    return (out, gx, total(dwq, 2), total(dqvb[:2], 1), total(dwo, 1).T, small[0], small[1], small[2],
            total(dwup, 1), total(dupb[0], 0), total(dwdn, 1).T, small[3], small[4], small[5])

def solution(mesh):
    rows = P(("dp", "tensor"), None)
    in_specs = (rows, P(None, None, "tensor"), P(None, "tensor"), P("tensor", None), P(), P(), P(), P(None, "tensor"),
                P("tensor"), P("tensor", None), P(), P(), P(), rows, P("dp"))
    out_specs = (rows, rows, P(None, None, "tensor"), P(None, "tensor"), P("tensor", None), P(), P(), P(),
                 P(None, "tensor"), P("tensor"), P("tensor", None), P(), P(), P())
    return jax.shard_map(on_device, mesh=mesh, in_specs=in_specs, out_specs=out_specs, check_vma=False)
```

```python
import functools
import math

import jax
import jax.numpy as jnp
from jax import lax
from jax.experimental import pallas as pl
from jax.experimental.pallas import tpu as pltpu
from jax.sharding import PartitionSpec as P

F32 = jnp.float32
BF = jnp.bfloat16
LMAX = 160
HDIM = 64
EPS = 1e-12
NEG = -1e30
MESH = pl.DeviceIdType.MESH
VMEM_LIMIT = 60 << 20

ERF_P = 0.3275911 * math.sqrt(0.5)
ERF_A = (0.254829592, -0.284496736, 1.421413741, -1.453152027, 1.061405429)


def dot(a, b):
    return lax.dot_general(a, b, (((1,), (0,)), ((), ())), preferred_element_type=F32)


def dot_nt(a, b):
    return lax.dot_general(a, b, (((1,), (1,)), ((), ())), preferred_element_type=F32)


def gelu_parts(v):
    bell = jnp.exp(v * v * -0.5)
    t = 1.0 / (1.0 + ERF_P * jnp.abs(v))
    tail = 0.5 * ERF_A[4]
    for a in ERF_A[3::-1]:
        tail = tail * t + 0.5 * a
    tail = tail * t * bell
    phi = jnp.where(v >= 0, 1.0 - tail, tail)
    return v * phi, phi + v * (bell * (1.0 / math.sqrt(2.0 * math.pi)))


def row_mean(x):
    return jnp.sum(x, axis=1, keepdims=True) * (1.0 / x.shape[1])


def col_sum(x):
    return jnp.sum(x, axis=0, keepdims=True)


def lane_head(width):
    return lax.broadcasted_iota(jnp.int32, (1, width), 1) // HDIM


def stack_heads(x):
    head = lane_head(x.shape[1])
    return jnp.concatenate(
        [jnp.where(head == h, x, jnp.zeros_like(x)) for h in range(x.shape[1] // HDIM)], axis=0
    )


def pick_heads(x):
    heads = x.shape[1] // HDIM
    r = x.shape[0] // heads
    head = lane_head(x.shape[1])
    out = x[:r]
    for h in range(1, heads):
        out = jnp.where(head == h, x[h * r : (h + 1) * r], out)
    return out


def places():
    dp = lax.axis_index("dp")
    return dp // 4, (dp // 2) % 2, dp % 2, lax.axis_index("tensor")


def at(z, y, core, x):
    return (z * 4 + y * 2 + core, x)


def enter(neighbours):
    barrier = pltpu.get_barrier_semaphore()
    for device in neighbours:
        pl.semaphore_signal(barrier, inc=1, device_id=device, device_id_type=MESH)
    pl.semaphore_wait(barrier, len(neighbours))


def remote(src, dst, sems, slot, device):
    return pltpu.make_async_remote_copy(
        src_ref=src, dst_ref=dst, send_sem=sems.at[0, slot], recv_sem=sems.at[1, slot],
        device_id=device, device_id_type=MESH,
    )


class Gather:
    def __init__(self, own, other, sems):
        z, y, core, x = places()
        self.px, self.py, self.pc = at(z, y, core, 1 - x), at(z, 1 - y, core, x), at(z, y, 1 - core, x)
        self.own, self.other, self.sems = own, other, sems
        self.y, self.core = y, core

    def neighbours(self):
        return (self.px, self.py, self.pc)

    def copy(self, k, stage):
        own, other = self.own[k], self.other[k]
        here, there = (self.y, self.core), (1 - self.y, self.core)
        if k == 0:
            here, there = (slice(None),) + here, (slice(None),) + there
        src, part, device = (
            (own, here, self.px), (other, here, self.py), (other, here, self.pc), (other, there, self.pc)
        )[stage]
        return remote(src.at[part], other.at[part], self.sems, 4 * k + stage, device)

    def fetch(self, k):
        self.copy(k, 0).start()

    def spread(self, k):
        self.copy(k, 0).wait_recv()
        self.copy(k, 1).start()
        self.copy(k, 2).start()

    def finish(self, k):
        self.copy(k, 1).wait_recv()
        self.copy(k, 3).start()

    def arrived(self, k):
        self.copy(k, 2).wait_recv()
        self.copy(k, 3).wait_recv()

    def sent(self, k):
        for stage in range(4):
            self.copy(k, stage).wait_send()


def attn_fwd_kernel(comm, *refs):
    if comm:
        (lens_ref, x_ref, wq_ref, wo_ref, bias_ref, ob_ref, wq_any, wo_any, up_any, dn_any,
         h1_ref, qkv_ref, att_ref, p_ref, wq_out, wo_out, up_out, dn_out, bias_out,
         att_s, wq_s, wo_s, bias_s, sems, local) = refs
    else:
        (lens_ref, x_ref, wq_ref, wo_ref, bias_ref, ob_ref, wq_s, wo_s, bias_s,
         h1_ref, qkv_ref, att_ref, p_ref, att_s) = refs
    p, i = pl.program_id(0), pl.program_id(1)
    rows, d = x_ref.shape
    block = rows // LMAX
    half = d // 2
    if comm:
        gather = Gather((wq_any, wo_any, up_any, dn_any, bias_ref), (wq_s, wo_s, up_out, dn_out, bias_s), sems)
        step = p * pl.num_programs(1) + i
        keep = [pltpu.make_async_copy(a, b, local.at[k]) for k, (a, b) in enumerate(
            ((wq_s, wq_out), (wo_s, wo_out), (bias_s, bias_out)))]

        @pl.when(step == 0)
        def _():
            enter(gather.neighbours())
            gather.fetch(0)
            gather.fetch(4)
            gather.fetch(1)

        @pl.when(step == 1)
        def _():
            gather.fetch(2)
            gather.fetch(3)

        @pl.when(step == 2)
        def _():
            gather.spread(0)
            gather.spread(4)
            gather.spread(1)

        @pl.when(step == 3)
        def _():
            gather.finish(0)
            gather.finish(4)
            gather.finish(1)

        @pl.when(step == 4)
        def _():
            for k in (0, 4, 1):
                gather.arrived(k)
            for copy in keep:
                copy.start()

        @pl.when(step == 5)
        def _():
            gather.spread(2)

        @pl.when(step == 6)
        def _():
            gather.spread(3)
            gather.finish(2)

    x = x_ref[...]
    first = lax.axis_index("tensor") * (pl.num_programs(1) * block)
    kpos = lax.broadcasted_iota(jnp.int32, (LMAX, 1), 0)

    def heads(wq, bias_of):
        for j in range(3):
            t = dot(x, wq[j].reshape(d, half))
            if j != 1:
                t += lanes(bias_of, j * half // 256, half)
            t = t.astype(BF)
            if j == 0:
                t = t * jnp.asarray(1.0 / math.sqrt(HDIM), BF)
            qkv_ref[j, 0] = t
        for c in range(block):
            rs = slice(c * LMAX, (c + 1) * LMAX)
            bias = jnp.where(kpos < lens_ref[first + i * block + c], 0.0, NEG).astype(F32)
            st = dot_nt(qkv_ref[1, 0, rs, :], stack_heads(qkv_ref[0, 0, rs, :])) + bias
            e = jnp.exp(st - jnp.max(st, axis=0, keepdims=True))
            probs = (e * (1.0 / jnp.sum(e, axis=0, keepdims=True))).astype(BF)
            p_ref[c, 0] = probs
            o = pick_heads(dot(probs.T, qkv_ref[2, 0, rs, :])).astype(BF)
            att_ref[0, rs, :] = o

    @pl.when(p == 0)
    def _():
        heads(wq_ref, bias_ref)
        att_s[i] = att_ref[0]

    @pl.when(p == 1)
    def _():
        heads(wq_s, bias_s)
        wo = wo_s[...].reshape(half, d)
        h1_ref[...] = x.astype(F32) + dot(att_s[i], wo_ref[...]) + dot(att_ref[0], wo) + ob_ref[...]

    if comm:

        @pl.when(step == 2 * pl.num_programs(1) - 1)
        def _():
            gather.finish(3)
            for copy in keep:
                copy.wait()
            gather.arrived(2)
            gather.arrived(3)
            for k in range(5):
                gather.sent(k)


def lanes(ref, line, width):
    parts = [ref[k // 16, k // 8 % 2, k % 8 : k % 8 + 1, :] for k in range(line, line + width // 128)]
    return parts[0] if len(parts) == 1 else jnp.concatenate(parts, axis=1)


def once(shape):
    return pl.BlockSpec(shape, lambda *_: (0,) * len(shape), pipeline_mode=pl.Buffered(1))


ANY = pl.BlockSpec(memory_space=pl.ANY)
SMEM = pl.BlockSpec(memory_space=pltpu.SMEM)


def attn_fwd(comm, block, lens, x, wq, wo, bias, ob, others):
    rows, d = x.shape
    half, r = d // 2, block * LMAX
    n = rows // r
    sds = jax.ShapeDtypeStruct
    row = pl.BlockSpec((r, d), lambda p, i: (i, 0))
    in_specs = [SMEM, row, once((3, d, half)), once((half, d)), once(bias.shape), once((1, d))]
    out_specs = [
        pl.BlockSpec((r, d), lambda p, i: (i * p, 0)),
        pl.BlockSpec((3, 1, r, half), lambda p, i: (0, p, i, 0)),
        pl.BlockSpec((1, r, half), lambda p, i: (p, i, 0)),
        pl.BlockSpec((block, 1, LMAX, half // HDIM * LMAX), lambda p, i: (i, p, 0, 0)),
    ]
    out_shape = [
        sds((rows, d), F32),
        sds((3, 2, rows, half), BF),
        sds((2, rows, half), BF),
        sds((rows // LMAX, 2, LMAX, half // HDIM * LMAX), BF),
    ]
    scratch = [pltpu.VMEM((n, r, half), BF)]
    args = [lens, x, wq, wo, bias, ob]
    if comm:
        in_specs += [ANY] * 4
        out_specs += [ANY] * 5
        out_shape += [sds(a.shape, a.dtype) for a in others + (bias,)]
        scratch += [pltpu.VMEM(a.shape, a.dtype) for a in others[:2] + (bias,)]
        scratch += [pltpu.SemaphoreType.DMA((2, 20)), pltpu.SemaphoreType.DMA((3,))]
    else:
        in_specs += [once((3, d, half)), once((half, d)), once(bias.shape)]
    params = dict(vmem_limit_bytes=VMEM_LIMIT)
    if comm:
        params.update(collective_id=0, has_side_effects=True)
    return pl.pallas_call(
        functools.partial(attn_fwd_kernel, comm), grid=(2, n), in_specs=in_specs, out_specs=out_specs,
        out_shape=out_shape, scratch_shapes=scratch, compiler_params=pltpu.CompilerParams(**params),
        name="attention_forward",
    )(*args, *others)


def ffn_kernel(CH, lens_ref, h1_ref, og_ref, upa_ref, upb_ref, dna_ref, dnb_ref, ba_ref, bb_ref,
               gain1_ref, shift1_ref, bias_dn_ref, gain2_ref, shift2_ref,
               out_ref, gone_ref, dup_ref, ddn_ref, small_ref,
               act_s, slope_s, nT_s, gT_s, acc_s, dup_s, ddn_s):
    i, n = pl.program_id(0), pl.num_programs(0)
    R, D = h1_ref.shape
    hid = upa_ref.shape[1]
    chunks = [(r, k * CH) for r in range(2) for k in range(hid // CH)]
    ups, dns, biases = (upa_ref, upb_ref), (dna_ref, dnb_ref), (ba_ref, bb_ref)

    @pl.when(i == 0)
    def _():
        dup_s[...] = jnp.zeros_like(dup_s)
        ddn_s[...] = jnp.zeros_like(ddn_s)
        small_ref[...] = jnp.zeros_like(small_ref)

    gain1, shift1, bias_dn, gain2, shift2 = (
        ref[...] for ref in (gain1_ref, shift1_ref, bias_dn_ref, gain2_ref, shift2_ref))
    h = h1_ref[...]
    c = h - row_mean(h)
    inv1 = lax.rsqrt(row_mean(c * c) + EPS)
    n1 = c * inv1
    normed = n1 * gain1 + shift1
    nlow = normed.astype(BF)
    nT_s[...] = nlow.T

    def up(chunk):
        r, s = chunk
        return dot(nlow, ups[r][:, s : s + CH]) + lanes(biases[r], (D + s) // 128, CH)

    pre = up(chunks[0])
    for k, (r, s) in enumerate(chunks):
        nxt = up(chunks[k + 1]) if k + 1 < len(chunks) else None
        a, sl = gelu_parts(pre)
        a = a.astype(BF)
        act_s[r, :, s : s + CH] = a
        slope_s[r, :, s : s + CH] = sl
        t = dot(a, dns[r][s : s + CH, :])
        if k == 0:
            acc_s[...] = t
        else:
            acc_s[...] += t
        pre = nxt
    h2 = normed + acc_s[...] + bias_dn
    c2 = h2 - row_mean(h2)
    inv2 = lax.rsqrt(row_mean(c2 * c2) + EPS)
    n2 = c2 * inv2
    out_ref[...] = (n2 * gain2 + shift2).astype(BF)

    row = i * R + lax.broadcasted_iota(jnp.int32, (R, 1), 0)
    live = jnp.zeros((R, 1), F32)
    first = (i * R) // LMAX
    for j in range((R - 2) // LMAX + 2):
        ch = jnp.minimum(first + j, n * R // LMAX - 1)
        length = lens_ref[lax.axis_index("tensor") * (n * R // LMAX) + ch]
        live = jnp.where((row >= ch * LMAX) & (row < ch * LMAX + length), 1.0, live)
    go = og_ref[...].astype(F32) * live
    small_ref[0, 4:5, :] += col_sum(go * n2)
    small_ref[0, 5:6, :] += col_sum(go)
    e = go * gain2
    gtwo = inv2 * (e - row_mean(e) - n2 * row_mean(e * n2))
    small_ref[0, 3:4, :] += col_sum(gtwo)
    glow = gtwo.astype(BF)
    gT_s[...] = glow.T

    def gact(chunk):
        r, s = chunk
        return dot_nt(glow, dns[r][s : s + CH, :])

    ga = gact(chunks[0])
    for k, (r, s) in enumerate(chunks):
        nxt = gact(chunks[k + 1]) if k + 1 < len(chunks) else None
        cs = slice(s, s + CH)
        gp = (ga * slope_s[r, :, cs]).astype(BF)
        ddn_s[r, :, cs] += dot(gT_s[...], act_s[r, :, cs])
        dup_s[r, :, cs] += dot(nT_s[...], gp)
        total = col_sum(gp.astype(F32))
        for o in range(0, CH, min(CH, D)):
            w = min(CH, D)
            line, lane = (s + o) // D, (s + o) % D
            small_ref[1 + r, line : line + 1, lane : lane + w] += total[:, o : o + w]
        t = dot_nt(gp, ups[r][:, cs])
        if k == 0:
            acc_s[...] = t
        else:
            acc_s[...] += t
        ga = nxt
    gin = gtwo + acc_s[...]
    small_ref[0, 1:2, :] += col_sum(gin * n1)
    small_ref[0, 2:3, :] += col_sum(gin)
    e = gin * gain1
    gone = inv1 * (e - row_mean(e) - n1 * row_mean(e * n1))
    small_ref[0, 0:1, :] += col_sum(gone)
    gone_ref[...] = gone

    @pl.when(i == n - 1)
    def _():
        dup_ref[...] = dup_s[...].astype(BF)
        ddn_ref[...] = ddn_s[...].astype(BF)


def ffn(R, CH, lens, h1, og, ups, dns, bias, vecs):
    rows, D = h1.shape
    hid = ups[0].shape[1]
    sds = jax.ShapeDtypeStruct
    row = pl.BlockSpec((R, D), lambda i: (i, 0))
    return pl.pallas_call(
        functools.partial(ffn_kernel, CH), grid=(rows // R,),
        in_specs=[SMEM, row, row, once((D, hid)), once((D, hid)), once((hid, D)), once((hid, D)),
                  once(bias[0].shape), once(bias[1].shape)] + [once((1, D))] * 5,
        out_specs=[row, row, once((2, D, hid)), once((2, D, hid)), once((3, 8, D))],
        out_shape=[sds((rows, D), BF), sds((rows, D), F32), sds((2, D, hid), BF), sds((2, D, hid), BF),
                   sds((3, 8, D), F32)],
        scratch_shapes=[pltpu.VMEM((2, R, hid), BF), pltpu.VMEM((2, R, hid), F32), pltpu.VMEM((D, R), BF),
                        pltpu.VMEM((D, R), BF), pltpu.VMEM((R, D), F32), pltpu.VMEM((2, D, hid), F32),
                        pltpu.VMEM((2, D, hid), F32)],
        compiler_params=pltpu.CompilerParams(vmem_limit_bytes=VMEM_LIMIT), name="feed_forward",
    )(lens, h1, og, *ups, *dns, *bias, *vecs)


def add_low(dst, a, b):
    lead = dst.shape[:-2]
    total = math.prod(lead)

    def one(k, carry):
        idx = []
        for s in reversed(lead):
            idx.append(k % s)
            k = k // s
        idx = tuple(reversed(idx))
        dst[idx] = (a[idx].astype(F32) + b[idx].astype(F32)).astype(BF)
        return carry

    if total == 1:
        idx = (0,) * len(lead)
        dst[idx] = (a[idx].astype(F32) + b[idx].astype(F32)).astype(BF)
    else:
        lax.fori_loop(0, total, one, 0)


class Reduce:
    def __init__(self, src, width, order, bufs, sems, base):
        self.z, self.y, self.core, self.x = places()
        z, y, core, x = self.z, self.y, self.core, self.x
        self.src, self.order, self.sems, self.base = src, order, sems, base
        self.rc, self.h, self.r1, self.w, self.r2, self.v, self.rz, self.full = bufs
        self.px, self.py, self.pc = at(z, y, core, 1 - x), at(z, 1 - y, core, x), at(z, y, 1 - core, x)

    def zdev(self, d):
        zt = lax.rem(self.z + d, 4)
        return zt, at(zt, self.y, self.core, self.x)

    def copies(self, stage):
        b, y, core, z = self.base, self.y, self.core, self.z
        if stage == 0:
            return [remote(self.src.at[:, 1 - core], self.rc, self.sems, b, self.pc)]
        if stage == 1:
            if self.order == "xy":
                return [remote(self.h.at[1], self.r1, self.sems, b + 1, self.px)]
            return [remote(self.h.at[:, 1 - y], self.r1, self.sems, b + 1, self.py)]
        if stage == 2:
            if self.order == "xy":
                return [remote(self.w.at[1 - y], self.r2, self.sems, b + 2, self.py)]
            return [remote(self.w.at[1], self.r2, self.sems, b + 2, self.px)]
        if stage == 3:
            out = []
            for d in (1, 2, 3):
                zt, dev = self.zdev(d)
                out.append(remote(self.v.at[zt], self.rz.at[d - 1], self.sems, b + 2 + d, dev))
            return out
        if stage == 4:
            out = []
            for d in (1, 2, 3):
                zt, dev = self.zdev(d)
                part = self.full.at[core, y, z]
                out.append(remote(part, part, self.sems, b + 5 + d, dev))
            return out
        if stage == 5:
            part = self.full.at[core, y]
            return [remote(part, part, self.sems, b + 9, self.py)]
        part = self.full.at[core]
        return [remote(part, part, self.sems, b + 10, self.pc)]

    def start(self, stage):
        for copy in self.copies(stage):
            copy.start()

    def combine(self, stage):
        y, core, z = self.y, self.core, self.z
        if stage == 0:
            add_low(self.h, self.src.at[:, core], self.rc)
        elif stage == 1:
            add_low(self.w, self.h.at[0] if self.order == "xy" else self.h.at[:, y], self.r1)
        elif stage == 2:
            mine = self.w.at[y] if self.order == "xy" else self.w.at[0]
            self.v[...] = (mine[...].astype(F32) + self.r2[...].astype(F32)).astype(BF).reshape(self.v.shape)
        elif stage == 3:
            s = self.v[z].astype(F32)
            for d in range(3):
                s = s + self.rz[d].astype(F32)
            self.full[core, y, z] = s.astype(BF)

    def take(self, stage):
        for copy in self.copies(stage):
            copy.wait()
        self.combine(stage)

    def step(self, stage):
        self.take(stage)
        if stage < 6:
            self.start(stage + 1)


def reduce_bufs(width, order, rows=128):
    first = (2, rows, width)
    return [pltpu.VMEM(s, BF) for s in (
        (2, 2, rows, width), (2, 2, rows, width), first, first, (rows, width), (4, rows // 4, width),
        (3, rows // 4, width), (2, 2, 4, rows // 4, width))]


class ReduceOwn(Reduce):
    def __init__(self, src_other, src_own, width, bufs, sems, base):
        Reduce.__init__(self, None, width, "xy", bufs[2:], sems, base)
        self.srcs = (src_own, src_other)
        self.rcs, self.hs = bufs[:2]

    def copies(self, stage):
        b = self.base
        if stage == "other":
            return [remote(self.srcs[1].at[1 - self.core], self.rcs.at[1], self.sems, b + 11, self.pc)]
        if stage == "own":
            return [remote(self.srcs[0].at[1 - self.core], self.rcs.at[0], self.sems, b, self.pc)]
        if stage == 1:
            return [remote(self.hs.at[1], self.r1, self.sems, b + 1, self.px)]
        return Reduce.copies(self, stage)

    def combine(self, stage):
        if stage == "other":
            add_low(self.hs.at[1], self.srcs[1].at[self.core], self.rcs.at[1])
        elif stage == "own":
            add_low(self.hs.at[0], self.srcs[0].at[self.core], self.rcs.at[0])
        elif stage == 1:
            add_low(self.w, self.hs.at[0], self.r1)
        else:
            Reduce.combine(self, stage)


def reduce_own_bufs(width, rows=128):
    pair = (2, 2, rows, width)
    one = (8, 128)
    return [pltpu.VMEM(s, BF) for s in (
        pair, pair, (16, 128), (16, 128), (2, rows, width), (2, rows, width), (rows, width),
        (4, rows // 4, width), (3, rows // 4, width), (2, 2, 4, rows // 4, width))]


class Butterfly:
    def __init__(self, acc, recv, sems, base):
        z, y, core, x = places()
        self.acc, self.recv, self.sems, self.base = acc, recv, sems, base
        self.devices = (at(z, y, 1 - core, x), at(z, y, core, 1 - x), at(z, 1 - y, core, x),
                        at(z + 1 - 2 * (z % 2), y, core, x), at((z + 2) % 4, y, core, x))

    def copy(self, k):
        return remote(self.acc.at[k], self.recv.at[k], self.sems, self.base + k, self.devices[k])

    def start(self, k):
        self.copy(k).start()

    def take(self, k):
        self.copy(k).wait()
        if k == 1:
            self.acc[k + 1, 0] = self.acc[k, 0] + self.recv[k, 0]
            self.acc[k + 1, 1] = self.acc[k, 1] + self.recv[k, 2]
            self.acc[k + 1, 2] = self.acc[k, 2] + self.recv[k, 1]
        else:
            self.acc[k + 1] = self.acc[k] + self.recv[k]

    def step(self, k):
        self.take(k)
        if k < 4:
            self.start(k + 1)


def attn_bwd_kernel(comm, *refs):
    (gone_ref, x_ref, qkv_ref, p_ref, att_ref, wqa_ref, wqb_ref, woa_ref, wob_ref) = refs[:9]
    refs = refs[9:]
    if comm:
        up_ref, dn_ref, small_ref = refs[:3]
        gx_ref, up_out, dn_out, wo_out, wq_out, small_out = refs[3:9]
        dq_s, dwq_s, dwo_s, gx_s, wo_src, q_own, q_oth, acc, recv, sems = refs[9:19]
        bufs = refs[19:]
    else:
        gx_ref, wo_out, wq_out, bias_out = refs[:4]
        dq_s, dwq_s, dwo_s, gx_s = refs[4:]
    p, i = pl.program_id(0), pl.program_id(1)
    n = pl.num_programs(1)
    rows, d = x_ref.shape
    block = rows // LMAX
    half = d // 2
    step = p * n + i
    if comm:
        red_up = Reduce(up_ref, half, "xy", bufs[0:8], sems, 0)
        red_dn = Reduce(dn_ref, half, "yx", bufs[8:16], sems, 11)
        red_wo = Reduce(wo_src, half, "xy", bufs[16:24], sems, 22)
        red_wq = ReduceOwn(q_oth, q_own, 3 * half, bufs[24:34], sems, 33)
        fly = Butterfly(acc, recv, sems, 45)

        @pl.when(step == 0)
        def _():
            enter(fly.devices[:3] + tuple(red_up.zdev(k)[1] for k in (1, 2, 3)))
            red_up.start(0)
            red_dn.start(0)
            acc[0] = small_ref[...]

        @pl.when(step == 1)
        def _():
            red_up.step(0)
            red_dn.step(0)

        @pl.when(step == 4)
        def _():
            red_up.step(1)
            red_dn.step(1)

        @pl.when(step == 5)
        def _():
            red_wo.step(0)
            red_wq.take("other")
            red_wq.start(1)

        @pl.when(step == 6)
        def _():
            red_up.step(2)
            red_dn.step(2)

        @pl.when(step == 7)
        def _():
            red_up.step(3)
            red_dn.step(3)

    @pl.when(i == 0)
    def _():
        dwq_s[...] = jnp.zeros_like(dwq_s)

        @pl.when(p == 0)
        def _():
            dwo_s[...] = jnp.zeros_like(dwo_s)
            if not comm:
                bias_out[...] = jnp.zeros_like(bias_out)

    glow = gone_ref[...].astype(BF)

    @pl.when(p == 0)
    def _():
        glT = glow.T
        dwo_s[0] += dot(glT, att_ref[0])
        dwo_s[1] += dot(glT, att_ref[1])

    def heads(wo, wq, which):
        ga = dot_nt(glow, wo).astype(BF)
        for c in range(block):
            rs = slice(c * LMAX, (c + 1) * LMAX)
            probs = p_ref[c, 0]
            k, v = qkv_ref[1, 0, rs, :], qkv_ref[2, 0, rs, :]
            gs = stack_heads(ga[rs])
            dp = dot_nt(v, gs)
            pf = probs.astype(F32)
            ds = (pf * (dp - jnp.sum(pf * dp, axis=0, keepdims=True))).astype(BF)
            dv = dot(probs, gs)
            dk = dot(ds, stack_heads(qkv_ref[0, 0, rs, :]))
            dq = pick_heads(dot(ds.T, k)) * (1.0 / math.sqrt(HDIM))
            dq_s[rs, 0:half] = dq.astype(BF)
            dq_s[rs, half : 2 * half] = dk.astype(BF)
            dq_s[rs, 2 * half :] = dv.astype(BF)
        dwq_s[...] += dot(x_ref[...].T, dq_s[...])
        bias = bias_out if not comm else acc.at[0]
        base = 0 if not comm else 1
        bias[base + which, 2:3, 0:half] += col_sum(dq_s[:, 0:half].astype(F32))
        bias[base + which, 2:3, half:d] += col_sum(dq_s[:, 2 * half :].astype(F32))
        total = dot_nt(dq_s[:, 0:half], wq[0].reshape(d, half))
        for j in (1, 2):
            total += dot_nt(dq_s[:, j * half : (j + 1) * half], wq[j].reshape(d, half))
        return total

    @pl.when(p == 0)
    def _():
        gx_s[i] = gone_ref[...] + heads(wob_ref[...].reshape(half, d), wqb_ref, 1)

    @pl.when(p == 1)
    def _():
        gx_ref[...] = (gx_s[i] + heads(woa_ref[...], wqa_ref, 0)).astype(BF)

    if not comm:

        @pl.when(i == n - 1)
        def _():
            wq_out[1 - p] = dwq_s[...].astype(BF)
            wo_out[...] = dwo_s[...].astype(BF)

        return

    def low(dst, src):
        for core in range(2):
            for y in range(2):
                at_row = (core * 2 + y) * (d // 4)
                dst[core, y] = src[at_row : at_row + d // 4].astype(BF)

    @pl.when(step == n - 1)
    def _():
        for r in range(2):
            low(wo_src.at[r], dwo_s.at[r])
        low(q_oth, dwq_s)
        red_wo.start(0)
        red_wq.start("other")

    @pl.when(step == 2 * n - 1)
    def _():
        low(q_own, dwq_s)
        red_wq.start("own")
        fly.start(0)
        red_wo.step(1)
        red_wq.take("own")
        red_wq.step(1)
        fly.step(0)
        red_up.step(4)
        red_dn.step(4)
        red_wo.step(2)
        fly.step(1)
        red_wq.step(2)
        red_up.step(5)
        red_dn.step(5)
        red_wo.step(3)
        fly.step(2)
        red_wq.step(3)
        red_wo.step(4)
        fly.step(3)
        red_up.step(6)
        red_dn.step(6)
        up_out[...] = red_up.full[...]
        dn_out[...] = red_dn.full[...]
        red_wq.step(4)
        red_wo.step(5)
        fly.step(4)
        small_out[...] = acc[5]
        red_wq.step(5)
        red_wo.step(6)
        wo_out[...] = red_wo.full[...]
        red_wq.step(6)
        wq_out[...] = red_wq.full[...]


def attn_bwd(comm, block, gone, x, qkv, probs, att, wq, wo, sums):
    rows, d = x.shape
    half, r = d // 2, block * LMAX
    n = rows // r
    sds = jax.ShapeDtypeStruct
    row = pl.BlockSpec((r, d), lambda p, i: (i, 0))
    in_specs = [
        row, row,
        pl.BlockSpec((3, 1, r, half), lambda p, i: (0, 1 - p, i, 0)),
        pl.BlockSpec((block, 1, LMAX, half // HDIM * LMAX), lambda p, i: (i, 1 - p, 0, 0)),
        pl.BlockSpec((2, r, half), lambda p, i: (0, i * (1 - p) + (n - 1) * p, 0)),
        once(wq[0].shape), once(wq[1].shape), once(wo[0].shape), once(wo[1].shape),
    ]
    gx_spec, gx_shape = pl.BlockSpec((r, d), lambda p, i: (i * p, 0)), sds((rows, d), BF)
    scratch = [pltpu.VMEM((r, 3 * half), BF), pltpu.VMEM((d, 3 * half), F32), pltpu.VMEM((2, d, half), F32),
               pltpu.VMEM((n, r, d), F32)]
    params = dict(vmem_limit_bytes=VMEM_LIMIT)
    if comm:
        up, dn, small = sums
        hid = up.shape[-1]
        split = lambda w: (2, 2, 4, d // 16, w)
        in_specs += [once(up.shape), once(dn.shape), once(small.shape)]
        out_specs = [gx_spec, once(split(hid)), once(split(hid)), once(split(half)), once(split(3 * half)),
                     once(small.shape)]
        out_shape = [gx_shape, sds(split(hid), BF), sds(split(hid), BF), sds(split(half), BF),
                     sds(split(3 * half), BF), sds(small.shape, F32)]
        rows4 = d // 4
        scratch += [pltpu.VMEM((2, 2, 2, rows4, half), BF), pltpu.VMEM((2, 2, rows4, 3 * half), BF),
                    pltpu.VMEM((2, 2, rows4, 3 * half), BF), pltpu.VMEM((6,) + small.shape, F32),
                    pltpu.VMEM((5,) + small.shape, F32), pltpu.SemaphoreType.DMA((2, 50))]
        scratch += reduce_bufs(hid, "xy", rows4) + reduce_bufs(hid, "yx", rows4) + reduce_bufs(half, "xy", rows4)
        scratch += reduce_own_bufs(3 * half, rows4)
        params.update(collective_id=1, has_side_effects=True)
    else:
        out_specs = [gx_spec, once((2, d, half)), once((2, d, 3 * half)), once((2, 8, d))]
        out_shape = [gx_shape, sds((2, d, half), BF), sds((2, d, 3 * half), BF), sds((2, 8, d), F32)]
    return pl.pallas_call(
        functools.partial(attn_bwd_kernel, comm), grid=(2, n), in_specs=in_specs, out_specs=out_specs,
        out_shape=out_shape, scratch_shapes=scratch, compiler_params=pltpu.CompilerParams(**params),
        name="attention_backward",
    )(gone, x, qkv, probs, att, *wq, *wo, *sums)


def tile_rows(rows):
    for r in (512, 640, 320):
        if rows % r == 0:
            return r
    return LMAX


def chain_block(chains):
    for c in (4, 2):
        if chains % c == 0:
            return c
    return 1


def on_device(comm, tokens, qkv_weight, qv_bias, out_weight, out_bias, gain_one, shift_one, up_weight, up_bias,
              down_weight, down_bias, gain_two, shift_two, out_grad, lengths):
    rows, d = tokens.shape
    chains = rows // LMAX
    half = d // 2
    vecs = [a[None] for a in (gain_one, shift_one, down_bias, gain_two, shift_two)]
    block = chain_block(chains)
    comm = comm and chains == 16

    def gather(a, dim):
        return lax.all_gather(a, "tensor", axis=dim, tiled=True)

    def table(qv, up):
        flat = jnp.concatenate([qv[0], qv[1], up]).astype(F32)
        return jnp.pad(flat, (0, 4096 - flat.shape[0])).reshape(2, 2, 8, 128)

    if comm:
        hid = up_weight.shape[1]
        bias = table(qv_bias, up_bias)
        quarters = (
            qkv_weight.reshape(3, 2, 2, d // 4, half), out_weight.reshape(2, 2, half // 4, d),
            up_weight.reshape(2, 2, d // 4, hid), down_weight.reshape(2, 2, hid // 4, d),
        )
        h1, qkv, att, probs, wqb, wob, wupb, wdnb, bias_b = attn_fwd(
            True, block, lengths, tokens, qkv_weight, out_weight, bias, out_bias[None], quarters)
        wqs, wos, bias = (qkv_weight, wqb), (out_weight, wob), (bias, bias_b)
        ups, dns = (up_weight, wupb.reshape(d, hid)), (down_weight, wdnb.reshape(hid, d))
    else:
        wq, wo = gather(qkv_weight, 2), gather(out_weight, 0)
        wup, wdn = gather(up_weight, 1), gather(down_weight, 0)
        hid = wup.shape[1] // 2
        qvb, upb = gather(qv_bias, 1), gather(up_bias, 0)
        bias = (table(qvb[:, :half], upb[:hid]), table(qvb[:, half:], upb[hid:]))
        wqs, wos = (wq[:, :, :half], wq[:, :, half:]), (wo[:half], wo[half:])
        ups, dns = (wup[:, :hid], wup[:, hid:]), (wdn[:hid], wdn[hid:])
        h1, qkv, att, probs = attn_fwd(
            False, block, lengths, tokens, wqs[0], wos[0], bias[0], out_bias[None], (wqs[1], wos[1], bias[1]))
    out, gone, dup, ddn, small = ffn(tile_rows(rows), 256, lengths, h1, out_grad, ups, dns, bias, vecs)
    if comm:
        split = (2, 2, 2, d // 4, hid)
        gx, dup, ddn, dwo, dwq, small = attn_bwd(
            True, block, gone, tokens, qkv, probs, att, wqs, wos, (dup.reshape(split), ddn.reshape(split), small))
        dup = dup.reshape(d, hid).astype(F32)
        ddn = ddn.reshape(d, hid).T.astype(F32)
        dwo = dwo.reshape(d, half).T.astype(F32)
        dwq = dwq.reshape(d, 3, half).transpose(1, 0, 2).astype(F32)
        dupb = small[1, : hid // d].reshape(hid)
        dqvb = small[1, 2].reshape(2, half)
        vecs = small[0]
    else:
        gx, dwo, dwq, dbias = attn_bwd(False, block, gone, tokens, qkv, probs, att, wqs, wos, ())

        def total(a, dim):
            a = lax.psum_scatter(a.astype(BF), "tensor", scatter_dimension=dim, tiled=True)
            return lax.psum(a, "dp").astype(F32)

        dwq = total(dwq.reshape(2, d, 3, half).transpose(2, 1, 0, 3).reshape(3, d, d), 2)
        dwo = total(jnp.concatenate([dwo[0], dwo[1]], axis=1), 1).T
        dup = total(jnp.concatenate([dup[0], dup[1]], axis=1), 1)
        ddn = total(jnp.concatenate([ddn[0], ddn[1]], axis=1), 1).T
        dupb = total(small[1:, : hid // d].reshape(2 * hid), 0)
        dqvb = total(dbias[:, 2].reshape(2, 2, half).transpose(1, 0, 2).reshape(2, d), 1)
        vecs = lax.psum(small[0], ("dp", "tensor"))
    return (out, gx, dwq, dqvb, dwo, vecs[0], vecs[1], vecs[2], dup, dupb, ddn, vecs[3], vecs[4], vecs[5])


def solution(mesh):
    comm = mesh.shape["dp"] == 16 and mesh.shape["tensor"] == 2
    rows = P(("dp", "tensor"), None)
    in_specs = (rows, P(None, None, "tensor"), P(None, "tensor"), P("tensor", None), P(), P(), P(), P(None, "tensor"),
                P("tensor"), P("tensor", None), P(), P(), P(), rows, P("dp"))
    out_specs = (rows, rows, P(None, None, "tensor"), P(None, "tensor"), P("tensor", None), P(), P(), P(),
                 P(None, "tensor"), P("tensor"), P("tensor", None), P(), P(), P())
    return jax.shard_map(functools.partial(on_device, comm), mesh=mesh, in_specs=in_specs, out_specs=out_specs,
                         check_vma=False)
```

```python
import functools
import math

import jax
import jax.numpy as jnp
from jax import lax
from jax.experimental import pallas as pl
from jax.experimental.pallas import tpu as pltpu
from jax.sharding import PartitionSpec as P

F32 = jnp.float32
BF = jnp.bfloat16
LMAX = 160
HDIM = 64
EPS = 1e-12
NEG = -1e30
MESH = pl.DeviceIdType.MESH
VMEM_LIMIT = 60 << 20

ERF_P = 0.3275911 * math.sqrt(0.5)
ERF_A = (0.254829592, -0.284496736, 1.421413741, -1.453152027, 1.061405429)


def dot(a, b):
    return lax.dot_general(a, b, (((1,), (0,)), ((), ())), preferred_element_type=F32)


def dot_nt(a, b):
    return lax.dot_general(a, b, (((1,), (1,)), ((), ())), preferred_element_type=F32)


def gelu_parts(v):
    bell = jnp.exp(v * v * -0.5)
    t = 1.0 / (1.0 + ERF_P * jnp.abs(v))
    tail = 0.5 * ERF_A[4]
    for a in ERF_A[3::-1]:
        tail = tail * t + 0.5 * a
    tail = tail * t * bell
    phi = jnp.where(v >= 0, 1.0 - tail, tail)
    return v * phi, phi + v * (bell * (1.0 / math.sqrt(2.0 * math.pi)))


def row_mean(x):
    return jnp.sum(x, axis=1, keepdims=True) * (1.0 / x.shape[1])


def col_sum(x):
    return jnp.sum(x, axis=0, keepdims=True)


def lane_head(width):
    return lax.broadcasted_iota(jnp.int32, (1, width), 1) // HDIM


def stack_heads(x):
    head = lane_head(x.shape[1])
    return jnp.concatenate(
        [jnp.where(head == h, x, jnp.zeros_like(x)) for h in range(x.shape[1] // HDIM)], axis=0
    )


def pick_heads(x):
    heads = x.shape[1] // HDIM
    r = x.shape[0] // heads
    head = lane_head(x.shape[1])
    out = x[:r]
    for h in range(1, heads):
        out = jnp.where(head == h, x[h * r : (h + 1) * r], out)
    return out


def places():
    dp = lax.axis_index("dp")
    return dp // 4, (dp // 2) % 2, dp % 2, lax.axis_index("tensor")


def at(z, y, core, x):
    return (z * 4 + y * 2 + core, x)


def enter(neighbours):
    barrier = pltpu.get_barrier_semaphore()
    for device in neighbours:
        pl.semaphore_signal(barrier, inc=1, device_id=device, device_id_type=MESH)
    pl.semaphore_wait(barrier, len(neighbours))


def remote(src, dst, sems, slot, device):
    return pltpu.make_async_remote_copy(
        src_ref=src, dst_ref=dst, send_sem=sems.at[0, slot], recv_sem=sems.at[1, slot],
        device_id=device, device_id_type=MESH,
    )


class Gather:
    PARTS = {
        "qa": (0, (slice(None),), (0,), True), "qb": (0, (slice(None),), (1,), True), "bias": (4, (), (), False),
        "wo": (1, (), (), False), "ua": (2, (), (0,), True), "ub": (2, (), (1,), True), "da": (3, (), (0,), True),
        "db": (3, (), (1,), True),
    }

    def __init__(self, own, other, sems):
        z, y, core, x = places()
        self.px, self.py, self.pc = at(z, y, core, 1 - x), at(z, 1 - y, core, x), at(z, y, 1 - core, x)
        self.own, self.other, self.sems = own, other, sems
        self.y, self.core = y, core

    def copy(self, name, stage):
        array, before, after, split = self.PARTS[name]
        own, other = self.own[array], self.other[array]
        lines = (self.y, 1 - self.y) if split else (None, None)
        here, there = (before + ((y,) if split else ()) + (self.core,) + after for y in lines)
        src, part, device = (
            (own, here, self.px), (other, here, self.py), (other, here, self.pc), (other, there, self.pc)
        )[stage]
        slot = 4 * list(self.PARTS).index(name) + stage
        return remote(src.at[part], other.at[part], self.sems, slot, device)

    def stages(self, name):
        return (0, 1, 2, 3) if self.PARTS[name][3] else (0, 2)

    def fetch(self, name):
        self.copy(name, 0).start()

    def spread(self, name):
        self.copy(name, 0).wait_recv()
        for stage in self.stages(name)[1:-1] if self.PARTS[name][3] else (2,):
            self.copy(name, stage).start()

    def finish(self, name):
        self.copy(name, 1).wait_recv()
        self.copy(name, 3).start()

    def arrived(self, name):
        for stage in self.stages(name)[2:] if self.PARTS[name][3] else (2,):
            self.copy(name, stage).wait_recv()

    def sent(self, name):
        for stage in self.stages(name):
            self.copy(name, stage).wait_send()


GATHER_PLAN = {
    0: ("fetch qa", "fetch qb", "fetch bias", "fetch wo", "fetch ua", "fetch ub", "fetch da", "fetch db",),
    4: ("spread qa",),
    5: ("spread qb",),
    6: ("spread bias",),
    7: ("finish qa", "spread wo",),
    8: ("finish qb", "spread ua", "arrived qa", "arrived qb", "arrived bias", "arrived wo",),
    9: ("spread ub",),
    11: ("finish ua", "spread da",),
    12: ("spread db",),
    13: ("finish ub",),
    14: ("finish da",),
}
GATHER_END = ("arrived ua", "arrived ub", "finish db", "arrived da", "arrived db",)


def attn_fwd_kernel(comm, *refs):
    if comm:
        (lens_ref, x_ref, wq_ref, wo_ref, bias_ref, ob_ref, wq_any, wo_any, up_any, dn_any,
         h1_ref, qkv_ref, att_ref, p_ref, xT_ref, wq_out, wo_out, up_out, dn_out, bias_out,
         att_s, wq_s, wo_s, bias_s, sems, local) = refs
    else:
        (lens_ref, x_ref, wq_ref, wo_ref, bias_ref, ob_ref, wq_s, wo_s, bias_s,
         h1_ref, qkv_ref, att_ref, p_ref, xT_ref, att_s) = refs
    p, i = pl.program_id(0), pl.program_id(1)
    rows, d = h1_ref.shape
    block = rows // LMAX
    half = d // 2
    sub = x_ref.shape[0] // rows
    if comm:
        gather = Gather((wq_any, wo_any, up_any, dn_any, bias_ref), (wq_s, wo_s, up_out, dn_out, bias_s), sems)
        step = p * pl.num_programs(1) + i
        keep = [pltpu.make_async_copy(a, b, local.at[k]) for k, (a, b) in enumerate(
            ((wq_s, wq_out), (wo_s, wo_out), (bias_s, bias_out)))]

        def follow(plan):
            for entry in plan:
                action, name = entry.split()
                getattr(gather, action)(name)

        @pl.when(step == 0)
        def _():
            enter((gather.px, gather.py, gather.pc))

        for at_step, plan in GATHER_PLAN.items():
            pl.when(step == at_step)(functools.partial(follow, plan))

        @pl.when(step == 8)
        def _():
            for copy in keep:
                copy.start()

    x = x_ref[pl.ds(lax.rem(i, sub) * rows, rows), :] if sub > 1 else x_ref[...]
    first = lax.axis_index("tensor") * (pl.num_programs(1) * block)
    kpos = lax.broadcasted_iota(jnp.int32, (LMAX, 1), 0)

    def heads(wq, bias_of):
        for j in range(3):
            t = dot(x, wq[j].reshape(d, half))
            if j != 1:
                t += lanes(bias_of, j * half // 256, half)
            t = t.astype(BF)
            if j == 0:
                t = t * jnp.asarray(1.0 / math.sqrt(HDIM), BF)
            qkv_ref[j, 0] = t
        for c in range(block):
            rs = slice(c * LMAX, (c + 1) * LMAX)
            bias = jnp.where(kpos < lens_ref[first + i * block + c], 0.0, NEG).astype(F32)
            st = dot_nt(qkv_ref[1, 0, rs, :], stack_heads(qkv_ref[0, 0, rs, :])) + bias
            e = jnp.exp(st - jnp.max(st, axis=0, keepdims=True))
            probs = (e * (1.0 / jnp.sum(e, axis=0, keepdims=True))).astype(BF)
            p_ref[c, 0] = probs
            o = pick_heads(dot(probs.T, qkv_ref[2, 0, rs, :])).astype(BF)
            att_ref[0, rs, :] = o

    @pl.when(p == 0)
    def _():
        heads(wq_ref, bias_ref)
        att_s[i] = att_ref[0]

        @pl.when(lax.rem(i, sub) == 0)
        def _():
            xT_ref[...] = x_ref[...].T

    @pl.when(p == 1)
    def _():
        heads(wq_s, bias_s)
        wo = wo_s[...].reshape(half, d)
        h1_ref[...] = x.astype(F32) + dot(att_s[i], wo_ref[...]) + dot(att_ref[0], wo) + ob_ref[...]

    if comm:

        @pl.when(step == 2 * pl.num_programs(1) - 1)
        def _():
            follow(GATHER_END)
            for copy in keep:
                copy.wait()
            for name in gather.PARTS:
                gather.sent(name)


def lanes(ref, line, width):
    parts = [ref[k // 16, k // 8 % 2, k % 8 : k % 8 + 1, :] for k in range(line, line + width // 128)]
    return parts[0] if len(parts) == 1 else jnp.concatenate(parts, axis=1)


def once(shape):
    return pl.BlockSpec(shape, lambda *_: (0,) * len(shape), pipeline_mode=pl.Buffered(1))


ANY = pl.BlockSpec(memory_space=pl.ANY)
SMEM = pl.BlockSpec(memory_space=pltpu.SMEM)


def attn_fwd(comm, block, lens, x, wq, wo, bias, ob, others):
    rows, d = x.shape
    half, r = d // 2, block * LMAX
    n = rows // r
    sds = jax.ShapeDtypeStruct
    sub = 2 if n % 2 == 0 else 1
    in_specs = [SMEM, pl.BlockSpec((sub * r, d), lambda p, i: (i // sub, 0)), once((3, d, half)), once((half, d)), once(bias.shape), once((1, d))]
    out_specs = [
        pl.BlockSpec((r, d), lambda p, i: (i * p, 0)),
        pl.BlockSpec((3, 1, r, half), lambda p, i: (0, p, i, 0)),
        pl.BlockSpec((1, r, half), lambda p, i: (p, i, 0)),
        pl.BlockSpec((block, 1, LMAX, half // HDIM * LMAX), lambda p, i: (i, p, 0, 0)),
        pl.BlockSpec((d, sub * r), lambda p, i: (0, (i * (1 - p) + (n - 1) * p) // sub)),
    ]
    out_shape = [
        sds((rows, d), F32),
        sds((3, 2, rows, half), BF),
        sds((2, rows, half), BF),
        sds((rows // LMAX, 2, LMAX, half // HDIM * LMAX), BF),
        sds((d, rows), BF),
    ]
    scratch = [pltpu.VMEM((n, r, half), BF)]
    args = [lens, x, wq, wo, bias, ob]
    if comm:
        in_specs += [ANY] * 4
        out_specs += [ANY] * 5
        out_shape += [sds(a.shape, a.dtype) for a in others + (bias,)]
        scratch += [pltpu.VMEM(a.shape, a.dtype) for a in others[:2] + (bias,)]
        scratch += [pltpu.SemaphoreType.DMA((2, 32)), pltpu.SemaphoreType.DMA((3,))]
    else:
        in_specs += [once((3, d, half)), once((half, d)), once(bias.shape)]
    params = dict(vmem_limit_bytes=VMEM_LIMIT)
    if comm:
        params.update(collective_id=0, has_side_effects=True)
    return pl.pallas_call(
        functools.partial(attn_fwd_kernel, comm), grid=(2, n), in_specs=in_specs, out_specs=out_specs,
        out_shape=out_shape, scratch_shapes=scratch, compiler_params=pltpu.CompilerParams(**params),
        name="attention_forward",
    )(*args, *others)


def ffn_kernel(CH, lens_ref, h1_ref, og_ref, upa_ref, upb_ref, dna_ref, dnb_ref, ba_ref, bb_ref,
               gain1_ref, shift1_ref, bias_dn_ref, gain2_ref, shift2_ref,
               out_ref, gone_ref, goneT_ref, dup_ref, ddn_ref, small_ref,
               act_s, slope_s, nT_s, gT_s, acc_s, dup_s, ddn_s):
    i, n = pl.program_id(0), pl.num_programs(0)
    R, D = h1_ref.shape
    hid = upa_ref.shape[1]
    chunks = [(r, k * CH) for r in range(2) for k in range(hid // CH)]
    ups, dns, biases = (upa_ref, upb_ref), (dna_ref, dnb_ref), (ba_ref, bb_ref)

    @pl.when(i == 0)
    def _():
        dup_s[...] = jnp.zeros_like(dup_s)
        ddn_s[...] = jnp.zeros_like(ddn_s)
        small_ref[...] = jnp.zeros_like(small_ref)

    gain1, shift1, bias_dn, gain2, shift2 = (
        ref[...] for ref in (gain1_ref, shift1_ref, bias_dn_ref, gain2_ref, shift2_ref))
    h = h1_ref[...]
    c = h - row_mean(h)
    inv1 = lax.rsqrt(row_mean(c * c) + EPS)
    n1 = c * inv1
    normed = n1 * gain1 + shift1
    nlow = normed.astype(BF)
    nT_s[...] = nlow.T

    def up(chunk):
        r, s = chunk
        return dot(nlow, ups[r][:, s : s + CH]) + lanes(biases[r], (D + s) // 128, CH)

    pre = up(chunks[0])
    for k, (r, s) in enumerate(chunks):
        nxt = up(chunks[k + 1]) if k + 1 < len(chunks) else None
        a, sl = gelu_parts(pre)
        a = a.astype(BF)
        act_s[r, :, s : s + CH] = a
        slope_s[r, :, s : s + CH] = sl
        t = dot(a, dns[r][s : s + CH, :])
        if k == 0:
            acc_s[...] = t
        else:
            acc_s[...] += t
        pre = nxt
    h2 = normed + acc_s[...] + bias_dn
    c2 = h2 - row_mean(h2)
    inv2 = lax.rsqrt(row_mean(c2 * c2) + EPS)
    n2 = c2 * inv2
    out_ref[...] = (n2 * gain2 + shift2).astype(BF)

    row = i * R + lax.broadcasted_iota(jnp.int32, (R, 1), 0)
    live = jnp.zeros((R, 1), F32)
    first = (i * R) // LMAX
    for j in range((R - 2) // LMAX + 2):
        ch = jnp.minimum(first + j, n * R // LMAX - 1)
        length = lens_ref[lax.axis_index("tensor") * (n * R // LMAX) + ch]
        live = jnp.where((row >= ch * LMAX) & (row < ch * LMAX + length), 1.0, live)
    go = og_ref[...].astype(F32) * live
    small_ref[0, 4:5, :] += col_sum(go * n2)
    small_ref[0, 5:6, :] += col_sum(go)
    e = go * gain2
    gtwo = inv2 * (e - row_mean(e) - n2 * row_mean(e * n2))
    small_ref[0, 3:4, :] += col_sum(gtwo)
    glow = gtwo.astype(BF)
    gT_s[...] = glow.T

    def gact(chunk):
        r, s = chunk
        return dot_nt(glow, dns[r][s : s + CH, :])

    ga = gact(chunks[0])
    for k, (r, s) in enumerate(chunks):
        nxt = gact(chunks[k + 1]) if k + 1 < len(chunks) else None
        cs = slice(s, s + CH)
        gp = (ga * slope_s[r, :, cs]).astype(BF)
        ddn_s[r, :, cs] += dot(gT_s[...], act_s[r, :, cs])
        dup_s[r, :, cs] += dot(nT_s[...], gp)
        total = col_sum(gp.astype(F32))
        for o in range(0, CH, min(CH, D)):
            w = min(CH, D)
            line, lane = (s + o) // D, (s + o) % D
            small_ref[1 + r, line : line + 1, lane : lane + w] += total[:, o : o + w]
        t = dot_nt(gp, ups[r][:, cs])
        if k == 0:
            acc_s[...] = t
        else:
            acc_s[...] += t
        ga = nxt
    gin = gtwo + acc_s[...]
    small_ref[0, 1:2, :] += col_sum(gin * n1)
    small_ref[0, 2:3, :] += col_sum(gin)
    e = gin * gain1
    gone = inv1 * (e - row_mean(e) - n1 * row_mean(e * n1))
    small_ref[0, 0:1, :] += col_sum(gone)
    gone_ref[...] = gone
    goneT_ref[...] = gone.astype(BF).T

    @pl.when(i == n - 1)
    def _():
        dup_ref[...] = dup_s[...].astype(BF)
        ddn_ref[...] = ddn_s[...].astype(BF)


def ffn(R, CH, lens, h1, og, ups, dns, bias, vecs):
    rows, D = h1.shape
    hid = ups[0].shape[1]
    sds = jax.ShapeDtypeStruct
    row = pl.BlockSpec((R, D), lambda i: (i, 0))
    return pl.pallas_call(
        functools.partial(ffn_kernel, CH), grid=(rows // R,),
        in_specs=[SMEM, row, row, once((D, hid)), once((D, hid)), once((hid, D)), once((hid, D)),
                  once(bias[0].shape), once(bias[1].shape)] + [once((1, D))] * 5,
        out_specs=[row, row, pl.BlockSpec((D, R), lambda i: (0, i)), once((2, D, hid)), once((2, D, hid)), once((3, 8, D))],
        out_shape=[sds((rows, D), BF), sds((rows, D), F32), sds((D, rows), BF), sds((2, D, hid), BF), sds((2, D, hid), BF),
                   sds((3, 8, D), F32)],
        scratch_shapes=[pltpu.VMEM((2, R, hid), BF), pltpu.VMEM((2, R, hid), F32), pltpu.VMEM((D, R), BF),
                        pltpu.VMEM((D, R), BF), pltpu.VMEM((R, D), F32), pltpu.VMEM((2, D, hid), F32),
                        pltpu.VMEM((2, D, hid), F32)],
        compiler_params=pltpu.CompilerParams(vmem_limit_bytes=VMEM_LIMIT), name="feed_forward",
    )(lens, h1, og, *ups, *dns, *bias, *vecs)


def add_low(dst, a, b):
    lead = dst.shape[:-2]
    total = math.prod(lead)

    def one(k, carry):
        idx = []
        for s in reversed(lead):
            idx.append(k % s)
            k = k // s
        idx = tuple(reversed(idx))
        dst[idx] = (a[idx].astype(F32) + b[idx].astype(F32)).astype(BF)
        return carry

    if total == 1:
        idx = (0,) * len(lead)
        dst[idx] = (a[idx].astype(F32) + b[idx].astype(F32)).astype(BF)
    else:
        lax.fori_loop(0, total, one, 0)


class Reduce:
    def __init__(self, src, width, order, bufs, sems, base):
        self.z, self.y, self.core, self.x = places()
        z, y, core, x = self.z, self.y, self.core, self.x
        self.src, self.order, self.sems, self.base = src, order, sems, base
        self.rc, self.h, self.r1, self.w, self.r2, self.v, self.rz, self.full = bufs
        self.px, self.py, self.pc = at(z, y, core, 1 - x), at(z, 1 - y, core, x), at(z, y, 1 - core, x)

    def zdev(self, d):
        zt = lax.rem(self.z + d, 4)
        return zt, at(zt, self.y, self.core, self.x)

    def copies(self, stage):
        b, y, core, z = self.base, self.y, self.core, self.z
        if stage == 0:
            return [remote(self.src.at[:, 1 - core], self.rc, self.sems, b, self.pc)]
        if stage == 1:
            if self.order == "xy":
                return [remote(self.h.at[1], self.r1, self.sems, b + 1, self.px)]
            return [remote(self.h.at[:, 1 - y], self.r1, self.sems, b + 1, self.py)]
        if stage == 2:
            if self.order == "xy":
                return [remote(self.w.at[1 - y], self.r2, self.sems, b + 2, self.py)]
            return [remote(self.w.at[1], self.r2, self.sems, b + 2, self.px)]
        if stage == 3:
            out = []
            for d in (1, 2, 3):
                zt, dev = self.zdev(d)
                out.append(remote(self.v.at[zt], self.rz.at[d - 1], self.sems, b + 2 + d, dev))
            return out
        if stage == 4:
            out = []
            for d in (1, 2, 3):
                zt, dev = self.zdev(d)
                part = self.full.at[core, y, z]
                out.append(remote(part, part, self.sems, b + 5 + d, dev))
            return out
        if stage == 5:
            part = self.full.at[core, y]
            return [remote(part, part, self.sems, b + 9, self.py)]
        part = self.full.at[core]
        return [remote(part, part, self.sems, b + 10, self.pc)]

    def start(self, stage):
        for copy in self.copies(stage):
            copy.start()

    def combine(self, stage):
        y, core, z = self.y, self.core, self.z
        if stage == 0:
            add_low(self.h, self.src.at[:, core], self.rc)
        elif stage == 1:
            add_low(self.w, self.h.at[0] if self.order == "xy" else self.h.at[:, y], self.r1)
        elif stage == 2:
            mine = self.w.at[y] if self.order == "xy" else self.w.at[0]
            self.v[...] = (mine[...].astype(F32) + self.r2[...].astype(F32)).astype(BF).reshape(self.v.shape)
        elif stage == 3:
            s = self.v[z].astype(F32)
            for d in range(3):
                s = s + self.rz[d].astype(F32)
            self.full[core, y, z] = s.astype(BF)

    def take(self, stage):
        for copy in self.copies(stage):
            copy.wait()
        self.combine(stage)

    def step(self, stage):
        self.take(stage)
        if stage < 6:
            self.start(stage + 1)


def reduce_bufs(width, order, rows=128):
    first = (2, rows, width)
    return [pltpu.VMEM(s, BF) for s in (
        (2, 2, rows, width), (2, 2, rows, width), first, first, (rows, width), (4, rows // 4, width),
        (3, rows // 4, width), (2, 2, 4, rows // 4, width))]


class ReduceOwn(Reduce):
    def __init__(self, src_other, src_own, width, bufs, sems, base):
        Reduce.__init__(self, None, width, "xy", (None, None) + tuple(bufs[4:]), sems, base)
        self.srcs = (src_own, src_other)
        self.rcs, self.hs = bufs[0:2], bufs[2:4]

    def copies(self, stage):
        b = self.base
        if stage == "other":
            return [remote(self.srcs[1].at[1 - self.core], self.rcs[1], self.sems, b + 11, self.pc)]
        if stage == "own":
            return [remote(self.srcs[0].at[1 - self.core], self.rcs[0], self.sems, b, self.pc)]
        if stage == 1:
            return [remote(self.hs[1], self.r1, self.sems, b + 1, self.px)]
        return Reduce.copies(self, stage)

    def combine(self, stage):
        if stage == "other":
            add_low(self.hs[1], self.srcs[1].at[self.core], self.rcs[1])
        elif stage == "own":
            add_low(self.hs[0], self.srcs[0].at[self.core], self.rcs[0])
        elif stage == 1:
            add_low(self.w, self.hs[0], self.r1)
        else:
            Reduce.combine(self, stage)

    def step(self, stage):
        if stage == "other":
            self.take(stage)
            self.start(1)
        elif stage == "own":
            self.take(stage)
            self.take(1)
            self.start(2)
        else:
            Reduce.step(self, stage)


def reduce_own_bufs(width, rows):
    pair = (2, rows, width)
    return [pltpu.VMEM(s, BF) for s in (
        pair, pair, pair, pair, pair, pair, (rows, width), (4, rows // 4, width), (3, rows // 4, width),
        (2, 2, 4, rows // 4, width))]


class Butterfly:
    def __init__(self, acc, recv, sems, base):
        z, y, core, x = places()
        self.acc, self.recv, self.sems, self.base = acc, recv, sems, base
        self.devices = (at(z, y, 1 - core, x), at(z, y, core, 1 - x), at(z, 1 - y, core, x),
                        at(z + 1 - 2 * (z % 2), y, core, x), at((z + 2) % 4, y, core, x))

    def copy(self, k):
        return remote(self.acc.at[k], self.recv.at[k], self.sems, self.base + k, self.devices[k])

    def start(self, k):
        self.copy(k).start()

    def take(self, k):
        self.copy(k).wait()
        if k == 1:
            self.acc[k + 1, 0] = self.acc[k, 0] + self.recv[k, 0]
            self.acc[k + 1, 1] = self.acc[k, 1] + self.recv[k, 2]
            self.acc[k + 1, 2] = self.acc[k, 2] + self.recv[k, 1]
        else:
            self.acc[k + 1] = self.acc[k] + self.recv[k]

    def step(self, k):
        self.take(k)
        if k < 4:
            self.start(k + 1)


PLAN = {
    2: ("D0 0",),
    3: ("U1 0", "D1 0",),
    6: ("D0 1", "U0 0",),
    7: ("U1 1",),
    8: ("D0 2",),
    9: ("D1 1", "U1 2", "O 0",),
    10: ("U0 1", "Qk other",),
    11: ("Qq other", "Qv other", "D0 3",),
    12: ("D1 2",),
    13: ("O 1", "U0 2", "U1 3",),
    15: ("D0 4", "O 2",),
}
TAIL_PLAN = {
    0: ("D1 3", "Qq own", "U0 3", "Qk own",),
    1: ("Qv own", "F 0",),
    2: ("U1 4", "Qq 2", "Qk 2", "Qv 2", "D1 4", "O 3",),
    3: ("D0 5", "Qq 3", "F 1", "D0 6", "U0 4", "Qk 3", "Qv 3", "F 2", "U1 5", "D1 5", "O 4", "Qq 4", "U1 6",),
    4: ("U0 5", "Qk 4", "O 5", "D1 6", "Qv 4", "F 3", "F 4", "Qk 5", "Qq 5", "Qv 5", "Qk 6", "U0 6", "O 6", "Qq 6", "Qv 6",),
}


def attn_bwd_kernel(comm, n, m, *refs):
    (gone_ref, grow_ref, qkv_ref, p_ref, wqa_ref, wqb_ref, woa_ref, wob_ref, xT_any, gT_any, att_any) = refs[:11]
    refs = refs[11:]
    if comm:
        up_ref, dn_ref, small_ref = refs[:3]
        gx_ref, up_out, dn_out, wo_out, wq_out, small_out = refs[3:9]
        dq_s, xT_s, gT_s, att_s, local, wo_src, q_oth, q_own, acc, recv, sems = refs[9:20]
        bufs = refs[20:]
    else:
        gx_ref, wo_out, wq_out, bias_out = refs[:4]
        dq_s, xT_s, gT_s, att_s, local = refs[4:]
    s = pl.program_id(0)
    r, d = gone_ref.shape
    block = r // LMAX
    half = d // 2
    loads = [pltpu.make_async_copy(a, b, local.at[k]) for k, (a, b) in enumerate(
        ((xT_any, xT_s), (gT_any, gT_s), (att_any, att_s)))]

    if comm:
        w = up_ref.shape[-1] // 2
        pieces = {}
        for k in range(2):
            cols = pl.ds(k * w, w)
            pieces["U%d" % k] = Reduce(up_ref.at[..., cols], w, 'xy', bufs[8 * k : 8 * k + 8], sems, 11 * k)
            pieces["D%d" % k] = Reduce(
                dn_ref.at[..., cols], w, 'yx', bufs[16 + 8 * k : 24 + 8 * k], sems, 22 + 11 * k)
        pieces["O"] = Reduce(wo_src, half, "xy", bufs[32:40], sems, 44)
        for k, name in enumerate("qkv"):
            pieces["Q" + name] = ReduceOwn(
                q_oth.at[k], q_own.at[k], half, bufs[40 + 10 * k : 50 + 10 * k], sems, 55 + 12 * k)
        pieces["F"] = fly = Butterfly(acc, recv, sems, 91)
        first = pieces["U0"]

        def follow(plan):
            for entry in plan:
                name, stage = entry.split()
                pieces[name].step(int(stage) if stage.isdigit() else stage)

        @pl.when(s == 0)
        def _():
            enter(fly.devices[:3] + tuple(first.zdev(k)[1] for k in (1, 2, 3)))
            for name in ("U0", "D0", "U1", "D1"):
                pieces[name].start(0)
            acc[0] = small_ref[...]

        for at_step, plan in PLAN.items():
            pl.when(s == at_step)(functools.partial(follow, plan))
        for at_step, plan in TAIL_PLAN.items():
            if at_step < m:
                pl.when(s == 2 * n + at_step)(functools.partial(follow, plan))

    @pl.when(s == 0)
    def _():
        for copy in loads:
            copy.start()
        if not comm:
            bias_out[...] = jnp.zeros_like(bias_out)

    def quarters(dst, value):
        for core in range(2):
            for y in range(2):
                first_row = (core * 2 + y) * (d // 4)
                dst[core, y] = value[first_row : first_row + d // 4]

    @pl.when(s == min(2, n - 1))
    def _():
        loads[1].wait()
        loads[2].wait()
        for rel in range(2):
            total = dot(gT_s[...], att_s[rel]).astype(BF)
            if comm:
                quarters(wo_src.at[rel], total)
            else:
                wo_out[rel] = total
        if comm:
            pieces["O"].start(0)

    def heads(wo, which, blk):
        ga = dot_nt(gone_ref[...].astype(BF), wo).astype(BF)
        for c in range(block):
            rs = slice(c * LMAX, (c + 1) * LMAX)
            probs = p_ref[c, 0]
            k, v = qkv_ref[1, 0, rs, :], qkv_ref[2, 0, rs, :]
            gs = stack_heads(ga[rs])
            dp = dot_nt(v, gs)
            pf = probs.astype(F32)
            ds = (pf * (dp - jnp.sum(pf * dp, axis=0, keepdims=True))).astype(BF)
            dv = dot(probs, gs)
            dk = dot(ds, stack_heads(qkv_ref[0, 0, rs, :]))
            dq = pick_heads(dot(ds.T, k)) * (1.0 / math.sqrt(HDIM))
            out = pl.ds(blk * r + c * LMAX, LMAX)
            dq_s[which, 0, out, :] = dq.astype(BF)
            dq_s[which, 1, out, :] = dk.astype(BF)
            dq_s[which, 2, out, :] = dv.astype(BF)

    def weights(which):
        for j in range(3):
            total = dot(xT_s[...], dq_s[which, j]).astype(BF)
            if comm:
                quarters((q_own, q_oth)[which].at[j], total)
                if which == 1:
                    pieces["Q" + "qkv"[j]].start("other")
                else:
                    pieces["Q" + "qkv"[j]].start("own")
            else:
                wq_out[which, j] = total
        ref, base = (acc.at[0], 1) if comm else (bias_out, 0)
        ref[base + which, 2:3, 0:half] = col_sum(dq_s[which, 0].astype(F32))
        ref[base + which, 2:3, half:d] = col_sum(dq_s[which, 2].astype(F32))

    @pl.when(s < n)
    def _():
        heads(wob_ref[...].reshape(half, d), 1, s)

        @pl.when(s == n - 1)
        def _():
            loads[0].wait()
            weights(1)

    @pl.when((s >= n) & (s < 2 * n))
    def _():
        heads(woa_ref[...], 0, s - n)

        @pl.when(s == 2 * n - 1)
        def _():
            weights(0)
            if comm:
                fly.start(0)

    @pl.when(s >= 2 * n)
    def _():
        rg = gx_ref.shape[0]
        rs = pl.ds((s - 2 * n) * rg, rg)
        total = grow_ref[...]
        for which, wq in ((1, wqb_ref), (0, wqa_ref)):
            for j in range(3):
                total += dot_nt(dq_s[which, j, rs, :], wq[j].reshape(d, half))
        gx_ref[...] = total.astype(BF)

    if comm:

        @pl.when(s == 2 * n + m - 1)
        def _():
            for at_step, plan in TAIL_PLAN.items():
                if at_step >= m:
                    follow(plan)
            for k in range(2):
                up_out[..., k * w : (k + 1) * w] = pieces["U%d" % k].full[...]
                dn_out[..., k * w : (k + 1) * w] = pieces["D%d" % k].full[...]
            wo_out[...] = pieces["O"].full[...]
            for k, name in enumerate("qkv"):
                wq_out[k] = pieces["Q" + name].full[...]
            small_out[...] = acc[5]


def attn_bwd(comm, block, gone, goneT, xT, qkv, probs, att, wq, wo, sums):
    rows, d = gone.shape
    half, r = d // 2, block * LMAX
    n = rows // r
    rg = min(rows, 4 * LMAX)
    m = rows // rg
    sds = jax.ShapeDtypeStruct

    def blk(s):
        return jnp.where(s < 2 * n, lax.rem(s, n), n - 1)

    def rel(s):
        return jnp.where(s < n, 1, 0)

    def tail(s):
        return jnp.maximum(s - 2 * n, 0)

    in_specs = [
        pl.BlockSpec((r, d), lambda s: (blk(s), 0)),
        pl.BlockSpec((rg, d), lambda s: (tail(s), 0)),
        pl.BlockSpec((3, 1, r, half), lambda s: (0, rel(s), blk(s), 0)),
        pl.BlockSpec((block, 1, LMAX, half // HDIM * LMAX), lambda s: (blk(s), rel(s), 0, 0)),
        once(wq[0].shape), once(wq[1].shape), once(wo[0].shape), once(wo[1].shape), ANY, ANY, ANY,
    ]
    gx_spec, gx_shape = pl.BlockSpec((rg, d), lambda s: (tail(s), 0)), sds((rows, d), BF)
    scratch = [pltpu.VMEM((2, 3, rows, half), BF), pltpu.VMEM(xT.shape, BF), pltpu.VMEM(goneT.shape, BF),
               pltpu.VMEM(att.shape, BF), pltpu.SemaphoreType.DMA((3,))]
    params = dict(vmem_limit_bytes=VMEM_LIMIT)
    if comm:
        up, dn, small = sums
        hid = up.shape[-1]
        split = lambda w: (2, 2, 4, d // 16, w)
        in_specs += [once(up.shape), once(dn.shape), once(small.shape)]
        out_specs = [gx_spec, once(split(hid)), once(split(hid)), once(split(half)), once((3,) + split(half)),
                     once(small.shape)]
        out_shape = [gx_shape, sds(split(hid), BF), sds(split(hid), BF), sds(split(half), BF),
                     sds((3,) + split(half), BF), sds(small.shape, F32)]
        rows4 = d // 4
        scratch += [pltpu.VMEM((2, 2, 2, rows4, half), BF), pltpu.VMEM((3, 2, 2, rows4, half), BF),
                    pltpu.VMEM((3, 2, 2, rows4, half), BF), pltpu.VMEM((6,) + small.shape, F32),
                    pltpu.VMEM((5,) + small.shape, F32), pltpu.SemaphoreType.DMA((2, 96))]
        for _ in range(4):
            scratch += reduce_bufs(hid // 2, "xy", rows4)
        scratch += reduce_bufs(half, "xy", rows4)
        for _ in range(3):
            scratch += reduce_own_bufs(half, rows4)
        params.update(collective_id=1, has_side_effects=True)
    else:
        out_specs = [gx_spec, once((2, d, half)), once((2, 3, d, half)), once((2, 8, d))]
        out_shape = [gx_shape, sds((2, d, half), BF), sds((2, 3, d, half), BF), sds((2, 8, d), F32)]
    return pl.pallas_call(
        functools.partial(attn_bwd_kernel, comm, n, m), grid=(2 * n + m,), in_specs=in_specs, out_specs=out_specs,
        out_shape=out_shape, scratch_shapes=scratch, compiler_params=pltpu.CompilerParams(**params),
        name="attention_backward",
    )(gone, gone, qkv, probs, *wq, *wo, xT, goneT, att, *sums)


def finish_kernel(gx_ref, up_ref, dn_ref, wo_ref, wq_ref, small_ref, gx_out, up_out, dn_out, wo_out, wq_out,
                  upb_out, qvb_out, *vec_outs):
    gx_out[...] = gx_ref[...]
    up_out[...] = up_ref[...].astype(F32)
    dn_out[...] = dn_ref[...].astype(F32).T
    wq_out[...] = wq_ref[...].astype(F32)

    @pl.when(pl.program_id(0) == 0)
    def _():
        d = small_ref.shape[2]
        half = d // 2
        wo_out[...] = wo_ref[...].astype(F32).T
        for k, out in enumerate(vec_outs):
            out[...] = small_ref[0, k]
        for k in range(upb_out.shape[0] // d):
            upb_out[k * d : (k + 1) * d] = small_ref[1, k]
        qvb_out[0:1, :] = small_ref[1, 2:3, 0:half]
        qvb_out[1:2, :] = small_ref[1, 2:3, half:d]


def finish(gx, up, dn, wo, wq, small):
    rows, d = gx.shape
    hid, half = up.shape[1], wo.shape[1]
    n = 4
    sds = jax.ShapeDtypeStruct
    gx_spec = pl.BlockSpec((rows // n, d), lambda i: (i, 0))
    up_spec = pl.BlockSpec((d // n, hid), lambda i: (i, 0))
    wq_spec = pl.BlockSpec((3, d // n, half), lambda i: (0, i, 0))
    return pl.pallas_call(
        finish_kernel, grid=(n,),
        in_specs=[gx_spec, up_spec, pl.BlockSpec((d, hid // n), lambda i: (0, i)), once(wo.shape), wq_spec,
                  once(small.shape)],
        out_specs=[gx_spec, up_spec, pl.BlockSpec((hid // n, d), lambda i: (i, 0)), once((half, d)), wq_spec,
                   once((hid,)), once((2, half))] + [once((d,))] * 6,
        out_shape=[sds(gx.shape, BF), sds(up.shape, F32), sds((hid, d), F32), sds((half, d), F32), sds(wq.shape, F32),
                   sds((hid,), F32), sds((2, half), F32)] + [sds((d,), F32)] * 6,
        compiler_params=pltpu.CompilerParams(vmem_limit_bytes=VMEM_LIMIT), name="finish",
    )(gx, up, dn, wo, wq, small)


def tile_rows(rows):
    for r in (512, 640, 320):
        if rows % r == 0:
            return r
    return LMAX


def chain_block(chains):
    for c in (4, 2):
        if chains % c == 0:
            return c
    return 1


def on_device(comm, tokens, qkv_weight, qv_bias, out_weight, out_bias, gain_one, shift_one, up_weight, up_bias,
              down_weight, down_bias, gain_two, shift_two, out_grad, lengths):
    rows, d = tokens.shape
    chains = rows // LMAX
    half = d // 2
    vecs = [a[None] for a in (gain_one, shift_one, down_bias, gain_two, shift_two)]
    block = chain_block(chains)
    comm = comm and chains == 16

    def gather(a, dim):
        return lax.all_gather(a, "tensor", axis=dim, tiled=True)

    def table(qv, up):
        flat = jnp.concatenate([qv[0], qv[1], up]).astype(F32)
        return jnp.pad(flat, (0, 4096 - flat.shape[0])).reshape(2, 2, 8, 128)

    if comm:
        hid = up_weight.shape[1]
        bias = table(qv_bias, up_bias)
        quarters = (
            qkv_weight.reshape(3, 2, 2, 2, d // 8, half), out_weight.reshape(2, half // 2, d),
            up_weight.reshape(2, 2, 2, d // 8, hid), down_weight.reshape(2, 2, 2, hid // 8, d),
        )
        h1, qkv, att, probs, xT, wqb, wob, wupb, wdnb, bias_b = attn_fwd(
            True, 2, lengths, tokens, qkv_weight, out_weight, bias, out_bias[None], quarters)
        wqs, wos, bias = (qkv_weight, wqb), (out_weight, wob), (bias, bias_b)
        ups, dns = (up_weight, wupb.reshape(d, hid)), (down_weight, wdnb.reshape(hid, d))
    else:
        wq, wo = gather(qkv_weight, 2), gather(out_weight, 0)
        wup, wdn = gather(up_weight, 1), gather(down_weight, 0)
        hid = wup.shape[1] // 2
        qvb, upb = gather(qv_bias, 1), gather(up_bias, 0)
        bias = (table(qvb[:, :half], upb[:hid]), table(qvb[:, half:], upb[hid:]))
        wqs, wos = (wq[:, :, :half], wq[:, :, half:]), (wo[:half], wo[half:])
        ups, dns = (wup[:, :hid], wup[:, hid:]), (wdn[:hid], wdn[hid:])
        h1, qkv, att, probs, xT = attn_fwd(
            False, block, lengths, tokens, wqs[0], wos[0], bias[0], out_bias[None], (wqs[1], wos[1], bias[1]))
    out, gone, goneT, dup, ddn, small = ffn(tile_rows(rows), 256, lengths, h1, out_grad, ups, dns, bias, vecs)
    small_block = 2 if chains % 2 == 0 else 1
    if comm:
        split = (2, 2, 2, d // 4, hid)
        gx, dup, ddn, dwo, dwq, small = attn_bwd(
            True, small_block, gone, goneT, xT, qkv, probs, att, wqs, wos, (dup.reshape(split), ddn.reshape(split), small))
        gx, dup, ddn, dwo, dwq, dupb, dqvb, *vecs = finish(
            gx, dup.reshape(d, hid), ddn.reshape(d, hid), dwo.reshape(d, half), dwq.reshape(3, d, half), small)
    else:
        gx, dwo, dwq, dbias = attn_bwd(False, small_block, gone, goneT, xT, qkv, probs, att, wqs, wos, ())

        def total(a, dim):
            a = lax.psum_scatter(a.astype(BF), "tensor", scatter_dimension=dim, tiled=True)
            return lax.psum(a, "dp").astype(F32)

        dwq = total(dwq.transpose(1, 2, 0, 3).reshape(3, d, d), 2)
        dwo = total(jnp.concatenate([dwo[0], dwo[1]], axis=1), 1).T
        dup = total(jnp.concatenate([dup[0], dup[1]], axis=1), 1)
        ddn = total(jnp.concatenate([ddn[0], ddn[1]], axis=1), 1).T
        dupb = total(small[1:, : hid // d].reshape(2 * hid), 0)
        dqvb = total(dbias[:, 2].reshape(2, 2, half).transpose(1, 0, 2).reshape(2, d), 1)
        vecs = lax.psum(small[0], ("dp", "tensor"))
    return (out, gx, dwq, dqvb, dwo, vecs[0], vecs[1], vecs[2], dup, dupb, ddn, vecs[3], vecs[4], vecs[5])


def solution(mesh):
    comm = mesh.shape["dp"] == 16 and mesh.shape["tensor"] == 2
    rows = P(("dp", "tensor"), None)
    in_specs = (rows, P(None, None, "tensor"), P(None, "tensor"), P("tensor", None), P(), P(), P(), P(None, "tensor"),
                P("tensor"), P("tensor", None), P(), P(), P(), rows, P("dp"))
    out_specs = (rows, rows, P(None, None, "tensor"), P(None, "tensor"), P("tensor", None), P(), P(), P(),
                 P(None, "tensor"), P("tensor"), P("tensor", None), P(), P(), P())
    return jax.shard_map(functools.partial(on_device, comm), mesh=mesh, in_specs=in_specs, out_specs=out_specs,
                         check_vma=False)
```

```python
import functools
import math

import jax
import jax.numpy as jnp
from jax import lax
from jax.experimental import pallas as pl
from jax.experimental.pallas import tpu as pltpu
from jax.sharding import PartitionSpec as P

F32 = jnp.float32
BF = jnp.bfloat16
LMAX = 160
HDIM = 64
EPS = 1e-12
NEG = -1e30
MESH = pl.DeviceIdType.MESH
VMEM_LIMIT = 60 << 20

ERF_P = 0.3275911 * math.sqrt(0.5)
ERF_A = (0.254829592, -0.284496736, 1.421413741, -1.453152027, 1.061405429)


def dot(a, b):
    return lax.dot_general(a, b, (((1,), (0,)), ((), ())), preferred_element_type=F32)


def dot_nt(a, b):
    return lax.dot_general(a, b, (((1,), (1,)), ((), ())), preferred_element_type=F32)


def gelu_parts(v):
    bell = jnp.exp(v * v * -0.5)
    t = 1.0 / (1.0 + ERF_P * jnp.abs(v))
    tail = 0.5 * ERF_A[4]
    for a in ERF_A[3::-1]:
        tail = tail * t + 0.5 * a
    tail = tail * t * bell
    phi = jnp.where(v >= 0, 1.0 - tail, tail)
    return v * phi, phi + v * (bell * (1.0 / math.sqrt(2.0 * math.pi)))


def row_mean(x):
    return jnp.sum(x, axis=1, keepdims=True) * (1.0 / x.shape[1])


def col_sum(x):
    return jnp.sum(x, axis=0, keepdims=True)


def lane_head(width):
    return lax.broadcasted_iota(jnp.int32, (1, width), 1) // HDIM


def stack_heads(x):
    head = lane_head(x.shape[1])
    return jnp.concatenate(
        [jnp.where(head == h, x, jnp.zeros_like(x)) for h in range(x.shape[1] // HDIM)], axis=0
    )


def pick_heads(x):
    heads = x.shape[1] // HDIM
    r = x.shape[0] // heads
    head = lane_head(x.shape[1])
    out = x[:r]
    for h in range(1, heads):
        out = jnp.where(head == h, x[h * r : (h + 1) * r], out)
    return out


def places():
    dp = lax.axis_index("dp")
    return dp // 4, (dp // 2) % 2, dp % 2, lax.axis_index("tensor")


def at(z, y, core, x):
    return (z * 4 + y * 2 + core, x)


def enter(neighbours):
    barrier = pltpu.get_barrier_semaphore()
    for device in neighbours:
        pl.semaphore_signal(barrier, inc=1, device_id=device, device_id_type=MESH)
    pl.semaphore_wait(barrier, len(neighbours))


def remote(src, dst, sems, slot, device):
    return pltpu.make_async_remote_copy(
        src_ref=src, dst_ref=dst, send_sem=sems.at[0, slot], recv_sem=sems.at[1, slot],
        device_id=device, device_id_type=MESH,
    )


class Gather:
    PARTS = {
        "qa": (0, (slice(None),), (0,), True), "qb": (0, (slice(None),), (1,), True), "bias": (4, (), (), False),
        "wo": (1, (), (), False), "ua": (2, (), (0,), True), "ub": (2, (), (1,), True), "da": (3, (), (0,), True),
        "db": (3, (), (1,), True),
    }

    def __init__(self, own, other, sems):
        z, y, core, x = places()
        self.px, self.py, self.pc = at(z, y, core, 1 - x), at(z, 1 - y, core, x), at(z, y, 1 - core, x)
        self.own, self.other, self.sems = own, other, sems
        self.y, self.core = y, core

    def copy(self, name, stage):
        array, before, after, split = self.PARTS[name]
        own, other = self.own[array], self.other[array]
        lines = (self.y, 1 - self.y) if split else (None, None)
        here, there = (before + ((y,) if split else ()) + (self.core,) + after for y in lines)
        src, part, device = (
            (own, here, self.px), (other, here, self.py), (other, here, self.pc), (other, there, self.pc)
        )[stage]
        slot = 4 * list(self.PARTS).index(name) + stage
        return remote(src.at[part], other.at[part], self.sems, slot, device)

    def stages(self, name):
        return (0, 1, 2, 3) if self.PARTS[name][3] else (0, 2)

    def fetch(self, name):
        self.copy(name, 0).start()

    def spread(self, name):
        self.copy(name, 0).wait_recv()
        for stage in self.stages(name)[1:-1] if self.PARTS[name][3] else (2,):
            self.copy(name, stage).start()

    def finish(self, name):
        self.copy(name, 1).wait_recv()
        self.copy(name, 3).start()

    def arrived(self, name):
        for stage in self.stages(name)[2:] if self.PARTS[name][3] else (2,):
            self.copy(name, stage).wait_recv()

    def sent(self, name):
        for stage in self.stages(name):
            self.copy(name, stage).wait_send()


GATHER_PLAN = {
    0: ("fetch qa", "fetch qb", "fetch bias", "fetch wo", "fetch ua", "fetch ub", "fetch da", "fetch db",),
    4: ("spread qa",),
    5: ("spread qb",),
    6: ("spread bias",),
    7: ("finish qa", "spread wo",),
    8: ("finish qb", "spread ua", "arrived qa", "arrived qb", "arrived bias", "arrived wo",),
    9: ("spread ub",),
    11: ("finish ua", "spread da",),
    12: ("spread db",),
    13: ("finish ub",),
    14: ("finish da",),
}
GATHER_END = ("arrived ua", "arrived ub", "finish db", "arrived da", "arrived db",)


def attn_fwd_kernel(comm, *refs):
    if comm:
        (lens_ref, x_ref, wq_ref, wo_ref, qv_ref, ob_ref, wq_any, wo_any, up_any, dn_any, upb_ref,
         h1_ref, qkv_ref, att_ref, p_ref, xT_ref, wq_out, wo_out, up_out, dn_out, bias_out,
         own_out, att_s, wq_s, wo_s, bias_s, bias_ref, sems, local) = refs
    else:
        (lens_ref, x_ref, wq_ref, wo_ref, bias_ref, ob_ref, wq_s, wo_s, bias_s,
         h1_ref, qkv_ref, att_ref, p_ref, xT_ref, att_s) = refs
    p, i = pl.program_id(0), pl.program_id(1)
    rows, d = h1_ref.shape
    block = rows // LMAX
    half = d // 2
    sub = x_ref.shape[0] // rows
    if comm:
        gather = Gather((wq_any, wo_any, up_any, dn_any, bias_ref), (wq_s, wo_s, up_out, dn_out, bias_s), sems)
        step = p * pl.num_programs(1) + i
        keep = [pltpu.make_async_copy(a, b, local.at[k]) for k, (a, b) in enumerate(
            ((wq_s, wq_out), (wo_s, wo_out), (bias_s, bias_out)))]

        def follow(plan):
            for entry in plan:
                action, name = entry.split()
                getattr(gather, action)(name)

        @pl.when(step == 0)
        def _():
            bias_ref[...] = jnp.zeros_like(bias_ref)
            qv, up = qv_ref[...].astype(F32), upb_ref[...].astype(F32).reshape(-1, 128)
            lines = [qv[k : k + 1, o : o + 128] for k in range(2) for o in range(0, half, 128)]
            lines += [up[k : k + 1] for k in range(up.shape[0])]
            for k, line in enumerate(lines):
                bias_ref[k // 16, k // 8 % 2, k % 8 : k % 8 + 1, :] = line
            own_out[...] = bias_ref[...]
            enter((gather.px, gather.py, gather.pc))

        for at_step, plan in GATHER_PLAN.items():
            pl.when(step == at_step)(functools.partial(follow, plan))

        @pl.when(step == 8)
        def _():
            for copy in keep:
                copy.start()

    x = x_ref[pl.ds(lax.rem(i, sub) * rows, rows), :] if sub > 1 else x_ref[...]
    first = lax.axis_index("tensor") * (pl.num_programs(1) * block)
    kpos = lax.broadcasted_iota(jnp.int32, (LMAX, 1), 0)

    def heads(wq, bias_of):
        for j in range(3):
            t = dot(x, wq[j].reshape(d, half))
            if j != 1:
                t += lanes(bias_of, j * half // 256, half)
            t = t.astype(BF)
            if j == 0:
                t = t * jnp.asarray(1.0 / math.sqrt(HDIM), BF)
            qkv_ref[j, 0] = t
        for c in range(block):
            rs = slice(c * LMAX, (c + 1) * LMAX)
            bias = jnp.where(kpos < lens_ref[first + i * block + c], 0.0, NEG).astype(F32)
            st = dot_nt(qkv_ref[1, 0, rs, :], stack_heads(qkv_ref[0, 0, rs, :])) + bias
            e = jnp.exp(st - jnp.max(st, axis=0, keepdims=True))
            probs = (e * (1.0 / jnp.sum(e, axis=0, keepdims=True))).astype(BF)
            p_ref[c, 0] = probs
            o = pick_heads(dot(probs.T, qkv_ref[2, 0, rs, :])).astype(BF)
            att_ref[0, rs, :] = o

    @pl.when(p == 0)
    def _():
        heads(wq_ref, bias_ref)
        att_s[i] = att_ref[0]

        @pl.when(lax.rem(i, sub) == 0)
        def _():
            xT_ref[...] = x_ref[...].T

    @pl.when(p == 1)
    def _():
        heads(wq_s, bias_s)
        wo = wo_s[...].reshape(half, d)
        h1_ref[...] = x.astype(F32) + dot(att_s[i], wo_ref[...]) + dot(att_ref[0], wo) + ob_ref[...]

    if comm:

        @pl.when(step == 2 * pl.num_programs(1) - 1)
        def _():
            follow(GATHER_END)
            for copy in keep:
                copy.wait()
            for name in gather.PARTS:
                gather.sent(name)


def lanes(ref, line, width):
    parts = [ref[k // 16, k // 8 % 2, k % 8 : k % 8 + 1, :] for k in range(line, line + width // 128)]
    return parts[0] if len(parts) == 1 else jnp.concatenate(parts, axis=1)


def once(shape):
    return pl.BlockSpec(shape, lambda *_: (0,) * len(shape), pipeline_mode=pl.Buffered(1))


ANY = pl.BlockSpec(memory_space=pl.ANY)
SMEM = pl.BlockSpec(memory_space=pltpu.SMEM)


def attn_fwd(comm, block, lens, x, wq, wo, bias, ob, others):
    rows, d = x.shape
    half, r = d // 2, block * LMAX
    n = rows // r
    sds = jax.ShapeDtypeStruct
    sub = 2 if n % 2 == 0 else 1
    in_specs = [SMEM, pl.BlockSpec((sub * r, d), lambda p, i: (i // sub, 0)), once((3, d, half)), once((half, d)), once(bias.shape), once((1, d))]
    out_specs = [
        pl.BlockSpec((r, d), lambda p, i: (i * p, 0)),
        pl.BlockSpec((3, 1, r, half), lambda p, i: (0, p, i, 0)),
        pl.BlockSpec((1, r, half), lambda p, i: (p, i, 0)),
        pl.BlockSpec((block, 1, LMAX, half // HDIM * LMAX), lambda p, i: (i, p, 0, 0)),
        pl.BlockSpec((d, sub * r), lambda p, i: (0, (i * (1 - p) + (n - 1) * p) // sub)),
    ]
    out_shape = [
        sds((rows, d), F32),
        sds((3, 2, rows, half), BF),
        sds((2, rows, half), BF),
        sds((rows // LMAX, 2, LMAX, half // HDIM * LMAX), BF),
        sds((d, rows), BF),
    ]
    scratch = [pltpu.VMEM((n, r, half), BF)]
    args = [lens, x, wq, wo, bias, ob]
    if comm:
        table = sds((2, 2, 8, 128), F32)
        in_specs += [ANY] * 4 + [once(others[4].shape)]
        out_specs += [ANY] * 5 + [once(table.shape)]
        out_shape += [sds(a.shape, a.dtype) for a in others[:4]] + [table, table]
        scratch += [pltpu.VMEM(a.shape, a.dtype) for a in others[:2] + (table, table)]
        scratch += [pltpu.SemaphoreType.DMA((2, 32)), pltpu.SemaphoreType.DMA((3,))]
    else:
        in_specs += [once((3, d, half)), once((half, d)), once(bias.shape)]
    params = dict(vmem_limit_bytes=VMEM_LIMIT)
    if comm:
        params.update(collective_id=0, has_side_effects=True)
    return pl.pallas_call(
        functools.partial(attn_fwd_kernel, comm), grid=(2, n), in_specs=in_specs, out_specs=out_specs,
        out_shape=out_shape, scratch_shapes=scratch, compiler_params=pltpu.CompilerParams(**params),
        name="attention_forward",
    )(*args, *others)


def ffn_kernel(CH, lens_ref, h1_ref, og_ref, upa_ref, upb_ref, dna_ref, dnb_ref, ba_ref, bb_ref,
               gain1_ref, shift1_ref, bias_dn_ref, gain2_ref, shift2_ref,
               out_ref, gone_ref, goneT_ref, dup_ref, ddn_ref, small_ref,
               act_s, slope_s, nT_s, gT_s, acc_s, dup_s, ddn_s):
    i, n = pl.program_id(0), pl.num_programs(0)
    R, D = h1_ref.shape
    hid = upa_ref.shape[1]
    chunks = [(r, k * CH) for r in range(2) for k in range(hid // CH)]
    ups, dns, biases = (upa_ref, upb_ref), (dna_ref, dnb_ref), (ba_ref, bb_ref)

    @pl.when(i == 0)
    def _():
        dup_s[...] = jnp.zeros_like(dup_s)
        ddn_s[...] = jnp.zeros_like(ddn_s)
        small_ref[...] = jnp.zeros_like(small_ref)

    gain1, shift1, bias_dn, gain2, shift2 = (
        ref[...] for ref in (gain1_ref, shift1_ref, bias_dn_ref, gain2_ref, shift2_ref))
    h = h1_ref[...]
    c = h - row_mean(h)
    inv1 = lax.rsqrt(row_mean(c * c) + EPS)
    n1 = c * inv1
    normed = n1 * gain1 + shift1
    nlow = normed.astype(BF)
    nT_s[...] = nlow.T

    def up(chunk):
        r, s = chunk
        return dot(nlow, ups[r][:, s : s + CH]) + lanes(biases[r], (D + s) // 128, CH)

    pre = up(chunks[0])
    for k, (r, s) in enumerate(chunks):
        nxt = up(chunks[k + 1]) if k + 1 < len(chunks) else None
        a, sl = gelu_parts(pre)
        a = a.astype(BF)
        act_s[r, :, s : s + CH] = a
        slope_s[r, :, s : s + CH] = sl
        t = dot(a, dns[r][s : s + CH, :])
        if k == 0:
            acc_s[...] = t
        else:
            acc_s[...] += t
        pre = nxt
    h2 = normed + acc_s[...] + bias_dn
    c2 = h2 - row_mean(h2)
    inv2 = lax.rsqrt(row_mean(c2 * c2) + EPS)
    n2 = c2 * inv2
    out_ref[...] = (n2 * gain2 + shift2).astype(BF)

    row = i * R + lax.broadcasted_iota(jnp.int32, (R, 1), 0)
    live = jnp.zeros((R, 1), F32)
    first = (i * R) // LMAX
    for j in range((R - 2) // LMAX + 2):
        ch = jnp.minimum(first + j, n * R // LMAX - 1)
        length = lens_ref[lax.axis_index("tensor") * (n * R // LMAX) + ch]
        live = jnp.where((row >= ch * LMAX) & (row < ch * LMAX + length), 1.0, live)
    go = og_ref[...].astype(F32) * live
    small_ref[0, 4:5, :] += col_sum(go * n2)
    small_ref[0, 5:6, :] += col_sum(go)
    e = go * gain2
    gtwo = inv2 * (e - row_mean(e) - n2 * row_mean(e * n2))
    small_ref[0, 3:4, :] += col_sum(gtwo)
    glow = gtwo.astype(BF)
    gT_s[...] = glow.T

    def gact(chunk):
        r, s = chunk
        return dot_nt(glow, dns[r][s : s + CH, :])

    ga = gact(chunks[0])
    for k, (r, s) in enumerate(chunks):
        nxt = gact(chunks[k + 1]) if k + 1 < len(chunks) else None
        cs = slice(s, s + CH)
        gp = (ga * slope_s[r, :, cs]).astype(BF)
        ddn_s[r, :, cs] += dot(gT_s[...], act_s[r, :, cs])
        dup_s[r, :, cs] += dot(nT_s[...], gp)
        total = col_sum(gp.astype(F32))
        for o in range(0, CH, min(CH, D)):
            w = min(CH, D)
            line, lane = (s + o) // D, (s + o) % D
            small_ref[1 + r, line : line + 1, lane : lane + w] += total[:, o : o + w]
        t = dot_nt(gp, ups[r][:, cs])
        if k == 0:
            acc_s[...] = t
        else:
            acc_s[...] += t
        ga = nxt
    gin = gtwo + acc_s[...]
    small_ref[0, 1:2, :] += col_sum(gin * n1)
    small_ref[0, 2:3, :] += col_sum(gin)
    e = gin * gain1
    gone = inv1 * (e - row_mean(e) - n1 * row_mean(e * n1))
    small_ref[0, 0:1, :] += col_sum(gone)
    gone_ref[...] = gone
    goneT_ref[...] = gone.astype(BF).T

    @pl.when(i == n - 1)
    def _():
        dup_ref[...] = dup_s[...].astype(BF)
        ddn_ref[...] = ddn_s[...].astype(BF)


def ffn(R, CH, lens, h1, og, ups, dns, bias, vecs):
    rows, D = h1.shape
    hid = ups[0].shape[1]
    sds = jax.ShapeDtypeStruct
    row = pl.BlockSpec((R, D), lambda i: (i, 0))
    return pl.pallas_call(
        functools.partial(ffn_kernel, CH), grid=(rows // R,),
        in_specs=[SMEM, row, row, once((D, hid)), once((D, hid)), once((hid, D)), once((hid, D)),
                  once(bias[0].shape), once(bias[1].shape)] + [once((1, D))] * 5,
        out_specs=[row, row, pl.BlockSpec((D, R), lambda i: (0, i)), once((2, D, hid)), once((2, D, hid)), once((3, 8, D))],
        out_shape=[sds((rows, D), BF), sds((rows, D), F32), sds((D, rows), BF), sds((2, D, hid), BF), sds((2, D, hid), BF),
                   sds((3, 8, D), F32)],
        scratch_shapes=[pltpu.VMEM((2, R, hid), BF), pltpu.VMEM((2, R, hid), F32), pltpu.VMEM((D, R), BF),
                        pltpu.VMEM((D, R), BF), pltpu.VMEM((R, D), F32), pltpu.VMEM((2, D, hid), F32),
                        pltpu.VMEM((2, D, hid), F32)],
        compiler_params=pltpu.CompilerParams(vmem_limit_bytes=VMEM_LIMIT), name="feed_forward",
    )(lens, h1, og, *ups, *dns, *bias, *vecs)


def add_low(dst, a, b):
    lead = dst.shape[:-2]
    total = math.prod(lead)

    def one(k, carry):
        idx = []
        for s in reversed(lead):
            idx.append(k % s)
            k = k // s
        idx = tuple(reversed(idx))
        dst[idx] = (a[idx].astype(F32) + b[idx].astype(F32)).astype(BF)
        return carry

    if total == 1:
        idx = (0,) * len(lead)
        dst[idx] = (a[idx].astype(F32) + b[idx].astype(F32)).astype(BF)
    else:
        lax.fori_loop(0, total, one, 0)


class Reduce:
    def __init__(self, src, mine, out, done, order, bufs, sems, base):
        self.mine, self.out, self.done = mine, out, done
        self.z, self.y, self.core, self.x = places()
        z, y, core, x = self.z, self.y, self.core, self.x
        self.src, self.order, self.sems, self.base = src, order, sems, base
        self.rc, self.h, self.r1, self.w, self.r2, self.v, self.rz, self.full = bufs
        self.px, self.py, self.pc = at(z, y, core, 1 - x), at(z, 1 - y, core, x), at(z, y, 1 - core, x)

    def zdev(self, d):
        zt = lax.rem(self.z + d, 4)
        return zt, at(zt, self.y, self.core, self.x)

    def copies(self, stage):
        b, y, core, z = self.base, self.y, self.core, self.z
        if stage == 0:
            return [remote(self.src.at[:, 1 - core], self.rc, self.sems, b, self.pc)]
        if stage == 1:
            if self.order == "xy":
                return [remote(self.h.at[1], self.r1, self.sems, b + 1, self.px)]
            return [remote(self.h.at[:, 1 - y], self.r1, self.sems, b + 1, self.py)]
        if stage == 2:
            if self.order == "xy":
                return [remote(self.w.at[1 - y], self.r2, self.sems, b + 2, self.py)]
            return [remote(self.w.at[1], self.r2, self.sems, b + 2, self.px)]
        if stage == 3:
            out = []
            for d in (1, 2, 3):
                zt, dev = self.zdev(d)
                out.append(remote(self.v.at[zt], self.rz.at[d - 1], self.sems, b + 2 + d, dev))
            return out
        if stage == 4:
            out = []
            for d in (1, 2, 3):
                zt, dev = self.zdev(d)
                part = self.full.at[core, y, z]
                out.append(remote(part, part, self.sems, b + 5 + d, dev))
            return out
        if stage == 5:
            part = self.full.at[core, y]
            return [remote(part, part, self.sems, b + 9, self.py)]
        part = self.full.at[core]
        return [remote(part, part, self.sems, b + 10, self.pc)]

    def start(self, stage):
        for copy in self.copies(stage):
            copy.start()

    def combine(self, stage):
        y, core, z = self.y, self.core, self.z
        if stage == 0:
            add_low(self.h, self.mine, self.rc)
        elif stage == 1:
            add_low(self.w, self.h.at[0] if self.order == "xy" else self.h.at[:, y], self.r1)
        elif stage == 2:
            mine = self.w.at[y] if self.order == "xy" else self.w.at[0]
            self.v[...] = (mine[...].astype(F32) + self.r2[...].astype(F32)).astype(BF).reshape(self.v.shape)
        elif stage == 3:
            s = self.v[z].astype(F32)
            for d in range(3):
                s = s + self.rz[d].astype(F32)
            self.full[core, y, z] = s.astype(BF)

    def take(self, stage):
        for copy in self.copies(stage):
            copy.wait()
        self.combine(stage)

    def step(self, stage):
        self.take(stage)
        if stage < 6:
            self.start(stage + 1)
        else:
            self.leave().start()

    def leave(self):
        return pltpu.make_async_copy(self.full, self.out, self.done)


def reduce_bufs(width, order, rows=128):
    first = (2, rows, width)
    return [pltpu.VMEM(s, BF) for s in (
        (2, 2, rows, width), (2, 2, rows, width), first, first, (rows, width), (4, rows // 4, width),
        (3, rows // 4, width), (2, 2, 4, rows // 4, width))]


class ReduceOwn(Reduce):
    def __init__(self, src_other, src_own, out, done, bufs, sems, base):
        Reduce.__init__(self, None, None, out, done, "xy", (None, None) + tuple(bufs[4:]), sems, base)
        self.srcs = (src_own, src_other)
        self.rcs, self.hs = bufs[0:2], bufs[2:4]

    def copies(self, stage):
        b = self.base
        if stage == "other":
            return [remote(self.srcs[1].at[1 - self.core], self.rcs[1], self.sems, b + 11, self.pc)]
        if stage == "own":
            return [remote(self.srcs[0].at[1 - self.core], self.rcs[0], self.sems, b, self.pc)]
        if stage == 1:
            return [remote(self.hs[1], self.r1, self.sems, b + 1, self.px)]
        return Reduce.copies(self, stage)

    def combine(self, stage):
        if stage == "other":
            add_low(self.hs[1], self.srcs[1].at[self.core], self.rcs[1])
        elif stage == "own":
            add_low(self.hs[0], self.srcs[0].at[self.core], self.rcs[0])
        elif stage == 1:
            add_low(self.w, self.hs[0], self.r1)
        else:
            Reduce.combine(self, stage)

    def step(self, stage):
        if stage == "other":
            self.take(stage)
            self.start(1)
        elif stage == "own":
            self.take(stage)
            self.take(1)
            self.start(2)
        else:
            Reduce.step(self, stage)


def reduce_own_bufs(width, rows):
    pair = (2, rows, width)
    return [pltpu.VMEM(s, BF) for s in (
        pair, pair, pair, pair, pair, pair, (rows, width), (4, rows // 4, width), (3, rows // 4, width),
        (2, 2, 4, rows // 4, width))]


class Butterfly:
    def __init__(self, acc, recv, sems, base):
        z, y, core, x = places()
        self.acc, self.recv, self.sems, self.base = acc, recv, sems, base
        self.devices = (at(z, y, 1 - core, x), at(z, y, core, 1 - x), at(z, 1 - y, core, x),
                        at(z + 1 - 2 * (z % 2), y, core, x), at((z + 2) % 4, y, core, x))

    def copy(self, k):
        return remote(self.acc.at[k], self.recv.at[k], self.sems, self.base + k, self.devices[k])

    def start(self, k):
        self.copy(k).start()

    def take(self, k):
        self.copy(k).wait()
        if k == 1:
            self.acc[k + 1, 0] = self.acc[k, 0] + self.recv[k, 0]
            self.acc[k + 1, 1] = self.acc[k, 1] + self.recv[k, 2]
            self.acc[k + 1, 2] = self.acc[k, 2] + self.recv[k, 1]
        else:
            self.acc[k + 1] = self.acc[k] + self.recv[k]

    def step(self, k):
        self.take(k)
        if k < 4:
            self.start(k + 1)


PLAN = {
    2: ("D0 0",),
    3: ("U1 0", "D1 0",),
    6: ("D0 1", "U0 0",),
    7: ("U1 1",),
    8: ("D0 2",),
    9: ("D1 1", "U1 2", "O 0",),
    10: ("U0 1", "Qk other",),
    11: ("Qq other", "Qv other", "D0 3",),
    12: ("D1 2",),
    13: ("O 1", "U0 2", "U1 3",),
    15: ("D0 4", "O 2",),
}
TAIL_PLAN = {
    0: ("D1 3", "Qq own", "U0 3", "Qk own",),
    1: ("Qv own", "F 0",),
    2: ("U1 4", "Qq 2", "Qk 2", "Qv 2", "D1 4", "O 3",),
    3: ("D0 5", "Qq 3", "F 1", "D0 6", "U0 4", "Qk 3", "Qv 3", "F 2", "U1 5", "D1 5", "O 4", "Qq 4", "U1 6",),
    4: ("U0 5", "Qk 4", "O 5", "D1 6", "Qv 4", "F 3", "F 4", "Qk 5", "Qq 5", "Qv 5", "Qk 6", "U0 6", "O 6", "Qq 6", "Qv 6",),
}


def attn_bwd_kernel(comm, n, m, *refs):
    (gone_ref, grow_ref, qkv_ref, p_ref, wqa_ref, wqb_ref, woa_ref, wob_ref, xT_any, gT_any, att_any) = refs[:11]
    refs = refs[11:]
    if comm:
        up_any, dn_any, small_ref = refs[:3]
        gx_ref, up_out, dn_out, wo_out, wq_out, small_out = refs[3:9]
        dq_s, xT_s, gT_s, att_s, local, wo_src, q_oth, q_own, acc, recv, sems, up_s, dn_s, done = refs[9:23]
        bufs = refs[23:]
    else:
        gx_ref, wo_out, wq_out, bias_out = refs[:4]
        dq_s, xT_s, gT_s, att_s, local = refs[4:]
    s = pl.program_id(0)
    r, d = gone_ref.shape
    block = r // LMAX
    half = d // 2
    loads = [pltpu.make_async_copy(a, b, local.at[k]) for k, (a, b) in enumerate(
        ((xT_any, xT_s), (gT_any, gT_s), (att_any, att_s)))]

    if comm:
        w = up_any.shape[-1] // 2
        z, y, core, x = places()
        pieces = {}
        for k in range(2):
            cols = pl.ds(k * w, w)
            pieces["U%d" % k] = Reduce(
                up_any.at[..., cols], up_s.at[..., cols], up_out.at[..., cols], done.at[k], "xy",
                bufs[8 * k : 8 * k + 8], sems, 11 * k)
            pieces["D%d" % k] = Reduce(
                dn_any.at[..., cols], dn_s.at[..., cols], dn_out.at[..., cols], done.at[2 + k], "yx",
                bufs[16 + 8 * k : 24 + 8 * k], sems, 22 + 11 * k)
        pieces["O"] = Reduce(wo_src, wo_src.at[:, core], wo_out, done.at[4], "xy", bufs[32:40], sems, 44)
        for k, name in enumerate("qkv"):
            pieces["Q" + name] = ReduceOwn(
                q_oth.at[k], q_own.at[k], wq_out.at[k], done.at[5 + k], bufs[40 + 10 * k : 50 + 10 * k], sems,
                55 + 12 * k)
        loads += [pltpu.make_async_copy(a.at[:, core], b, local.at[3 + k]) for k, (a, b) in enumerate(
            ((up_any, up_s), (dn_any, dn_s)))]
        pieces["F"] = fly = Butterfly(acc, recv, sems, 91)
        first = pieces["U0"]

        def follow(plan):
            for entry in plan:
                name, stage = entry.split()
                pieces[name].step(int(stage) if stage.isdigit() else stage)

        @pl.when(s == 0)
        def _():
            enter(fly.devices[:3] + tuple(first.zdev(k)[1] for k in (1, 2, 3)))
            for name in ("U0", "D0", "U1", "D1"):
                pieces[name].start(0)
            acc[0] = small_ref[...]

        @pl.when(s == 1)
        def _():
            loads[3].wait()
            loads[4].wait()

        for at_step, plan in PLAN.items():
            pl.when(s == at_step)(functools.partial(follow, plan))
        for at_step, plan in TAIL_PLAN.items():
            if at_step < m:
                pl.when(s == 2 * n + at_step)(functools.partial(follow, plan))

    @pl.when(s == 0)
    def _():
        for copy in loads[3:] + loads[:3]:
            copy.start()
        if not comm:
            bias_out[...] = jnp.zeros_like(bias_out)

    def quarters(dst, value):
        for core in range(2):
            for y in range(2):
                first_row = (core * 2 + y) * (d // 4)
                dst[core, y] = value[first_row : first_row + d // 4]

    @pl.when(s == min(2, n - 1))
    def _():
        loads[1].wait()
        loads[2].wait()
        for rel in range(2):
            total = dot(gT_s[...], att_s[rel]).astype(BF)
            if comm:
                quarters(wo_src.at[rel], total)
            else:
                wo_out[rel] = total
        if comm:
            pieces["O"].start(0)

    def heads(wo, which, blk):
        ga = dot_nt(gone_ref[...].astype(BF), wo).astype(BF)
        for c in range(block):
            rs = slice(c * LMAX, (c + 1) * LMAX)
            probs = p_ref[c, 0]
            k, v = qkv_ref[1, 0, rs, :], qkv_ref[2, 0, rs, :]
            gs = stack_heads(ga[rs])
            dp = dot_nt(v, gs)
            pf = probs.astype(F32)
            ds = (pf * (dp - jnp.sum(pf * dp, axis=0, keepdims=True))).astype(BF)
            dv = dot(probs, gs)
            dk = dot(ds, stack_heads(qkv_ref[0, 0, rs, :]))
            dq = pick_heads(dot(ds.T, k)) * (1.0 / math.sqrt(HDIM))
            out = pl.ds(blk * r + c * LMAX, LMAX)
            dq_s[which, 0, out, :] = dq.astype(BF)
            dq_s[which, 1, out, :] = dk.astype(BF)
            dq_s[which, 2, out, :] = dv.astype(BF)

    def weights(which):
        for j in range(3):
            total = dot(xT_s[...], dq_s[which, j]).astype(BF)
            if comm:
                quarters((q_own, q_oth)[which].at[j], total)
                if which == 1:
                    pieces["Q" + "qkv"[j]].start("other")
                else:
                    pieces["Q" + "qkv"[j]].start("own")
            else:
                wq_out[which, j] = total
        ref, base = (acc.at[0], 1) if comm else (bias_out, 0)
        ref[base + which, 2:3, 0:half] = col_sum(dq_s[which, 0].astype(F32))
        ref[base + which, 2:3, half:d] = col_sum(dq_s[which, 2].astype(F32))

    @pl.when(s < n)
    def _():
        heads(wob_ref[...].reshape(half, d), 1, s)

        @pl.when(s == n - 1)
        def _():
            loads[0].wait()
            weights(1)

    @pl.when((s >= n) & (s < 2 * n))
    def _():
        heads(woa_ref[...], 0, s - n)

        @pl.when(s == 2 * n - 1)
        def _():
            weights(0)
            if comm:
                fly.start(0)

    @pl.when(s >= 2 * n)
    def _():
        rg = gx_ref.shape[0]
        rs = pl.ds((s - 2 * n) * rg, rg)
        total = grow_ref[...]
        for which, wq in ((1, wqb_ref), (0, wqa_ref)):
            for j in range(3):
                total += dot_nt(dq_s[which, j, rs, :], wq[j].reshape(d, half))
        gx_ref[...] = total.astype(BF)

    if comm:

        @pl.when(s == 2 * n + m - 1)
        def _():
            for at_step, plan in TAIL_PLAN.items():
                if at_step >= m:
                    follow(plan)
            for name, piece in pieces.items():
                if name != "F":
                    piece.leave().wait()
            small_out[...] = acc[5]


def attn_bwd(comm, block, gone, goneT, xT, qkv, probs, att, wq, wo, sums):
    rows, d = gone.shape
    half, r = d // 2, block * LMAX
    n = rows // r
    rg = min(rows, 4 * LMAX)
    m = rows // rg
    sds = jax.ShapeDtypeStruct

    def blk(s):
        return jnp.where(s < 2 * n, lax.rem(s, n), n - 1)

    def rel(s):
        return jnp.where(s < n, 1, 0)

    def tail(s):
        return jnp.maximum(s - 2 * n, 0)

    in_specs = [
        pl.BlockSpec((r, d), lambda s: (blk(s), 0)),
        pl.BlockSpec((rg, d), lambda s: (tail(s), 0)),
        pl.BlockSpec((3, 1, r, half), lambda s: (0, rel(s), blk(s), 0)),
        pl.BlockSpec((block, 1, LMAX, half // HDIM * LMAX), lambda s: (blk(s), rel(s), 0, 0)),
        once(wq[0].shape), once(wq[1].shape), once(wo[0].shape), once(wo[1].shape), ANY, ANY, ANY,
    ]
    gx_spec, gx_shape = pl.BlockSpec((rg, d), lambda s: (tail(s), 0)), sds((rows, d), BF)
    scratch = [pltpu.VMEM((2, 3, rows, half), BF), pltpu.VMEM(xT.shape, BF), pltpu.VMEM(goneT.shape, BF),
               pltpu.VMEM(att.shape, BF), pltpu.SemaphoreType.DMA((5,))]
    params = dict(vmem_limit_bytes=VMEM_LIMIT)
    if comm:
        up, dn, small = sums
        hid = up.shape[-1]
        split = lambda w: (2, 2, 4, d // 16, w)
        in_specs += [ANY, ANY, once(small.shape)]
        out_specs = [gx_spec, ANY, ANY, ANY, ANY, once(small.shape)]
        out_shape = [gx_shape, sds(split(hid), BF), sds(split(hid), BF), sds(split(half), BF),
                     sds((3,) + split(half), BF), sds(small.shape, F32)]
        rows4 = d // 4
        scratch += [pltpu.VMEM((2, 2, 2, rows4, half), BF), pltpu.VMEM((3, 2, 2, rows4, half), BF),
                    pltpu.VMEM((3, 2, 2, rows4, half), BF), pltpu.VMEM((6,) + small.shape, F32),
                    pltpu.VMEM((5,) + small.shape, F32), pltpu.SemaphoreType.DMA((2, 96)),
                    pltpu.VMEM((2, 2, rows4, hid), BF), pltpu.VMEM((2, 2, rows4, hid), BF),
                    pltpu.SemaphoreType.DMA((8,))]
        for _ in range(4):
            scratch += reduce_bufs(hid // 2, "xy", rows4)
        scratch += reduce_bufs(half, "xy", rows4)
        for _ in range(3):
            scratch += reduce_own_bufs(half, rows4)
        params.update(collective_id=1, has_side_effects=True)
    else:
        out_specs = [gx_spec, once((2, d, half)), once((2, 3, d, half)), once((2, 8, d))]
        out_shape = [gx_shape, sds((2, d, half), BF), sds((2, 3, d, half), BF), sds((2, 8, d), F32)]
    return pl.pallas_call(
        functools.partial(attn_bwd_kernel, comm, n, m), grid=(2 * n + m,), in_specs=in_specs, out_specs=out_specs,
        out_shape=out_shape, scratch_shapes=scratch, compiler_params=pltpu.CompilerParams(**params),
        name="attention_backward",
    )(gone, gone, qkv, probs, *wq, *wo, xT, goneT, att, *sums)


def finish_kernel(gx_ref, up_ref, dn_ref, wo_ref, wq_ref, small_ref, gx_out, up_out, dn_out, wo_out, wq_out,
                  upb_out, qvb_out, *vec_outs):
    gx_out[...] = gx_ref[...]
    up_out[...] = up_ref[...].astype(F32)
    dn_out[...] = dn_ref[...].astype(F32).T
    wq_out[...] = wq_ref[...].astype(F32)

    @pl.when(pl.program_id(0) == 0)
    def _():
        d = small_ref.shape[2]
        half = d // 2
        wo_out[...] = wo_ref[...].astype(F32).T
        for k, out in enumerate(vec_outs):
            out[...] = small_ref[0, k]
        for k in range(upb_out.shape[0] // d):
            upb_out[k * d : (k + 1) * d] = small_ref[1, k]
        qvb_out[0:1, :] = small_ref[1, 2:3, 0:half]
        qvb_out[1:2, :] = small_ref[1, 2:3, half:d]


def finish(gx, up, dn, wo, wq, small):
    rows, d = gx.shape
    hid, half = up.shape[1], wo.shape[1]
    n = 2
    sds = jax.ShapeDtypeStruct
    gx_spec = pl.BlockSpec((rows // n, d), lambda i: (i, 0))
    up_spec = pl.BlockSpec((d // n, hid), lambda i: (i, 0))
    wq_spec = pl.BlockSpec((3, d // n, half), lambda i: (0, i, 0))
    return pl.pallas_call(
        finish_kernel, grid=(n,),
        in_specs=[gx_spec, up_spec, pl.BlockSpec((d, hid // n), lambda i: (0, i)), once(wo.shape), wq_spec,
                  once(small.shape)],
        out_specs=[gx_spec, up_spec, pl.BlockSpec((hid // n, d), lambda i: (i, 0)), once((half, d)), wq_spec,
                   once((hid,)), once((2, half))] + [once((d,))] * 6,
        out_shape=[sds(gx.shape, BF), sds(up.shape, F32), sds((hid, d), F32), sds((half, d), F32), sds(wq.shape, F32),
                   sds((hid,), F32), sds((2, half), F32)] + [sds((d,), F32)] * 6,
        compiler_params=pltpu.CompilerParams(vmem_limit_bytes=VMEM_LIMIT), name="finish",
    )(gx, up, dn, wo, wq, small)


def tile_rows(rows):
    for r in (512, 640, 320):
        if rows % r == 0:
            return r
    return LMAX


def chain_block(chains):
    for c in (4, 2):
        if chains % c == 0:
            return c
    return 1


def on_device(comm, tokens, qkv_weight, qv_bias, out_weight, out_bias, gain_one, shift_one, up_weight, up_bias,
              down_weight, down_bias, gain_two, shift_two, out_grad, lengths):
    rows, d = tokens.shape
    chains = rows // LMAX
    half = d // 2
    vecs = [a[None] for a in (gain_one, shift_one, down_bias, gain_two, shift_two)]
    block = chain_block(chains)
    comm = comm and chains == 16

    def gather(a, dim):
        return lax.all_gather(a, "tensor", axis=dim, tiled=True)

    def table(qv, up):
        flat = jnp.concatenate([qv[0], qv[1], up]).astype(F32)
        return jnp.pad(flat, (0, 4096 - flat.shape[0])).reshape(2, 2, 8, 128)

    if comm:
        hid = up_weight.shape[1]
        quarters = (
            qkv_weight.reshape(3, 2, 2, 2, d // 8, half), out_weight.reshape(2, half // 2, d),
            up_weight.reshape(2, 2, 2, d // 8, hid), down_weight.reshape(2, 2, 2, hid // 8, d), up_bias,
        )
        h1, qkv, att, probs, xT, wqb, wob, wupb, wdnb, bias_b, bias = attn_fwd(
            True, 2, lengths, tokens, qkv_weight, out_weight, qv_bias, out_bias[None], quarters)
        wqs, wos, bias = (qkv_weight, wqb), (out_weight, wob), (bias, bias_b)
        ups, dns = (up_weight, wupb.reshape(d, hid)), (down_weight, wdnb.reshape(hid, d))
    else:
        wq, wo = gather(qkv_weight, 2), gather(out_weight, 0)
        wup, wdn = gather(up_weight, 1), gather(down_weight, 0)
        hid = wup.shape[1] // 2
        qvb, upb = gather(qv_bias, 1), gather(up_bias, 0)
        bias = (table(qvb[:, :half], upb[:hid]), table(qvb[:, half:], upb[hid:]))
        wqs, wos = (wq[:, :, :half], wq[:, :, half:]), (wo[:half], wo[half:])
        ups, dns = (wup[:, :hid], wup[:, hid:]), (wdn[:hid], wdn[hid:])
        h1, qkv, att, probs, xT = attn_fwd(
            False, block, lengths, tokens, wqs[0], wos[0], bias[0], out_bias[None], (wqs[1], wos[1], bias[1]))
    out, gone, goneT, dup, ddn, small = ffn(tile_rows(rows), 256, lengths, h1, out_grad, ups, dns, bias, vecs)
    small_block = 2 if chains % 2 == 0 else 1
    if comm:
        split = (2, 2, 2, d // 4, hid)
        gx, dup, ddn, dwo, dwq, small = attn_bwd(
            True, small_block, gone, goneT, xT, qkv, probs, att, wqs, wos, (dup.reshape(split), ddn.reshape(split), small))
        gx, dup, ddn, dwo, dwq, dupb, dqvb, *vecs = finish(
            gx, dup.reshape(d, hid), ddn.reshape(d, hid), dwo.reshape(d, half), dwq.reshape(3, d, half), small)
    else:
        gx, dwo, dwq, dbias = attn_bwd(False, small_block, gone, goneT, xT, qkv, probs, att, wqs, wos, ())

        def total(a, dim):
            a = lax.psum_scatter(a.astype(BF), "tensor", scatter_dimension=dim, tiled=True)
            return lax.psum(a, "dp").astype(F32)

        dwq = total(dwq.transpose(1, 2, 0, 3).reshape(3, d, d), 2)
        dwo = total(jnp.concatenate([dwo[0], dwo[1]], axis=1), 1).T
        dup = total(jnp.concatenate([dup[0], dup[1]], axis=1), 1)
        ddn = total(jnp.concatenate([ddn[0], ddn[1]], axis=1), 1).T
        dupb = total(small[1:, : hid // d].reshape(2 * hid), 0)
        dqvb = total(dbias[:, 2].reshape(2, 2, half).transpose(1, 0, 2).reshape(2, d), 1)
        vecs = lax.psum(small[0], ("dp", "tensor"))
    return (out, gx, dwq, dqvb, dwo, vecs[0], vecs[1], vecs[2], dup, dupb, ddn, vecs[3], vecs[4], vecs[5])


def solution(mesh):
    comm = mesh.shape["dp"] == 16 and mesh.shape["tensor"] == 2
    rows = P(("dp", "tensor"), None)
    in_specs = (rows, P(None, None, "tensor"), P(None, "tensor"), P("tensor", None), P(), P(), P(), P(None, "tensor"),
                P("tensor"), P("tensor", None), P(), P(), P(), rows, P("dp"))
    out_specs = (rows, rows, P(None, None, "tensor"), P(None, "tensor"), P("tensor", None), P(), P(), P(),
                 P(None, "tensor"), P("tensor"), P("tensor", None), P(), P(), P())
    return jax.shard_map(functools.partial(on_device, comm), mesh=mesh, in_specs=in_specs, out_specs=out_specs,
                         check_vma=False)
```

```python
import functools
import math

import jax
import jax.numpy as jnp
from jax import lax
from jax.experimental import pallas as pl
from jax.experimental.pallas import tpu as pltpu
from jax.sharding import PartitionSpec as P

F32 = jnp.float32
BF = jnp.bfloat16
LMAX = 160
HDIM = 64
EPS = 1e-12
NEG = -1e30
MESH = pl.DeviceIdType.MESH
VMEM_LIMIT = 60 << 20

ERF_P = 0.3275911 * math.sqrt(0.5)
ERF_A = (0.254829592, -0.284496736, 1.421413741, -1.453152027, 1.061405429)


def dot(a, b):
    return lax.dot_general(a, b, (((1,), (0,)), ((), ())), preferred_element_type=F32)


def dot_nt(a, b):
    return lax.dot_general(a, b, (((1,), (1,)), ((), ())), preferred_element_type=F32)


def gelu_parts(v):
    bell = jnp.exp(v * v * -0.5)
    t = 1.0 / (1.0 + ERF_P * jnp.abs(v))
    tail = 0.5 * ERF_A[4]
    for a in ERF_A[3::-1]:
        tail = tail * t + 0.5 * a
    tail = tail * t * bell
    phi = jnp.where(v >= 0, 1.0 - tail, tail)
    return v * phi, phi + v * (bell * (1.0 / math.sqrt(2.0 * math.pi)))


def row_mean(x):
    return jnp.sum(x, axis=1, keepdims=True) * (1.0 / x.shape[1])


def col_sum(x):
    return jnp.sum(x, axis=0, keepdims=True)


def lane_head(width):
    return lax.broadcasted_iota(jnp.int32, (1, width), 1) // HDIM


def stack_heads(x):
    head = lane_head(x.shape[1])
    return jnp.concatenate(
        [jnp.where(head == h, x, jnp.zeros_like(x)) for h in range(x.shape[1] // HDIM)], axis=0
    )


def pick_heads(x):
    heads = x.shape[1] // HDIM
    r = x.shape[0] // heads
    head = lane_head(x.shape[1])
    out = x[:r]
    for h in range(1, heads):
        out = jnp.where(head == h, x[h * r : (h + 1) * r], out)
    return out


def places():
    dp = lax.axis_index("dp")
    return dp // 4, (dp // 2) % 2, dp % 2, lax.axis_index("tensor")


def at(z, y, core, x):
    return (z * 4 + y * 2 + core, x)


def greet(neighbours):
    barrier = pltpu.get_barrier_semaphore()
    for device in neighbours:
        pl.semaphore_signal(barrier, inc=1, device_id=device, device_id_type=MESH)


def greeted(count):
    pl.semaphore_wait(pltpu.get_barrier_semaphore(), count)


def enter(neighbours):
    greet(neighbours)
    greeted(len(neighbours))


def remote(src, dst, sems, slot, device):
    return pltpu.make_async_remote_copy(
        src_ref=src, dst_ref=dst, send_sem=sems.at[0, slot], recv_sem=sems.at[1, slot],
        device_id=device, device_id_type=MESH,
    )


class Gather:
    PARTS = {
        "qa": (0, (slice(None),), (0,), True), "qb": (0, (slice(None),), (1,), True), "bias": (4, (), (), False),
        "wo": (1, (), (), False), "ua": (2, (), (0,), True), "ub": (2, (), (1,), True), "da": (3, (), (0,), True),
        "db": (3, (), (1,), True),
    }

    def __init__(self, own, other, sems):
        z, y, core, x = places()
        self.px, self.py, self.pc = at(z, y, core, 1 - x), at(z, 1 - y, core, x), at(z, y, 1 - core, x)
        self.own, self.other, self.sems = own, other, sems
        self.y, self.core = y, core

    def copy(self, name, stage):
        array, before, after, split = self.PARTS[name]
        own, other = self.own[array], self.other[array]
        lines = (self.y, 1 - self.y) if split else (None, None)
        here, there = (before + ((y,) if split else ()) + (self.core,) + after for y in lines)
        src, part, device = (
            (own, here, self.px), (other, here, self.py), (other, here, self.pc), (other, there, self.pc)
        )[stage]
        slot = 4 * list(self.PARTS).index(name) + stage
        return remote(src.at[part], other.at[part], self.sems, slot, device)

    def stages(self, name):
        return (0, 1, 2, 3) if self.PARTS[name][3] else (0, 2)

    def fetch(self, name):
        self.copy(name, 0).start()

    def spread(self, name):
        self.copy(name, 0).wait_recv()
        for stage in self.stages(name)[1:-1] if self.PARTS[name][3] else (2,):
            self.copy(name, stage).start()

    def finish(self, name):
        self.copy(name, 1).wait_recv()
        self.copy(name, 3).start()

    def arrived(self, name):
        for stage in self.stages(name)[2:] if self.PARTS[name][3] else (2,):
            self.copy(name, stage).wait_recv()

    def sent(self, name):
        for stage in self.stages(name):
            self.copy(name, stage).wait_send()


GATHER_PLAN = {
    0: ("fetch qa", "fetch qb", "fetch bias", "fetch wo", "fetch ua", "fetch ub", "fetch da", "fetch db",),
    4: ("spread qa",),
    5: ("spread qb",),
    6: ("spread bias",),
    7: ("finish qa", "spread wo",),
    8: ("finish qb", "spread ua", "arrived qa", "arrived qb", "arrived bias", "arrived wo",),
    9: ("spread ub",),
    11: ("finish ua", "spread da",),
    12: ("spread db",),
    13: ("finish ub",),
    14: ("finish da",),
}
GATHER_END = ("arrived ua", "arrived ub", "finish db", "arrived da", "arrived db",)


def attn_fwd_kernel(comm, *refs):
    if comm:
        (lens_ref, x_ref, wq_ref, wo_ref, qv_ref, ob_ref, wq_any, wo_any, up_any, dn_any, upb_ref,
         h1_ref, qkv_ref, att_ref, p_ref, xT_ref, wq_out, wo_out, up_out, dn_out, bias_out,
         own_out, att_s, wq_s, wo_s, bias_s, bias_ref, sems, local) = refs
    else:
        (lens_ref, x_ref, wq_ref, wo_ref, bias_ref, ob_ref, wq_s, wo_s, bias_s,
         h1_ref, qkv_ref, att_ref, p_ref, xT_ref, att_s) = refs
    p, i = pl.program_id(0), pl.program_id(1)
    rows, d = h1_ref.shape
    block = rows // LMAX
    half = d // 2
    sub = x_ref.shape[0] // rows
    if comm:
        gather = Gather((wq_any, wo_any, up_any, dn_any, bias_ref), (wq_s, wo_s, up_out, dn_out, bias_s), sems)
        step = p * pl.num_programs(1) + i
        keep = [pltpu.make_async_copy(a, b, local.at[k]) for k, (a, b) in enumerate(
            ((wq_s, wq_out), (wo_s, wo_out), (bias_s, bias_out)))]

        def follow(plan):
            for entry in plan:
                action, name = entry.split()
                getattr(gather, action)(name)

        @pl.when(step == 0)
        def _():
            bias_ref[...] = jnp.zeros_like(bias_ref)
            qv, up = qv_ref[...].astype(F32), upb_ref[...].astype(F32).reshape(-1, 128)
            lines = [qv[k : k + 1, o : o + 128] for k in range(2) for o in range(0, half, 128)]
            lines += [up[k : k + 1] for k in range(up.shape[0])]
            for k, line in enumerate(lines):
                bias_ref[k // 16, k // 8 % 2, k % 8 : k % 8 + 1, :] = line
            own_out[...] = bias_ref[...]
            enter((gather.px, gather.py, gather.pc))

        for at_step, plan in GATHER_PLAN.items():
            pl.when(step == at_step)(functools.partial(follow, plan))

        @pl.when(step == 8)
        def _():
            for copy in keep:
                copy.start()

    x = x_ref[pl.ds(lax.rem(i, sub) * rows, rows), :] if sub > 1 else x_ref[...]
    first = lax.axis_index("tensor") * (pl.num_programs(1) * block)
    kpos = lax.broadcasted_iota(jnp.int32, (LMAX, 1), 0)

    def heads(wq, bias_of):
        for j in range(3):
            t = dot(x, wq[j].reshape(d, half))
            if j != 1:
                t += lanes(bias_of, j * half // 256, half)
            t = t.astype(BF)
            if j == 0:
                t = t * jnp.asarray(1.0 / math.sqrt(HDIM), BF)
            qkv_ref[j, 0] = t
        for c in range(block):
            rs = slice(c * LMAX, (c + 1) * LMAX)
            bias = jnp.where(kpos < lens_ref[first + i * block + c], 0.0, NEG).astype(F32)
            st = dot_nt(qkv_ref[1, 0, rs, :], stack_heads(qkv_ref[0, 0, rs, :])) + bias
            e = jnp.exp(st - jnp.max(st, axis=0, keepdims=True))
            probs = (e * (1.0 / jnp.sum(e, axis=0, keepdims=True))).astype(BF)
            p_ref[c, 0] = probs
            o = pick_heads(dot(probs.T, qkv_ref[2, 0, rs, :])).astype(BF)
            att_ref[0, rs, :] = o

    @pl.when(p == 0)
    def _():
        heads(wq_ref, bias_ref)
        att_s[i] = att_ref[0]

        @pl.when(lax.rem(i, sub) == 0)
        def _():
            xT_ref[...] = x_ref[...].T

    @pl.when(p == 1)
    def _():
        heads(wq_s, bias_s)
        wo = wo_s[...].reshape(half, d)
        h1_ref[...] = x.astype(F32) + dot(att_s[i], wo_ref[...]) + dot(att_ref[0], wo) + ob_ref[...]

    if comm:

        @pl.when(step == 2 * pl.num_programs(1) - 1)
        def _():
            follow(GATHER_END)
            for copy in keep:
                copy.wait()
            for name in gather.PARTS:
                gather.sent(name)


def lanes(ref, line, width):
    parts = [ref[k // 16, k // 8 % 2, k % 8 : k % 8 + 1, :] for k in range(line, line + width // 128)]
    return parts[0] if len(parts) == 1 else jnp.concatenate(parts, axis=1)


def once(shape):
    return pl.BlockSpec(shape, lambda *_: (0,) * len(shape), pipeline_mode=pl.Buffered(1))


ANY = pl.BlockSpec(memory_space=pl.ANY)
SMEM = pl.BlockSpec(memory_space=pltpu.SMEM)


def attn_fwd(comm, block, lens, x, wq, wo, bias, ob, others):
    rows, d = x.shape
    half, r = d // 2, block * LMAX
    n = rows // r
    sds = jax.ShapeDtypeStruct
    sub = 2 if n % 2 == 0 else 1
    in_specs = [SMEM, pl.BlockSpec((sub * r, d), lambda p, i: (i // sub, 0)), once((3, d, half)), once((half, d)), once(bias.shape), once((1, d))]
    out_specs = [
        pl.BlockSpec((r, d), lambda p, i: (i * p, 0)),
        pl.BlockSpec((3, 1, r, half), lambda p, i: (0, p, i, 0)),
        pl.BlockSpec((1, r, half), lambda p, i: (p, i, 0)),
        pl.BlockSpec((block, 1, LMAX, half // HDIM * LMAX), lambda p, i: (i, p, 0, 0)),
        pl.BlockSpec((d, sub * r), lambda p, i: (0, (i * (1 - p) + (n - 1) * p) // sub)),
    ]
    out_shape = [
        sds((rows, d), F32),
        sds((3, 2, rows, half), BF),
        sds((2, rows, half), BF),
        sds((rows // LMAX, 2, LMAX, half // HDIM * LMAX), BF),
        sds((d, rows), BF),
    ]
    scratch = [pltpu.VMEM((n, r, half), BF)]
    args = [lens, x, wq, wo, bias, ob]
    if comm:
        table = sds((2, 2, 8, 128), F32)
        in_specs += [ANY] * 4 + [once(others[4].shape)]
        out_specs += [ANY] * 5 + [once(table.shape)]
        out_shape += [sds(a.shape, a.dtype) for a in others[:4]] + [table, table]
        scratch += [pltpu.VMEM(a.shape, a.dtype) for a in others[:2] + (table, table)]
        scratch += [pltpu.SemaphoreType.DMA((2, 32)), pltpu.SemaphoreType.DMA((3,))]
    else:
        in_specs += [once((3, d, half)), once((half, d)), once(bias.shape)]
    params = dict(vmem_limit_bytes=VMEM_LIMIT)
    if comm:
        params.update(collective_id=0, has_side_effects=True)
    return pl.pallas_call(
        functools.partial(attn_fwd_kernel, comm), grid=(2, n), in_specs=in_specs, out_specs=out_specs,
        out_shape=out_shape, scratch_shapes=scratch, compiler_params=pltpu.CompilerParams(**params),
        name="attention_forward",
    )(*args, *others)


def ffn_kernel(CH, lens_ref, h1_ref, og_ref, upa_ref, upb_ref, dna_ref, dnb_ref, ba_ref, bb_ref,
               gain1_ref, shift1_ref, bias_dn_ref, gain2_ref, shift2_ref,
               out_ref, gone_ref, goneT_ref, dup_ref, ddn_ref, small_ref,
               act_s, slope_s, nT_s, gT_s, acc_s, dup_s, ddn_s):
    i, n = pl.program_id(0), pl.num_programs(0)
    R, D = h1_ref.shape
    hid = upa_ref.shape[1]
    chunks = [(r, k * CH) for r in range(2) for k in range(hid // CH)]
    ups, dns, biases = (upa_ref, upb_ref), (dna_ref, dnb_ref), (ba_ref, bb_ref)

    @pl.when(i == 0)
    def _():
        dup_s[...] = jnp.zeros_like(dup_s)
        ddn_s[...] = jnp.zeros_like(ddn_s)
        small_ref[...] = jnp.zeros_like(small_ref)

    gain1, shift1, bias_dn, gain2, shift2 = (
        ref[...] for ref in (gain1_ref, shift1_ref, bias_dn_ref, gain2_ref, shift2_ref))
    h = h1_ref[...]
    c = h - row_mean(h)
    inv1 = lax.rsqrt(row_mean(c * c) + EPS)
    n1 = c * inv1
    normed = n1 * gain1 + shift1
    nlow = normed.astype(BF)
    nT_s[...] = nlow.T

    def up(chunk):
        r, s = chunk
        return dot(nlow, ups[r][:, s : s + CH]) + lanes(biases[r], (D + s) // 128, CH)

    pre = up(chunks[0])
    for k, (r, s) in enumerate(chunks):
        nxt = up(chunks[k + 1]) if k + 1 < len(chunks) else None
        a, sl = gelu_parts(pre)
        a = a.astype(BF)
        act_s[r, :, s : s + CH] = a
        slope_s[r, :, s : s + CH] = sl
        t = dot(a, dns[r][s : s + CH, :])
        if k == 0:
            acc_s[...] = t
        else:
            acc_s[...] += t
        pre = nxt
    h2 = normed + acc_s[...] + bias_dn
    c2 = h2 - row_mean(h2)
    inv2 = lax.rsqrt(row_mean(c2 * c2) + EPS)
    n2 = c2 * inv2
    out_ref[...] = (n2 * gain2 + shift2).astype(BF)

    row = i * R + lax.broadcasted_iota(jnp.int32, (R, 1), 0)
    live = jnp.zeros((R, 1), F32)
    first = (i * R) // LMAX
    for j in range((R - 2) // LMAX + 2):
        ch = jnp.minimum(first + j, n * R // LMAX - 1)
        length = lens_ref[lax.axis_index("tensor") * (n * R // LMAX) + ch]
        live = jnp.where((row >= ch * LMAX) & (row < ch * LMAX + length), 1.0, live)
    go = og_ref[...].astype(F32) * live
    small_ref[0, 4:5, :] += col_sum(go * n2)
    small_ref[0, 5:6, :] += col_sum(go)
    e = go * gain2
    gtwo = inv2 * (e - row_mean(e) - n2 * row_mean(e * n2))
    small_ref[0, 3:4, :] += col_sum(gtwo)
    glow = gtwo.astype(BF)
    gT_s[...] = glow.T

    def gact(chunk):
        r, s = chunk
        return dot_nt(glow, dns[r][s : s + CH, :])

    ga = gact(chunks[0])
    for k, (r, s) in enumerate(chunks):
        nxt = gact(chunks[k + 1]) if k + 1 < len(chunks) else None
        cs = slice(s, s + CH)
        gp = (ga * slope_s[r, :, cs]).astype(BF)
        ddn_s[r, :, cs] += dot(gT_s[...], act_s[r, :, cs])
        dup_s[r, :, cs] += dot(nT_s[...], gp)
        total = col_sum(gp.astype(F32))
        for o in range(0, CH, min(CH, D)):
            w = min(CH, D)
            line, lane = (s + o) // D, (s + o) % D
            small_ref[1 + r, line : line + 1, lane : lane + w] += total[:, o : o + w]
        t = dot_nt(gp, ups[r][:, cs])
        if k == 0:
            acc_s[...] = t
        else:
            acc_s[...] += t
        ga = nxt
    gin = gtwo + acc_s[...]
    small_ref[0, 1:2, :] += col_sum(gin * n1)
    small_ref[0, 2:3, :] += col_sum(gin)
    e = gin * gain1
    gone = inv1 * (e - row_mean(e) - n1 * row_mean(e * n1))
    small_ref[0, 0:1, :] += col_sum(gone)
    gone_ref[...] = gone
    goneT_ref[...] = gone.astype(BF).T

    @pl.when(i == n - 1)
    def _():
        dup_ref[...] = dup_s[...].astype(BF)
        ddn_ref[...] = ddn_s[...].astype(BF)


def ffn(R, CH, lens, h1, og, ups, dns, bias, vecs):
    rows, D = h1.shape
    hid = ups[0].shape[1]
    sds = jax.ShapeDtypeStruct
    row = pl.BlockSpec((R, D), lambda i: (i, 0))
    return pl.pallas_call(
        functools.partial(ffn_kernel, CH), grid=(rows // R,),
        in_specs=[SMEM, row, row, once((D, hid)), once((D, hid)), once((hid, D)), once((hid, D)),
                  once(bias[0].shape), once(bias[1].shape)] + [once((1, D))] * 5,
        out_specs=[row, row, pl.BlockSpec((D, R), lambda i: (0, i)), once((2, D, hid)), once((2, D, hid)), once((3, 8, D))],
        out_shape=[sds((rows, D), BF), sds((rows, D), F32), sds((D, rows), BF), sds((2, D, hid), BF), sds((2, D, hid), BF),
                   sds((3, 8, D), F32)],
        scratch_shapes=[pltpu.VMEM((2, R, hid), BF), pltpu.VMEM((2, R, hid), F32), pltpu.VMEM((D, R), BF),
                        pltpu.VMEM((D, R), BF), pltpu.VMEM((R, D), F32), pltpu.VMEM((2, D, hid), F32),
                        pltpu.VMEM((2, D, hid), F32)],
        compiler_params=pltpu.CompilerParams(vmem_limit_bytes=VMEM_LIMIT), name="feed_forward",
    )(lens, h1, og, *ups, *dns, *bias, *vecs)


def add_low(dst, a, b):
    lead = dst.shape[:-2]
    total = math.prod(lead)

    def one(k, carry):
        idx = []
        for s in reversed(lead):
            idx.append(k % s)
            k = k // s
        idx = tuple(reversed(idx))
        dst[idx] = (a[idx].astype(F32) + b[idx].astype(F32)).astype(BF)
        return carry

    if total == 1:
        idx = (0,) * len(lead)
        dst[idx] = (a[idx].astype(F32) + b[idx].astype(F32)).astype(BF)
    else:
        lax.fori_loop(0, total, one, 0)


class Reduce:
    def __init__(self, src, mine, out, done, order, bufs, sems, base):
        self.mine, self.out, self.done = mine, out, done
        self.z, self.y, self.core, self.x = places()
        z, y, core, x = self.z, self.y, self.core, self.x
        self.src, self.order, self.sems, self.base = src, order, sems, base
        self.rc, self.h, self.r1, self.w, self.r2, self.v, self.rz, self.full = bufs
        self.px, self.py, self.pc = at(z, y, core, 1 - x), at(z, 1 - y, core, x), at(z, y, 1 - core, x)

    def zdev(self, d):
        zt = lax.rem(self.z + d, 4)
        return zt, at(zt, self.y, self.core, self.x)

    def copies(self, stage):
        b, y, core, z = self.base, self.y, self.core, self.z
        if stage == 0:
            return [remote(self.src.at[:, 1 - core], self.rc, self.sems, b, self.pc)]
        if stage == 1:
            if self.order == "xy":
                return [remote(self.h.at[1], self.r1, self.sems, b + 1, self.px)]
            return [remote(self.h.at[:, 1 - y], self.r1, self.sems, b + 1, self.py)]
        if stage == 2:
            if self.order == "xy":
                return [remote(self.w.at[1 - y], self.r2, self.sems, b + 2, self.py)]
            return [remote(self.w.at[1], self.r2, self.sems, b + 2, self.px)]
        if stage == 3:
            out = []
            for d in (1, 2, 3):
                zt, dev = self.zdev(d)
                out.append(remote(self.v.at[zt], self.rz.at[d - 1], self.sems, b + 2 + d, dev))
            return out
        if stage == 4:
            out = []
            for d in (1, 2, 3):
                zt, dev = self.zdev(d)
                part = self.full.at[core, y, z]
                out.append(remote(part, part, self.sems, b + 5 + d, dev))
            return out
        if stage == 5:
            part = self.full.at[core, y]
            return [remote(part, part, self.sems, b + 9, self.py)]
        part = self.full.at[core]
        return [remote(part, part, self.sems, b + 10, self.pc)]

    def start(self, stage):
        for copy in self.copies(stage):
            copy.start()

    def combine(self, stage):
        y, core, z = self.y, self.core, self.z
        if stage == 0:
            add_low(self.h, self.mine, self.rc)
        elif stage == 1:
            add_low(self.w, self.h.at[0] if self.order == "xy" else self.h.at[:, y], self.r1)
        elif stage == 2:
            mine = self.w.at[y] if self.order == "xy" else self.w.at[0]
            self.v[...] = (mine[...].astype(F32) + self.r2[...].astype(F32)).astype(BF).reshape(self.v.shape)
        elif stage == 3:
            s = self.v[z].astype(F32)
            for d in range(3):
                s = s + self.rz[d].astype(F32)
            self.full[core, y, z] = s.astype(BF)

    def take(self, stage):
        for copy in self.copies(stage):
            copy.wait()
        self.combine(stage)

    def step(self, stage):
        self.take(stage)
        if stage < 6:
            self.start(stage + 1)
        else:
            self.leave().start()

    def leave(self):
        return pltpu.make_async_copy(self.full, self.out, self.done)


def reduce_bufs(width, order, rows=128):
    first = (2, rows, width)
    return [pltpu.VMEM(s, BF) for s in (
        (2, 2, rows, width), (2, 2, rows, width), first, first, (rows, width), (4, rows // 4, width),
        (3, rows // 4, width), (2, 2, 4, rows // 4, width))]


class ReduceOwn(Reduce):
    def __init__(self, src_other, src_own, out, done, bufs, sems, base):
        Reduce.__init__(self, None, None, out, done, "xy", (None, None) + tuple(bufs[4:]), sems, base)
        self.srcs = (src_own, src_other)
        self.rcs, self.hs = bufs[0:2], bufs[2:4]

    def copies(self, stage):
        b = self.base
        if stage == "other":
            return [remote(self.srcs[1].at[1 - self.core], self.rcs[1], self.sems, b + 11, self.pc)]
        if stage == "own":
            return [remote(self.srcs[0].at[1 - self.core], self.rcs[0], self.sems, b, self.pc)]
        if stage == 1:
            return [remote(self.hs[1], self.r1, self.sems, b + 1, self.px)]
        return Reduce.copies(self, stage)

    def combine(self, stage):
        if stage == "other":
            add_low(self.hs[1], self.srcs[1].at[self.core], self.rcs[1])
        elif stage == "own":
            add_low(self.hs[0], self.srcs[0].at[self.core], self.rcs[0])
        elif stage == 1:
            add_low(self.w, self.hs[0], self.r1)
        else:
            Reduce.combine(self, stage)

    def step(self, stage):
        if stage == "other":
            self.take(stage)
            self.start(1)
        elif stage == "own":
            self.take(stage)
            self.take(1)
            self.start(2)
        else:
            Reduce.step(self, stage)


def reduce_own_bufs(width, rows):
    pair = (2, rows, width)
    return [pltpu.VMEM(s, BF) for s in (
        pair, pair, pair, pair, pair, pair, (rows, width), (4, rows // 4, width), (3, rows // 4, width),
        (2, 2, 4, rows // 4, width))]


class Butterfly:
    def __init__(self, acc, recv, sems, base):
        z, y, core, x = places()
        self.acc, self.recv, self.sems, self.base = acc, recv, sems, base
        self.devices = (at(z, y, 1 - core, x), at(z, y, core, 1 - x), at(z, 1 - y, core, x),
                        at(z + 1 - 2 * (z % 2), y, core, x), at((z + 2) % 4, y, core, x))

    def copy(self, k):
        return remote(self.acc.at[k], self.recv.at[k], self.sems, self.base + k, self.devices[k])

    def start(self, k):
        self.copy(k).start()

    def take(self, k):
        self.copy(k).wait()
        if k == 1:
            self.acc[k + 1, 0] = self.acc[k, 0] + self.recv[k, 0]
            self.acc[k + 1, 1] = self.acc[k, 1] + self.recv[k, 2]
            self.acc[k + 1, 2] = self.acc[k, 2] + self.recv[k, 1]
        else:
            self.acc[k + 1] = self.acc[k] + self.recv[k]

    def step(self, k):
        self.take(k)
        if k < 4:
            self.start(k + 1)


PLAN = {
    2: ("D0 0",),
    3: ("U1 0", "D1 0",),
    6: ("D0 1", "U0 0",),
    7: ("U1 1",),
    8: ("D0 2",),
    9: ("D1 1", "U1 2", "O 0",),
    10: ("U0 1", "Qk other",),
    11: ("Qq other", "Qv other", "D0 3",),
    12: ("D1 2",),
    13: ("O 1", "U0 2", "U1 3",),
    15: ("D0 4", "O 2",),
}
TAIL_PLAN = {
    0: ("D1 3", "Qq own", "U0 3", "Qk own",),
    1: ("Qv own", "F 0",),
    2: ("F 1", "U1 4", "Qq 2", "Qk 2", "Qv 2", "D1 4", "O 3",),
    3: ("F 2", "D0 5", "Qq 3", "D0 6", "U0 4", "Qk 3", "Qv 3", "U1 5", "D1 5", "O 4", "Qq 4", "U1 6",),
    4: ("F 3", "U0 5", "Qk 4", "O 5", "D1 6", "Qv 4", "Qq 5", "F 4", "Qk 5", "Qv 5", "Qk 6", "U0 6", "O 6", "Qq 6", "Qv 6",),
}


def attn_bwd_kernel(comm, n, m, *refs):
    (gone_ref, grow_ref, qkv_ref, p_ref, wqa_ref, wqb_ref, woa_ref, wob_ref, xT_any, gT_any, att_any) = refs[:11]
    refs = refs[11:]
    if comm:
        up_any, dn_any, small_ref = refs[:3]
        gx_ref, up_out, dn_out, wo_out, wq_out, small_out = refs[3:9]
        dq_s, xT_s, gT_s, att_s, local, wo_src, q_oth, q_own, acc, recv, sems, up_s, dn_s, done = refs[9:23]
        bufs = refs[23:]
    else:
        gx_ref, wo_out, wq_out, bias_out = refs[:4]
        dq_s, xT_s, gT_s, att_s, local = refs[4:]
    s = pl.program_id(0)
    r, d = gone_ref.shape
    block = r // LMAX
    half = d // 2
    loads = [pltpu.make_async_copy(a, b, local.at[k]) for k, (a, b) in enumerate(
        ((xT_any, xT_s), (gT_any, gT_s), (att_any, att_s)))]

    if comm:
        w = up_any.shape[-1] // 2
        z, y, core, x = places()
        pieces = {}
        for k in range(2):
            cols = pl.ds(k * w, w)
            pieces["U%d" % k] = Reduce(
                up_any.at[..., cols], up_s.at[..., cols], up_out.at[..., cols], done.at[k], "xy",
                bufs[8 * k : 8 * k + 8], sems, 11 * k)
            pieces["D%d" % k] = Reduce(
                dn_any.at[..., cols], dn_s.at[..., cols], dn_out.at[..., cols], done.at[2 + k], "yx",
                bufs[16 + 8 * k : 24 + 8 * k], sems, 22 + 11 * k)
        pieces["O"] = Reduce(wo_src, wo_src.at[:, core], wo_out, done.at[4], "xy", bufs[32:40], sems, 44)
        for k, name in enumerate("qkv"):
            pieces["Q" + name] = ReduceOwn(
                q_oth.at[k], q_own.at[k], wq_out.at[k], done.at[5 + k], bufs[40 + 10 * k : 50 + 10 * k], sems,
                55 + 12 * k)
        loads += [pltpu.make_async_copy(a.at[:, core], b, local.at[3 + k]) for k, (a, b) in enumerate(
            ((up_any, up_s), (dn_any, dn_s)))]
        pieces["F"] = fly = Butterfly(acc, recv, sems, 91)
        first = pieces["U0"]

        def follow(plan):
            for entry in plan:
                name, stage = entry.split()
                pieces[name].step(int(stage) if stage.isdigit() else stage)

        @pl.when(s == 0)
        def _():
            greet(fly.devices[:3] + tuple(first.zdev(k)[1] for k in (1, 2, 3)))
            acc[0] = small_ref[...]

        @pl.when(s == 1)
        def _():
            greeted(6)
            for name in ("U0", "D0", "U1", "D1"):
                pieces[name].start(0)
            loads[3].wait()
            loads[4].wait()

        for at_step, plan in PLAN.items():
            pl.when(s == at_step)(functools.partial(follow, plan))
        for at_step, plan in TAIL_PLAN.items():
            if at_step < m:
                pl.when(s == 2 * n + at_step)(functools.partial(follow, plan))

    @pl.when(s == 0)
    def _():
        for copy in loads[3:] + loads[:3]:
            copy.start()
        if not comm:
            bias_out[...] = jnp.zeros_like(bias_out)

    def quarters(dst, value):
        for core in range(2):
            for y in range(2):
                first_row = (core * 2 + y) * (d // 4)
                dst[core, y] = value[first_row : first_row + d // 4]

    @pl.when(s == min(2, n - 1))
    def _():
        loads[1].wait()
        loads[2].wait()
        for rel in range(2):
            total = dot(gT_s[...], att_s[rel]).astype(BF)
            if comm:
                quarters(wo_src.at[rel], total)
            else:
                wo_out[rel] = total
        if comm:
            pieces["O"].start(0)

    def heads(wo, which, blk):
        ga = dot_nt(gone_ref[...].astype(BF), wo).astype(BF)
        for c in range(block):
            rs = slice(c * LMAX, (c + 1) * LMAX)
            probs = p_ref[c, 0]
            k, v = qkv_ref[1, 0, rs, :], qkv_ref[2, 0, rs, :]
            gs = stack_heads(ga[rs])
            dp = dot_nt(v, gs)
            pf = probs.astype(F32)
            ds = (pf * (dp - jnp.sum(pf * dp, axis=0, keepdims=True))).astype(BF)
            dv = dot(probs, gs)
            dk = dot(ds, stack_heads(qkv_ref[0, 0, rs, :]))
            dq = pick_heads(dot(ds.T, k)) * (1.0 / math.sqrt(HDIM))
            out = pl.ds(blk * r + c * LMAX, LMAX)
            dq_s[which, 0, out, :] = dq.astype(BF)
            dq_s[which, 1, out, :] = dk.astype(BF)
            dq_s[which, 2, out, :] = dv.astype(BF)

    def weights(which):
        for j in range(3):
            total = dot(xT_s[...], dq_s[which, j]).astype(BF)
            if comm:
                quarters((q_own, q_oth)[which].at[j], total)
                if which == 1:
                    pieces["Q" + "qkv"[j]].start("other")
                else:
                    pieces["Q" + "qkv"[j]].start("own")
            else:
                wq_out[which, j] = total
        ref, base = (acc.at[0], 1) if comm else (bias_out, 0)
        ref[base + which, 2:3, 0:half] = col_sum(dq_s[which, 0].astype(F32))
        ref[base + which, 2:3, half:d] = col_sum(dq_s[which, 2].astype(F32))

    @pl.when(s < n)
    def _():
        heads(wob_ref[...].reshape(half, d), 1, s)

        @pl.when(s == n - 1)
        def _():
            loads[0].wait()
            weights(1)

    @pl.when((s >= n) & (s < 2 * n))
    def _():
        heads(woa_ref[...], 0, s - n)

        @pl.when(s == 2 * n - 1)
        def _():
            weights(0)
            if comm:
                fly.start(0)

    @pl.when(s >= 2 * n)
    def _():
        rg = gx_ref.shape[0]
        rs = pl.ds((s - 2 * n) * rg, rg)
        total = grow_ref[...]
        for which, wq in ((1, wqb_ref), (0, wqa_ref)):
            for j in range(3):
                total += dot_nt(dq_s[which, j, rs, :], wq[j].reshape(d, half))
        gx_ref[...] = total.astype(BF)

    if comm:

        @pl.when(s == 2 * n + m - 1)
        def _():
            for at_step, plan in TAIL_PLAN.items():
                if at_step >= m:
                    follow(plan)
            for name, piece in pieces.items():
                if name != "F":
                    piece.leave().wait()
            small_out[...] = acc[5]


def attn_bwd(comm, block, gone, goneT, xT, qkv, probs, att, wq, wo, sums):
    rows, d = gone.shape
    half, r = d // 2, block * LMAX
    n = rows // r
    rg = min(rows, 4 * LMAX)
    m = rows // rg
    sds = jax.ShapeDtypeStruct

    def blk(s):
        return jnp.where(s < 2 * n, lax.rem(s, n), n - 1)

    def rel(s):
        return jnp.where(s < n, 1, 0)

    def tail(s):
        return jnp.maximum(s - 2 * n, 0)

    in_specs = [
        pl.BlockSpec((r, d), lambda s: (blk(s), 0)),
        pl.BlockSpec((rg, d), lambda s: (tail(s), 0)),
        pl.BlockSpec((3, 1, r, half), lambda s: (0, rel(s), blk(s), 0)),
        pl.BlockSpec((block, 1, LMAX, half // HDIM * LMAX), lambda s: (blk(s), rel(s), 0, 0)),
        once(wq[0].shape), once(wq[1].shape), once(wo[0].shape), once(wo[1].shape), ANY, ANY, ANY,
    ]
    gx_spec, gx_shape = pl.BlockSpec((rg, d), lambda s: (tail(s), 0)), sds((rows, d), BF)
    scratch = [pltpu.VMEM((2, 3, rows, half), BF), pltpu.VMEM(xT.shape, BF), pltpu.VMEM(goneT.shape, BF),
               pltpu.VMEM(att.shape, BF), pltpu.SemaphoreType.DMA((5,))]
    params = dict(vmem_limit_bytes=VMEM_LIMIT)
    if comm:
        up, dn, small = sums
        hid = up.shape[-1]
        split = lambda w: (2, 2, 4, d // 16, w)
        in_specs += [ANY, ANY, once(small.shape)]
        out_specs = [gx_spec, ANY, ANY, ANY, ANY, once(small.shape)]
        out_shape = [gx_shape, sds(split(hid), BF), sds(split(hid), BF), sds(split(half), BF),
                     sds((3,) + split(half), BF), sds(small.shape, F32)]
        rows4 = d // 4
        scratch += [pltpu.VMEM((2, 2, 2, rows4, half), BF), pltpu.VMEM((3, 2, 2, rows4, half), BF),
                    pltpu.VMEM((3, 2, 2, rows4, half), BF), pltpu.VMEM((6,) + small.shape, F32),
                    pltpu.VMEM((5,) + small.shape, F32), pltpu.SemaphoreType.DMA((2, 96)),
                    pltpu.VMEM((2, 2, rows4, hid), BF), pltpu.VMEM((2, 2, rows4, hid), BF),
                    pltpu.SemaphoreType.DMA((8,))]
        for _ in range(4):
            scratch += reduce_bufs(hid // 2, "xy", rows4)
        scratch += reduce_bufs(half, "xy", rows4)
        for _ in range(3):
            scratch += reduce_own_bufs(half, rows4)
        params.update(collective_id=1, has_side_effects=True)
    else:
        out_specs = [gx_spec, once((2, d, half)), once((2, 3, d, half)), once((2, 8, d))]
        out_shape = [gx_shape, sds((2, d, half), BF), sds((2, 3, d, half), BF), sds((2, 8, d), F32)]
    return pl.pallas_call(
        functools.partial(attn_bwd_kernel, comm, n, m), grid=(2 * n + m,), in_specs=in_specs, out_specs=out_specs,
        out_shape=out_shape, scratch_shapes=scratch, compiler_params=pltpu.CompilerParams(**params),
        name="attention_backward",
    )(gone, gone, qkv, probs, *wq, *wo, xT, goneT, att, *sums)


def finish_kernel(gx_ref, up_ref, dn_ref, wo_ref, wq_ref, small_ref, gx_out, up_out, dn_out, wo_out, wq_out,
                  upb_out, qvb_out, *vec_outs):
    gx_out[...] = gx_ref[...]
    up_out[...] = up_ref[...].astype(F32)
    dn_out[...] = dn_ref[...].astype(F32).T
    wq_out[...] = wq_ref[...].astype(F32)

    @pl.when(pl.program_id(0) == 0)
    def _():
        d = small_ref.shape[2]
        half = d // 2
        wo_out[...] = wo_ref[...].astype(F32).T
        for k, out in enumerate(vec_outs):
            out[...] = small_ref[0, k]
        for k in range(upb_out.shape[0] // d):
            upb_out[k * d : (k + 1) * d] = small_ref[1, k]
        qvb_out[0:1, :] = small_ref[1, 2:3, 0:half]
        qvb_out[1:2, :] = small_ref[1, 2:3, half:d]


def finish(gx, up, dn, wo, wq, small):
    rows, d = gx.shape
    hid, half = up.shape[1], wo.shape[1]
    n = 2
    sds = jax.ShapeDtypeStruct
    gx_spec = pl.BlockSpec((rows // n, d), lambda i: (i, 0))
    up_spec = pl.BlockSpec((d // n, hid), lambda i: (i, 0))
    wq_spec = pl.BlockSpec((3, d // n, half), lambda i: (0, i, 0))
    return pl.pallas_call(
        finish_kernel, grid=(n,),
        in_specs=[gx_spec, up_spec, pl.BlockSpec((d, hid // n), lambda i: (0, i)), once(wo.shape), wq_spec,
                  once(small.shape)],
        out_specs=[gx_spec, up_spec, pl.BlockSpec((hid // n, d), lambda i: (i, 0)), once((half, d)), wq_spec,
                   once((hid,)), once((2, half))] + [once((d,))] * 6,
        out_shape=[sds(gx.shape, BF), sds(up.shape, F32), sds((hid, d), F32), sds((half, d), F32), sds(wq.shape, F32),
                   sds((hid,), F32), sds((2, half), F32)] + [sds((d,), F32)] * 6,
        compiler_params=pltpu.CompilerParams(vmem_limit_bytes=VMEM_LIMIT), name="finish",
    )(gx, up, dn, wo, wq, small)


def tile_rows(rows):
    for r in (512, 640, 320):
        if rows % r == 0:
            return r
    return LMAX


def chain_block(chains):
    for c in (4, 2):
        if chains % c == 0:
            return c
    return 1


def on_device(comm, tokens, qkv_weight, qv_bias, out_weight, out_bias, gain_one, shift_one, up_weight, up_bias,
              down_weight, down_bias, gain_two, shift_two, out_grad, lengths):
    rows, d = tokens.shape
    chains = rows // LMAX
    half = d // 2
    vecs = [a[None] for a in (gain_one, shift_one, down_bias, gain_two, shift_two)]
    block = chain_block(chains)
    comm = comm and chains == 16

    def gather(a, dim):
        return lax.all_gather(a, "tensor", axis=dim, tiled=True)

    def table(qv, up):
        flat = jnp.concatenate([qv[0], qv[1], up]).astype(F32)
        return jnp.pad(flat, (0, 4096 - flat.shape[0])).reshape(2, 2, 8, 128)

    if comm:
        hid = up_weight.shape[1]
        quarters = (
            qkv_weight.reshape(3, 2, 2, 2, d // 8, half), out_weight.reshape(2, half // 2, d),
            up_weight.reshape(2, 2, 2, d // 8, hid), down_weight.reshape(2, 2, 2, hid // 8, d), up_bias,
        )
        h1, qkv, att, probs, xT, wqb, wob, wupb, wdnb, bias_b, bias = attn_fwd(
            True, 2, lengths, tokens, qkv_weight, out_weight, qv_bias, out_bias[None], quarters)
        wqs, wos, bias = (qkv_weight, wqb), (out_weight, wob), (bias, bias_b)
        ups, dns = (up_weight, wupb.reshape(d, hid)), (down_weight, wdnb.reshape(hid, d))
    else:
        wq, wo = gather(qkv_weight, 2), gather(out_weight, 0)
        wup, wdn = gather(up_weight, 1), gather(down_weight, 0)
        hid = wup.shape[1] // 2
        qvb, upb = gather(qv_bias, 1), gather(up_bias, 0)
        bias = (table(qvb[:, :half], upb[:hid]), table(qvb[:, half:], upb[hid:]))
        wqs, wos = (wq[:, :, :half], wq[:, :, half:]), (wo[:half], wo[half:])
        ups, dns = (wup[:, :hid], wup[:, hid:]), (wdn[:hid], wdn[hid:])
        h1, qkv, att, probs, xT = attn_fwd(
            False, block, lengths, tokens, wqs[0], wos[0], bias[0], out_bias[None], (wqs[1], wos[1], bias[1]))
    out, gone, goneT, dup, ddn, small = ffn(tile_rows(rows), 256, lengths, h1, out_grad, ups, dns, bias, vecs)
    small_block = 2 if chains % 2 == 0 else 1
    if comm:
        split = (2, 2, 2, d // 4, hid)
        gx, dup, ddn, dwo, dwq, small = attn_bwd(
            True, small_block, gone, goneT, xT, qkv, probs, att, wqs, wos, (dup.reshape(split), ddn.reshape(split), small))
        gx, dup, ddn, dwo, dwq, dupb, dqvb, *vecs = finish(
            gx, dup.reshape(d, hid), ddn.reshape(d, hid), dwo.reshape(d, half), dwq.reshape(3, d, half), small)
    else:
        gx, dwo, dwq, dbias = attn_bwd(False, small_block, gone, goneT, xT, qkv, probs, att, wqs, wos, ())

        def total(a, dim):
            a = lax.psum_scatter(a.astype(BF), "tensor", scatter_dimension=dim, tiled=True)
            return lax.psum(a, "dp").astype(F32)

        dwq = total(dwq.transpose(1, 2, 0, 3).reshape(3, d, d), 2)
        dwo = total(jnp.concatenate([dwo[0], dwo[1]], axis=1), 1).T
        dup = total(jnp.concatenate([dup[0], dup[1]], axis=1), 1)
        ddn = total(jnp.concatenate([ddn[0], ddn[1]], axis=1), 1).T
        dupb = total(small[1:, : hid // d].reshape(2 * hid), 0)
        dqvb = total(dbias[:, 2].reshape(2, 2, half).transpose(1, 0, 2).reshape(2, d), 1)
        vecs = lax.psum(small[0], ("dp", "tensor"))
    return (out, gx, dwq, dqvb, dwo, vecs[0], vecs[1], vecs[2], dup, dupb, ddn, vecs[3], vecs[4], vecs[5])


def solution(mesh):
    comm = mesh.shape["dp"] == 16 and mesh.shape["tensor"] == 2
    rows = P(("dp", "tensor"), None)
    in_specs = (rows, P(None, None, "tensor"), P(None, "tensor"), P("tensor", None), P(), P(), P(), P(None, "tensor"),
                P("tensor"), P("tensor", None), P(), P(), P(), rows, P("dp"))
    out_specs = (rows, rows, P(None, None, "tensor"), P(None, "tensor"), P("tensor", None), P(), P(), P(),
                 P(None, "tensor"), P("tensor"), P("tensor", None), P(), P(), P())
    return jax.shard_map(functools.partial(on_device, comm), mesh=mesh, in_specs=in_specs, out_specs=out_specs,
                         check_vma=False)
```

```python
import functools
import math

import jax
import jax.numpy as jnp
from jax import lax
from jax.experimental import pallas as pl
from jax.experimental.pallas import tpu as pltpu
from jax.sharding import PartitionSpec as P

F32 = jnp.float32
BF = jnp.bfloat16
LMAX = 160
HDIM = 64
EPS = 1e-12
NEG = -1e30
MESH = pl.DeviceIdType.MESH
VMEM_LIMIT = 60 << 20

ERF_P = 0.3275911 * math.sqrt(0.5)
ERF_A = (0.254829592, -0.284496736, 1.421413741, -1.453152027, 1.061405429)


def dot(a, b):
    return lax.dot_general(a, b, (((1,), (0,)), ((), ())), preferred_element_type=F32)


def dot_nt(a, b):
    return lax.dot_general(a, b, (((1,), (1,)), ((), ())), preferred_element_type=F32)


def gelu_parts(v):
    bell = jnp.exp(v * v * -0.5)
    t = 1.0 / (1.0 + ERF_P * jnp.abs(v))
    tail = 0.5 * ERF_A[4]
    for a in ERF_A[3::-1]:
        tail = tail * t + 0.5 * a
    tail = tail * t * bell
    phi = jnp.where(v >= 0, 1.0 - tail, tail)
    return v * phi, phi + v * (bell * (1.0 / math.sqrt(2.0 * math.pi)))


def row_mean(x):
    return jnp.sum(x, axis=1, keepdims=True) * (1.0 / x.shape[1])


def col_sum(x):
    return jnp.sum(x, axis=0, keepdims=True)


def lane_head(width):
    return lax.broadcasted_iota(jnp.int32, (1, width), 1) // HDIM


def stack_heads(x):
    head = lane_head(x.shape[1])
    return jnp.concatenate(
        [jnp.where(head == h, x, jnp.zeros_like(x)) for h in range(x.shape[1] // HDIM)], axis=0
    )


def pick_heads(x):
    heads = x.shape[1] // HDIM
    r = x.shape[0] // heads
    head = lane_head(x.shape[1])
    out = x[:r]
    for h in range(1, heads):
        out = jnp.where(head == h, x[h * r : (h + 1) * r], out)
    return out


def places():
    dp = lax.axis_index("dp")
    return dp // 4, (dp // 2) % 2, dp % 2, lax.axis_index("tensor")


def at(z, y, core, x):
    return (z * 4 + y * 2 + core, x)


def greet(neighbours):
    barrier = pltpu.get_barrier_semaphore()
    for device in neighbours:
        pl.semaphore_signal(barrier, inc=1, device_id=device, device_id_type=MESH)


def greeted(count):
    pl.semaphore_wait(pltpu.get_barrier_semaphore(), count)


def remote(src, dst, sems, slot, device):
    return pltpu.make_async_remote_copy(
        src_ref=src, dst_ref=dst, send_sem=sems.at[0, slot], recv_sem=sems.at[1, slot],
        device_id=device, device_id_type=MESH,
    )


class Gather:
    PARTS = {
        "qa": (0, (slice(None),), (0,), True), "qb": (0, (slice(None),), (1,), True), "bias": (4, (), (), False),
        "wo": (1, (), (), False), "ua": (2, (), (0,), True), "ub": (2, (), (1,), True), "da": (3, (), (0,), True),
        "db": (3, (), (1,), True),
    }

    def __init__(self, own, other, sems):
        z, y, core, x = places()
        self.px, self.py, self.pc = at(z, y, core, 1 - x), at(z, 1 - y, core, x), at(z, y, 1 - core, x)
        self.own, self.other, self.sems = own, other, sems
        self.y, self.core = y, core

    def copy(self, name, stage):
        array, before, after, split = self.PARTS[name]
        own, other = self.own[array], self.other[array]
        lines = (self.y, 1 - self.y) if split else (None, None)
        here, there = (before + ((y,) if split else ()) + (self.core,) + after for y in lines)
        src, part, device = (
            (own, here, self.px), (other, here, self.py), (other, here, self.pc), (other, there, self.pc)
        )[stage]
        slot = 4 * list(self.PARTS).index(name) + stage
        return remote(src.at[part], other.at[part], self.sems, slot, device)

    def stages(self, name):
        return (0, 1, 2, 3) if self.PARTS[name][3] else (0, 2)

    def fetch(self, name):
        self.copy(name, 0).start()

    def spread(self, name):
        self.copy(name, 0).wait_recv()
        for stage in self.stages(name)[1:-1] if self.PARTS[name][3] else (2,):
            self.copy(name, stage).start()

    def finish(self, name):
        self.copy(name, 1).wait_recv()
        self.copy(name, 3).start()

    def arrived(self, name):
        for stage in self.stages(name)[2:] if self.PARTS[name][3] else (2,):
            self.copy(name, stage).wait_recv()

    def sent(self, name):
        for stage in self.stages(name):
            self.copy(name, stage).wait_send()


GATHER_PLAN = {
    1: ("fetch qa", "fetch qb", "fetch bias", "fetch wo", "fetch ua", "fetch ub", "fetch da", "fetch db",),
    4: ("spread qa",),
    5: ("spread qb",),
    6: ("spread bias",),
    7: ("finish qa", "spread wo",),
    8: ("finish qb", "spread ua", "arrived qa", "arrived qb", "arrived bias", "arrived wo",),
    9: ("spread ub",),
    11: ("finish ua", "spread da",),
    12: ("spread db",),
    13: ("finish ub",),
    14: ("finish da",),
}
GATHER_END = ("arrived ua", "arrived ub", "finish db", "arrived da", "arrived db",)


def attn_fwd_kernel(comm, *refs):
    if comm:
        (lens_ref, x_ref, wq_ref, wo_ref, qv_ref, ob_ref, wq_any, wo_any, up_any, dn_any, upb_ref,
         h1_ref, qkv_ref, att_ref, p_ref, xT_ref, wq_out, wo_out, up_out, dn_out, bias_out,
         own_out, att_s, wq_s, wo_s, bias_s, bias_ref, sems, local) = refs
    else:
        (lens_ref, x_ref, wq_ref, wo_ref, bias_ref, ob_ref, wq_s, wo_s, bias_s,
         h1_ref, qkv_ref, att_ref, p_ref, xT_ref, att_s) = refs
    p, i = pl.program_id(0), pl.program_id(1)
    rows, d = h1_ref.shape
    block = rows // LMAX
    half = d // 2
    sub = x_ref.shape[0] // rows
    if comm:
        gather = Gather((wq_any, wo_any, up_any, dn_any, bias_ref), (wq_s, wo_s, up_out, dn_out, bias_s), sems)
        step = p * pl.num_programs(1) + i
        keep = [pltpu.make_async_copy(a, b, local.at[k]) for k, (a, b) in enumerate(
            ((wq_s, wq_out), (wo_s, wo_out), (bias_s, bias_out)))]

        def follow(plan):
            for entry in plan:
                action, name = entry.split()
                getattr(gather, action)(name)

        @pl.when(step == 0)
        def _():
            bias_ref[...] = jnp.zeros_like(bias_ref)
            qv, up = qv_ref[...].astype(F32), upb_ref[...].astype(F32).reshape(-1, 128)
            lines = [qv[k : k + 1, o : o + 128] for k in range(2) for o in range(0, half, 128)]
            lines += [up[k : k + 1] for k in range(up.shape[0])]
            for k, line in enumerate(lines):
                bias_ref[k // 16, k // 8 % 2, k % 8 : k % 8 + 1, :] = line
            own_out[...] = bias_ref[...]
            greet((gather.px, gather.py, gather.pc))

        @pl.when(step == 1)
        def _():
            greeted(3)

        for at_step, plan in GATHER_PLAN.items():
            pl.when(step == at_step)(functools.partial(follow, plan))

        @pl.when(step == 8)
        def _():
            for copy in keep:
                copy.start()

    x = x_ref[pl.ds(lax.rem(i, sub) * rows, rows), :] if sub > 1 else x_ref[...]
    first = lax.axis_index("tensor") * (pl.num_programs(1) * block)
    kpos = lax.broadcasted_iota(jnp.int32, (LMAX, 1), 0)

    def heads(wq, bias_of):
        for j in range(3):
            t = dot(x, wq[j].reshape(d, half))
            if j != 1:
                t += lanes(bias_of, j * half // 256, half)
            t = t.astype(BF)
            if j == 0:
                t = t * jnp.asarray(1.0 / math.sqrt(HDIM), BF)
            qkv_ref[j, 0] = t
        for c in range(block):
            rs = slice(c * LMAX, (c + 1) * LMAX)
            bias = jnp.where(kpos < lens_ref[first + i * block + c], 0.0, NEG).astype(F32)
            st = dot_nt(qkv_ref[1, 0, rs, :], stack_heads(qkv_ref[0, 0, rs, :])) + bias
            e = jnp.exp(st - jnp.max(st, axis=0, keepdims=True))
            probs = (e * (1.0 / jnp.sum(e, axis=0, keepdims=True))).astype(BF)
            p_ref[c, 0] = probs
            o = pick_heads(dot(probs.T, qkv_ref[2, 0, rs, :])).astype(BF)
            att_ref[0, rs, :] = o

    @pl.when(p == 0)
    def _():
        heads(wq_ref, bias_ref)
        att_s[i] = att_ref[0]

        @pl.when(lax.rem(i, sub) == 0)
        def _():
            xT_ref[...] = x_ref[...].T

    @pl.when(p == 1)
    def _():
        heads(wq_s, bias_s)
        wo = wo_s[...].reshape(half, d)
        h1_ref[...] = x.astype(F32) + dot(att_s[i], wo_ref[...]) + dot(att_ref[0], wo) + ob_ref[...]

    if comm:

        @pl.when(step == 2 * pl.num_programs(1) - 1)
        def _():
            follow(GATHER_END)
            for copy in keep:
                copy.wait()
            for name in gather.PARTS:
                gather.sent(name)


def lanes(ref, line, width):
    parts = [ref[k // 16, k // 8 % 2, k % 8 : k % 8 + 1, :] for k in range(line, line + width // 128)]
    return parts[0] if len(parts) == 1 else jnp.concatenate(parts, axis=1)


def once(shape):
    return pl.BlockSpec(shape, lambda *_: (0,) * len(shape), pipeline_mode=pl.Buffered(1))


ANY = pl.BlockSpec(memory_space=pl.ANY)
SMEM = pl.BlockSpec(memory_space=pltpu.SMEM)


def attn_fwd(comm, block, lens, x, wq, wo, bias, ob, others):
    rows, d = x.shape
    half, r = d // 2, block * LMAX
    n = rows // r
    sds = jax.ShapeDtypeStruct
    sub = 2 if n % 2 == 0 else 1
    in_specs = [SMEM, pl.BlockSpec((sub * r, d), lambda p, i: (i // sub, 0)), once((3, d, half)), once((half, d)), once(bias.shape), once((1, d))]
    out_specs = [
        pl.BlockSpec((r, d), lambda p, i: (i * p, 0)),
        pl.BlockSpec((3, 1, r, half), lambda p, i: (0, p, i, 0)),
        pl.BlockSpec((1, r, half), lambda p, i: (p, i, 0)),
        pl.BlockSpec((block, 1, LMAX, half // HDIM * LMAX), lambda p, i: (i, p, 0, 0)),
        pl.BlockSpec((d, sub * r), lambda p, i: (0, (i * (1 - p) + (n - 1) * p) // sub)),
    ]
    out_shape = [
        sds((rows, d), F32),
        sds((3, 2, rows, half), BF),
        sds((2, rows, half), BF),
        sds((rows // LMAX, 2, LMAX, half // HDIM * LMAX), BF),
        sds((d, rows), BF),
    ]
    scratch = [pltpu.VMEM((n, r, half), BF)]
    args = [lens, x, wq, wo, bias, ob]
    if comm:
        table = sds((2, 2, 8, 128), F32)
        in_specs += [ANY] * 4 + [once(others[4].shape)]
        out_specs += [ANY] * 5 + [once(table.shape)]
        out_shape += [sds(a.shape, a.dtype) for a in others[:4]] + [table, table]
        scratch += [pltpu.VMEM(a.shape, a.dtype) for a in others[:2] + (table, table)]
        scratch += [pltpu.SemaphoreType.DMA((2, 32)), pltpu.SemaphoreType.DMA((3,))]
    else:
        in_specs += [once((3, d, half)), once((half, d)), once(bias.shape)]
    params = dict(vmem_limit_bytes=VMEM_LIMIT)
    if comm:
        params.update(collective_id=0, has_side_effects=True)
    return pl.pallas_call(
        functools.partial(attn_fwd_kernel, comm), grid=(2, n), in_specs=in_specs, out_specs=out_specs,
        out_shape=out_shape, scratch_shapes=scratch, compiler_params=pltpu.CompilerParams(**params),
        name="attention_forward",
    )(*args, *others)


def ffn_kernel(CH, lens_ref, h1_ref, og_ref, upa_ref, upb_ref, dna_ref, dnb_ref, ba_ref, bb_ref,
               gain1_ref, shift1_ref, bias_dn_ref, gain2_ref, shift2_ref,
               out_ref, gone_ref, goneT_ref, dup_ref, ddn_ref, small_ref,
               act_s, slope_s, nT_s, gT_s, acc_s, dup_s, ddn_s):
    i, n = pl.program_id(0), pl.num_programs(0)
    R, D = h1_ref.shape
    hid = upa_ref.shape[1]
    chunks = [(r, k * CH) for r in range(2) for k in range(hid // CH)]
    ups, dns, biases = (upa_ref, upb_ref), (dna_ref, dnb_ref), (ba_ref, bb_ref)

    @pl.when(i == 0)
    def _():
        dup_s[...] = jnp.zeros_like(dup_s)
        ddn_s[...] = jnp.zeros_like(ddn_s)
        small_ref[...] = jnp.zeros_like(small_ref)

    gain1, shift1, bias_dn, gain2, shift2 = (
        ref[...] for ref in (gain1_ref, shift1_ref, bias_dn_ref, gain2_ref, shift2_ref))
    h = h1_ref[...]
    c = h - row_mean(h)
    inv1 = lax.rsqrt(row_mean(c * c) + EPS)
    n1 = c * inv1
    normed = n1 * gain1 + shift1
    nlow = normed.astype(BF)
    nT_s[...] = nlow.T

    def up(chunk):
        r, s = chunk
        return dot(nlow, ups[r][:, s : s + CH]) + lanes(biases[r], (D + s) // 128, CH)

    pre = up(chunks[0])
    for k, (r, s) in enumerate(chunks):
        nxt = up(chunks[k + 1]) if k + 1 < len(chunks) else None
        a, sl = gelu_parts(pre)
        a = a.astype(BF)
        act_s[r, :, s : s + CH] = a
        slope_s[r, :, s : s + CH] = sl
        t = dot(a, dns[r][s : s + CH, :])
        if k == 0:
            acc_s[...] = t
        else:
            acc_s[...] += t
        pre = nxt
    h2 = normed + acc_s[...] + bias_dn
    c2 = h2 - row_mean(h2)
    inv2 = lax.rsqrt(row_mean(c2 * c2) + EPS)
    n2 = c2 * inv2
    out_ref[...] = (n2 * gain2 + shift2).astype(BF)

    row = i * R + lax.broadcasted_iota(jnp.int32, (R, 1), 0)
    live = jnp.zeros((R, 1), F32)
    first = (i * R) // LMAX
    for j in range((R - 2) // LMAX + 2):
        ch = jnp.minimum(first + j, n * R // LMAX - 1)
        length = lens_ref[lax.axis_index("tensor") * (n * R // LMAX) + ch]
        live = jnp.where((row >= ch * LMAX) & (row < ch * LMAX + length), 1.0, live)
    go = og_ref[...].astype(F32) * live
    small_ref[0, 4:5, :] += col_sum(go * n2)
    small_ref[0, 5:6, :] += col_sum(go)
    e = go * gain2
    gtwo = inv2 * (e - row_mean(e) - n2 * row_mean(e * n2))
    small_ref[0, 3:4, :] += col_sum(gtwo)
    glow = gtwo.astype(BF)
    gT_s[...] = glow.T

    def gact(chunk):
        r, s = chunk
        return dot_nt(glow, dns[r][s : s + CH, :])

    ga = gact(chunks[0])
    for k, (r, s) in enumerate(chunks):
        nxt = gact(chunks[k + 1]) if k + 1 < len(chunks) else None
        cs = slice(s, s + CH)
        gp = (ga * slope_s[r, :, cs]).astype(BF)
        ddn_s[r, :, cs] += dot(gT_s[...], act_s[r, :, cs])
        dup_s[r, :, cs] += dot(nT_s[...], gp)
        total = col_sum(gp.astype(F32))
        for o in range(0, CH, min(CH, D)):
            w = min(CH, D)
            line, lane = (s + o) // D, (s + o) % D
            small_ref[1 + r, line : line + 1, lane : lane + w] += total[:, o : o + w]
        t = dot_nt(gp, ups[r][:, cs])
        if k == 0:
            acc_s[...] = t
        else:
            acc_s[...] += t
        ga = nxt
    gin = gtwo + acc_s[...]
    small_ref[0, 1:2, :] += col_sum(gin * n1)
    small_ref[0, 2:3, :] += col_sum(gin)
    e = gin * gain1
    gone = inv1 * (e - row_mean(e) - n1 * row_mean(e * n1))
    small_ref[0, 0:1, :] += col_sum(gone)
    gone_ref[...] = gone
    goneT_ref[...] = gone.astype(BF).T

    @pl.when(i == n - 1)
    def _():
        dup_ref[...] = dup_s[...].astype(BF)
        ddn_ref[...] = ddn_s[...].astype(BF)


def ffn(R, CH, lens, h1, og, ups, dns, bias, vecs):
    rows, D = h1.shape
    hid = ups[0].shape[1]
    sds = jax.ShapeDtypeStruct
    row = pl.BlockSpec((R, D), lambda i: (i, 0))
    return pl.pallas_call(
        functools.partial(ffn_kernel, CH), grid=(rows // R,),
        in_specs=[SMEM, row, row, once((D, hid)), once((D, hid)), once((hid, D)), once((hid, D)),
                  once(bias[0].shape), once(bias[1].shape)] + [once((1, D))] * 5,
        out_specs=[row, row, pl.BlockSpec((D, R), lambda i: (0, i)), once((2, D, hid)), once((2, D, hid)), once((3, 8, D))],
        out_shape=[sds((rows, D), BF), sds((rows, D), F32), sds((D, rows), BF), sds((2, D, hid), BF), sds((2, D, hid), BF),
                   sds((3, 8, D), F32)],
        scratch_shapes=[pltpu.VMEM((2, R, hid), BF), pltpu.VMEM((2, R, hid), F32), pltpu.VMEM((D, R), BF),
                        pltpu.VMEM((D, R), BF), pltpu.VMEM((R, D), F32), pltpu.VMEM((2, D, hid), F32),
                        pltpu.VMEM((2, D, hid), F32)],
        compiler_params=pltpu.CompilerParams(vmem_limit_bytes=VMEM_LIMIT), name="feed_forward",
    )(lens, h1, og, *ups, *dns, *bias, *vecs)


def add_low(dst, a, b):
    lead = dst.shape[:-2]
    total = math.prod(lead)

    def one(k, carry):
        idx = []
        for s in reversed(lead):
            idx.append(k % s)
            k = k // s
        idx = tuple(reversed(idx))
        dst[idx] = (a[idx].astype(F32) + b[idx].astype(F32)).astype(BF)
        return carry

    if total == 1:
        idx = (0,) * len(lead)
        dst[idx] = (a[idx].astype(F32) + b[idx].astype(F32)).astype(BF)
    else:
        lax.fori_loop(0, total, one, 0)


class Reduce:
    def __init__(self, src, mine, out, done, order, bufs, sems, base):
        self.mine, self.out, self.done = mine, out, done
        self.z, self.y, self.core, self.x = places()
        z, y, core, x = self.z, self.y, self.core, self.x
        self.src, self.order, self.sems, self.base = src, order, sems, base
        self.rc, self.h, self.r1, self.w, self.r2, self.v, self.rz, self.full = bufs
        self.px, self.py, self.pc = at(z, y, core, 1 - x), at(z, 1 - y, core, x), at(z, y, 1 - core, x)

    def zdev(self, d):
        zt = lax.rem(self.z + d, 4)
        return zt, at(zt, self.y, self.core, self.x)

    def copies(self, stage):
        b, y, core, z = self.base, self.y, self.core, self.z
        if stage == 0:
            return [remote(self.src.at[:, 1 - core], self.rc, self.sems, b, self.pc)]
        if stage == 1:
            if self.order == "xy":
                return [remote(self.h.at[1], self.r1, self.sems, b + 1, self.px)]
            return [remote(self.h.at[:, 1 - y], self.r1, self.sems, b + 1, self.py)]
        if stage == 2:
            if self.order == "xy":
                return [remote(self.w.at[1 - y], self.r2, self.sems, b + 2, self.py)]
            return [remote(self.w.at[1], self.r2, self.sems, b + 2, self.px)]
        if stage == 3:
            out = []
            for d in (1, 2, 3):
                zt, dev = self.zdev(d)
                out.append(remote(self.v.at[zt], self.rz.at[d - 1], self.sems, b + 2 + d, dev))
            return out
        if stage == 4:
            out = []
            for d in (1, 2, 3):
                zt, dev = self.zdev(d)
                part = self.full.at[core, y, z]
                out.append(remote(part, part, self.sems, b + 5 + d, dev))
            return out
        if stage == 5:
            part = self.full.at[core, y]
            return [remote(part, part, self.sems, b + 9, self.py)]
        part = self.full.at[core]
        return [remote(part, part, self.sems, b + 10, self.pc)]

    def start(self, stage):
        for copy in self.copies(stage):
            copy.start()

    def combine(self, stage):
        y, core, z = self.y, self.core, self.z
        if stage == 0:
            add_low(self.h, self.mine, self.rc)
        elif stage == 1:
            add_low(self.w, self.h.at[0] if self.order == "xy" else self.h.at[:, y], self.r1)
        elif stage == 2:
            mine = self.w.at[y] if self.order == "xy" else self.w.at[0]
            self.v[...] = (mine[...].astype(F32) + self.r2[...].astype(F32)).astype(BF).reshape(self.v.shape)
        elif stage == 3:
            s = self.v[z].astype(F32)
            for d in range(3):
                s = s + self.rz[d].astype(F32)
            self.full[core, y, z] = s.astype(BF)

    def take(self, stage):
        for copy in self.copies(stage):
            copy.wait()
        self.combine(stage)

    def step(self, stage):
        self.take(stage)
        if stage < 6:
            self.start(stage + 1)
        else:
            self.leave().start()

    def leave(self):
        return pltpu.make_async_copy(self.full, self.out, self.done)


def reduce_bufs(width, order, rows=128):
    first = (2, rows, width)
    return [pltpu.VMEM(s, BF) for s in (
        (2, 2, rows, width), (2, 2, rows, width), first, first, (rows, width), (4, rows // 4, width),
        (3, rows // 4, width), (2, 2, 4, rows // 4, width))]


class ReduceOwn(Reduce):
    def __init__(self, src_other, src_own, out, done, bufs, sems, base):
        Reduce.__init__(self, None, None, out, done, "xy", (None, None) + tuple(bufs[4:]), sems, base)
        self.srcs = (src_own, src_other)
        self.rcs, self.hs = bufs[0:2], bufs[2:4]

    def copies(self, stage):
        b = self.base
        if stage == "other":
            return [remote(self.srcs[1].at[1 - self.core], self.rcs[1], self.sems, b + 11, self.pc)]
        if stage == "own":
            return [remote(self.srcs[0].at[1 - self.core], self.rcs[0], self.sems, b, self.pc)]
        if stage == 1:
            return [remote(self.hs[1], self.r1, self.sems, b + 1, self.px)]
        return Reduce.copies(self, stage)

    def combine(self, stage):
        if stage == "other":
            add_low(self.hs[1], self.srcs[1].at[self.core], self.rcs[1])
        elif stage == "own":
            add_low(self.hs[0], self.srcs[0].at[self.core], self.rcs[0])
        elif stage == 1:
            add_low(self.w, self.hs[0], self.r1)
        else:
            Reduce.combine(self, stage)

    def step(self, stage):
        if stage == "other":
            self.take(stage)
            self.start(1)
        elif stage == "own":
            self.take(stage)
            self.take(1)
            self.start(2)
        else:
            Reduce.step(self, stage)


def reduce_own_bufs(width, rows):
    pair = (2, rows, width)
    return [pltpu.VMEM(s, BF) for s in (
        pair, pair, pair, pair, pair, pair, (rows, width), (4, rows // 4, width), (3, rows // 4, width),
        (2, 2, 4, rows // 4, width))]


class Butterfly:
    def __init__(self, acc, recv, sems, base):
        z, y, core, x = places()
        self.acc, self.recv, self.sems, self.base = acc, recv, sems, base
        self.devices = (at(z, y, 1 - core, x), at(z, y, core, 1 - x), at(z, 1 - y, core, x),
                        at(z + 1 - 2 * (z % 2), y, core, x), at((z + 2) % 4, y, core, x))

    def copy(self, k):
        return remote(self.acc.at[k], self.recv.at[k], self.sems, self.base + k, self.devices[k])

    def start(self, k):
        self.copy(k).start()

    def take(self, k):
        self.copy(k).wait()
        if k == 1:
            self.acc[k + 1, 0] = self.acc[k, 0] + self.recv[k, 0]
            self.acc[k + 1, 1] = self.acc[k, 1] + self.recv[k, 2]
            self.acc[k + 1, 2] = self.acc[k, 2] + self.recv[k, 1]
        else:
            self.acc[k + 1] = self.acc[k] + self.recv[k]

    def step(self, k):
        self.take(k)
        if k < 4:
            self.start(k + 1)


PLAN = {
    2: ("D0 0",),
    3: ("U1 0", "D1 0",),
    6: ("D0 1", "U0 0",),
    7: ("U1 1",),
    8: ("D0 2",),
    9: ("D1 1", "U1 2", "O 0",),
    10: ("U0 1", "Qk other",),
    11: ("Qq other", "Qv other", "D0 3",),
    12: ("D1 2",),
    13: ("O 1", "U0 2", "U1 3",),
    15: ("D0 4", "O 2",),
}
TAIL_PLAN = {
    0: ("D1 3", "Qq own", "U0 3", "Qk own",),
    1: ("Qv own", "F 0",),
    2: ("F 1", "U1 4", "Qq 2", "Qk 2", "Qv 2", "D1 4", "O 3",),
    3: ("F 2", "D0 5", "Qq 3", "D0 6", "U0 4", "Qk 3", "Qv 3", "U1 5", "D1 5", "O 4", "Qq 4", "U1 6",),
    4: ("F 3", "U0 5", "Qk 4", "O 5", "D1 6", "Qv 4", "Qq 5", "F 4", "Qk 5", "Qv 5", "Qk 6", "U0 6", "O 6", "Qq 6", "Qv 6",),
}


def attn_bwd_kernel(comm, n, m, *refs):
    (gone_ref, grow_ref, qkv_ref, p_ref, wqa_ref, wqb_ref, woa_ref, wob_ref, xT_any, gT_any, att_any) = refs[:11]
    refs = refs[11:]
    if comm:
        up_any, dn_any, small_ref = refs[:3]
        gx_ref, up_out, dn_out, wo_out, wq_out, small_out = refs[3:9]
        dq_s, xT_s, gT_s, att_s, local, wo_src, q_oth, q_own, acc, recv, sems, up_s, dn_s, done = refs[9:23]
        bufs = refs[23:]
    else:
        gx_ref, wo_out, wq_out, bias_out = refs[:4]
        dq_s, xT_s, gT_s, att_s, local = refs[4:]
    s = pl.program_id(0)
    r, d = gone_ref.shape
    block = r // LMAX
    half = d // 2
    loads = [pltpu.make_async_copy(a, b, local.at[k]) for k, (a, b) in enumerate(
        ((xT_any, xT_s), (gT_any, gT_s), (att_any, att_s)))]

    if comm:
        w = up_any.shape[-1] // 2
        z, y, core, x = places()
        pieces = {}
        for k in range(2):
            cols = pl.ds(k * w, w)
            pieces["U%d" % k] = Reduce(
                up_any.at[..., cols], up_s.at[..., cols], up_out.at[..., cols], done.at[k], "xy",
                bufs[8 * k : 8 * k + 8], sems, 11 * k)
            pieces["D%d" % k] = Reduce(
                dn_any.at[..., cols], dn_s.at[..., cols], dn_out.at[..., cols], done.at[2 + k], "yx",
                bufs[16 + 8 * k : 24 + 8 * k], sems, 22 + 11 * k)
        pieces["O"] = Reduce(wo_src, wo_src.at[:, core], wo_out, done.at[4], "xy", bufs[32:40], sems, 44)
        for k, name in enumerate("qkv"):
            pieces["Q" + name] = ReduceOwn(
                q_oth.at[k], q_own.at[k], wq_out.at[k], done.at[5 + k], bufs[40 + 10 * k : 50 + 10 * k], sems,
                55 + 12 * k)
        loads += [pltpu.make_async_copy(a.at[:, core], b, local.at[3 + k]) for k, (a, b) in enumerate(
            ((up_any, up_s), (dn_any, dn_s)))]
        pieces["F"] = fly = Butterfly(acc, recv, sems, 91)
        first = pieces["U0"]

        def follow(plan):
            for entry in plan:
                name, stage = entry.split()
                pieces[name].step(int(stage) if stage.isdigit() else stage)

        @pl.when(s == 0)
        def _():
            greet(fly.devices[:3] + tuple(first.zdev(k)[1] for k in (1, 2, 3)))
            acc[0] = small_ref[...]

        @pl.when(s == 1)
        def _():
            greeted(6)
            for name in ("U0", "D0", "U1", "D1"):
                pieces[name].start(0)
            loads[3].wait()
            loads[4].wait()

        for at_step, plan in PLAN.items():
            pl.when(s == at_step)(functools.partial(follow, plan))
        for at_step, plan in TAIL_PLAN.items():
            if at_step < m:
                pl.when(s == 2 * n + at_step)(functools.partial(follow, plan))

    @pl.when(s == 0)
    def _():
        for copy in loads[3:] + loads[:3]:
            copy.start()
        if not comm:
            bias_out[...] = jnp.zeros_like(bias_out)

    def quarters(dst, value):
        for core in range(2):
            for y in range(2):
                first_row = (core * 2 + y) * (d // 4)
                dst[core, y] = value[first_row : first_row + d // 4]

    @pl.when(s == min(2, n - 1))
    def _():
        loads[1].wait()
        loads[2].wait()
        for rel in range(2):
            total = dot(gT_s[...], att_s[rel]).astype(BF)
            if comm:
                quarters(wo_src.at[rel], total)
            else:
                wo_out[rel] = total
        if comm:
            pieces["O"].start(0)

    def heads(wo, which, blk):
        ga = dot_nt(gone_ref[...].astype(BF), wo).astype(BF)
        for c in range(block):
            rs = slice(c * LMAX, (c + 1) * LMAX)
            probs = p_ref[c, 0]
            k, v = qkv_ref[1, 0, rs, :], qkv_ref[2, 0, rs, :]
            gs = stack_heads(ga[rs])
            dp = dot_nt(v, gs)
            pf = probs.astype(F32)
            ds = (pf * (dp - jnp.sum(pf * dp, axis=0, keepdims=True))).astype(BF)
            dv = dot(probs, gs)
            dk = dot(ds, stack_heads(qkv_ref[0, 0, rs, :]))
            dq = pick_heads(dot(ds.T, k)) * (1.0 / math.sqrt(HDIM))
            out = pl.ds(blk * r + c * LMAX, LMAX)
            dq_s[which, 0, out, :] = dq.astype(BF)
            dq_s[which, 1, out, :] = dk.astype(BF)
            dq_s[which, 2, out, :] = dv.astype(BF)

    def weights(which):
        for j in range(3):
            total = dot(xT_s[...], dq_s[which, j]).astype(BF)
            if comm:
                quarters((q_own, q_oth)[which].at[j], total)
                if which == 1:
                    pieces["Q" + "qkv"[j]].start("other")
                else:
                    pieces["Q" + "qkv"[j]].start("own")
            else:
                wq_out[which, j] = total
        ref, base = (acc.at[0], 1) if comm else (bias_out, 0)
        ref[base + which, 2:3, 0:half] = col_sum(dq_s[which, 0].astype(F32))
        ref[base + which, 2:3, half:d] = col_sum(dq_s[which, 2].astype(F32))

    @pl.when(s < n)
    def _():
        heads(wob_ref[...].reshape(half, d), 1, s)

        @pl.when(s == n - 1)
        def _():
            loads[0].wait()
            weights(1)

    @pl.when((s >= n) & (s < 2 * n))
    def _():
        heads(woa_ref[...], 0, s - n)

        @pl.when(s == 2 * n - 1)
        def _():
            weights(0)
            if comm:
                fly.start(0)

    @pl.when(s >= 2 * n)
    def _():
        rg = gx_ref.shape[0]
        rs = pl.ds((s - 2 * n) * rg, rg)
        total = grow_ref[...]
        for which, wq in ((1, wqb_ref), (0, wqa_ref)):
            for j in range(3):
                total += dot_nt(dq_s[which, j, rs, :], wq[j].reshape(d, half))
        gx_ref[...] = total.astype(BF)

    if comm:

        @pl.when(s == 2 * n + m - 1)
        def _():
            for at_step, plan in TAIL_PLAN.items():
                if at_step >= m:
                    follow(plan)
            for name, piece in pieces.items():
                if name != "F":
                    piece.leave().wait()
            small_out[...] = acc[5]


def attn_bwd(comm, block, gone, goneT, xT, qkv, probs, att, wq, wo, sums):
    rows, d = gone.shape
    half, r = d // 2, block * LMAX
    n = rows // r
    rg = min(rows, 4 * LMAX)
    m = rows // rg
    sds = jax.ShapeDtypeStruct

    def blk(s):
        return jnp.where(s < 2 * n, lax.rem(s, n), n - 1)

    def rel(s):
        return jnp.where(s < n, 1, 0)

    def tail(s):
        return jnp.maximum(s - 2 * n, 0)

    in_specs = [
        pl.BlockSpec((r, d), lambda s: (blk(s), 0)),
        pl.BlockSpec((rg, d), lambda s: (tail(s), 0)),
        pl.BlockSpec((3, 1, r, half), lambda s: (0, rel(s), blk(s), 0)),
        pl.BlockSpec((block, 1, LMAX, half // HDIM * LMAX), lambda s: (blk(s), rel(s), 0, 0)),
        once(wq[0].shape), once(wq[1].shape), once(wo[0].shape), once(wo[1].shape), ANY, ANY, ANY,
    ]
    gx_spec, gx_shape = pl.BlockSpec((rg, d), lambda s: (tail(s), 0)), sds((rows, d), BF)
    scratch = [pltpu.VMEM((2, 3, rows, half), BF), pltpu.VMEM(xT.shape, BF), pltpu.VMEM(goneT.shape, BF),
               pltpu.VMEM(att.shape, BF), pltpu.SemaphoreType.DMA((5,))]
    params = dict(vmem_limit_bytes=VMEM_LIMIT)
    if comm:
        up, dn, small = sums
        hid = up.shape[-1]
        split = lambda w: (2, 2, 4, d // 16, w)
        in_specs += [ANY, ANY, once(small.shape)]
        out_specs = [gx_spec, ANY, ANY, ANY, ANY, once(small.shape)]
        out_shape = [gx_shape, sds(split(hid), BF), sds(split(hid), BF), sds(split(half), BF),
                     sds((3,) + split(half), BF), sds(small.shape, F32)]
        rows4 = d // 4
        scratch += [pltpu.VMEM((2, 2, 2, rows4, half), BF), pltpu.VMEM((3, 2, 2, rows4, half), BF),
                    pltpu.VMEM((3, 2, 2, rows4, half), BF), pltpu.VMEM((6,) + small.shape, F32),
                    pltpu.VMEM((5,) + small.shape, F32), pltpu.SemaphoreType.DMA((2, 96)),
                    pltpu.VMEM((2, 2, rows4, hid), BF), pltpu.VMEM((2, 2, rows4, hid), BF),
                    pltpu.SemaphoreType.DMA((8,))]
        for _ in range(4):
            scratch += reduce_bufs(hid // 2, "xy", rows4)
        scratch += reduce_bufs(half, "xy", rows4)
        for _ in range(3):
            scratch += reduce_own_bufs(half, rows4)
        params.update(collective_id=1, has_side_effects=True)
    else:
        out_specs = [gx_spec, once((2, d, half)), once((2, 3, d, half)), once((2, 8, d))]
        out_shape = [gx_shape, sds((2, d, half), BF), sds((2, 3, d, half), BF), sds((2, 8, d), F32)]
    return pl.pallas_call(
        functools.partial(attn_bwd_kernel, comm, n, m), grid=(2 * n + m,), in_specs=in_specs, out_specs=out_specs,
        out_shape=out_shape, scratch_shapes=scratch, compiler_params=pltpu.CompilerParams(**params),
        name="attention_backward",
    )(gone, gone, qkv, probs, *wq, *wo, xT, goneT, att, *sums)


def finish_kernel(gx_ref, up_ref, dn_ref, wo_ref, wq_ref, small_ref, gx_out, up_out, dn_out, wo_out, wq_out,
                  upb_out, qvb_out, *vec_outs):
    gx_out[...] = gx_ref[...]
    up_out[...] = up_ref[...].astype(F32)
    dn_out[...] = dn_ref[...].astype(F32).T
    wq_out[...] = wq_ref[...].astype(F32)

    @pl.when(pl.program_id(0) == 0)
    def _():
        d = small_ref.shape[2]
        half = d // 2
        wo_out[...] = wo_ref[...].astype(F32).T
        for k, out in enumerate(vec_outs):
            out[...] = small_ref[0, k]
        for k in range(upb_out.shape[0] // d):
            upb_out[k * d : (k + 1) * d] = small_ref[1, k]
        qvb_out[0:1, :] = small_ref[1, 2:3, 0:half]
        qvb_out[1:2, :] = small_ref[1, 2:3, half:d]


def finish(gx, up, dn, wo, wq, small):
    rows, d = gx.shape
    hid, half = up.shape[1], wo.shape[1]
    n = 2
    sds = jax.ShapeDtypeStruct
    gx_spec = pl.BlockSpec((rows // n, d), lambda i: (i, 0))
    up_spec = pl.BlockSpec((d // n, hid), lambda i: (i, 0))
    wq_spec = pl.BlockSpec((3, d // n, half), lambda i: (0, i, 0))
    return pl.pallas_call(
        finish_kernel, grid=(n,),
        in_specs=[gx_spec, up_spec, pl.BlockSpec((d, hid // n), lambda i: (0, i)), once(wo.shape), wq_spec,
                  once(small.shape)],
        out_specs=[gx_spec, up_spec, pl.BlockSpec((hid // n, d), lambda i: (i, 0)), once((half, d)), wq_spec,
                   once((hid,)), once((2, half))] + [once((d,))] * 6,
        out_shape=[sds(gx.shape, BF), sds(up.shape, F32), sds((hid, d), F32), sds((half, d), F32), sds(wq.shape, F32),
                   sds((hid,), F32), sds((2, half), F32)] + [sds((d,), F32)] * 6,
        compiler_params=pltpu.CompilerParams(vmem_limit_bytes=VMEM_LIMIT), name="finish",
    )(gx, up, dn, wo, wq, small)


def tile_rows(rows):
    for r in (512, 640, 320):
        if rows % r == 0:
            return r
    return LMAX


def chain_block(chains):
    for c in (4, 2):
        if chains % c == 0:
            return c
    return 1


def on_device(comm, tokens, qkv_weight, qv_bias, out_weight, out_bias, gain_one, shift_one, up_weight, up_bias,
              down_weight, down_bias, gain_two, shift_two, out_grad, lengths):
    rows, d = tokens.shape
    chains = rows // LMAX
    half = d // 2
    vecs = [a[None] for a in (gain_one, shift_one, down_bias, gain_two, shift_two)]
    block = chain_block(chains)
    comm = comm and chains == 16

    def gather(a, dim):
        return lax.all_gather(a, "tensor", axis=dim, tiled=True)

    def table(qv, up):
        flat = jnp.concatenate([qv[0], qv[1], up]).astype(F32)
        return jnp.pad(flat, (0, 4096 - flat.shape[0])).reshape(2, 2, 8, 128)

    if comm:
        hid = up_weight.shape[1]
        quarters = (
            qkv_weight.reshape(3, 2, 2, 2, d // 8, half), out_weight.reshape(2, half // 2, d),
            up_weight.reshape(2, 2, 2, d // 8, hid), down_weight.reshape(2, 2, 2, hid // 8, d), up_bias,
        )
        h1, qkv, att, probs, xT, wqb, wob, wupb, wdnb, bias_b, bias = attn_fwd(
            True, 2, lengths, tokens, qkv_weight, out_weight, qv_bias, out_bias[None], quarters)
        wqs, wos, bias = (qkv_weight, wqb), (out_weight, wob), (bias, bias_b)
        ups, dns = (up_weight, wupb.reshape(d, hid)), (down_weight, wdnb.reshape(hid, d))
    else:
        wq, wo = gather(qkv_weight, 2), gather(out_weight, 0)
        wup, wdn = gather(up_weight, 1), gather(down_weight, 0)
        hid = wup.shape[1] // 2
        qvb, upb = gather(qv_bias, 1), gather(up_bias, 0)
        bias = (table(qvb[:, :half], upb[:hid]), table(qvb[:, half:], upb[hid:]))
        wqs, wos = (wq[:, :, :half], wq[:, :, half:]), (wo[:half], wo[half:])
        ups, dns = (wup[:, :hid], wup[:, hid:]), (wdn[:hid], wdn[hid:])
        h1, qkv, att, probs, xT = attn_fwd(
            False, block, lengths, tokens, wqs[0], wos[0], bias[0], out_bias[None], (wqs[1], wos[1], bias[1]))
    out, gone, goneT, dup, ddn, small = ffn(tile_rows(rows), 256, lengths, h1, out_grad, ups, dns, bias, vecs)
    small_block = 2 if chains % 2 == 0 else 1
    if comm:
        split = (2, 2, 2, d // 4, hid)
        gx, dup, ddn, dwo, dwq, small = attn_bwd(
            True, small_block, gone, goneT, xT, qkv, probs, att, wqs, wos, (dup.reshape(split), ddn.reshape(split), small))
        gx, dup, ddn, dwo, dwq, dupb, dqvb, *vecs = finish(
            gx, dup.reshape(d, hid), ddn.reshape(d, hid), dwo.reshape(d, half), dwq.reshape(3, d, half), small)
    else:
        gx, dwo, dwq, dbias = attn_bwd(False, small_block, gone, goneT, xT, qkv, probs, att, wqs, wos, ())

        def total(a, dim):
            a = lax.psum_scatter(a.astype(BF), "tensor", scatter_dimension=dim, tiled=True)
            return lax.psum(a, "dp").astype(F32)

        dwq = total(dwq.transpose(1, 2, 0, 3).reshape(3, d, d), 2)
        dwo = total(jnp.concatenate([dwo[0], dwo[1]], axis=1), 1).T
        dup = total(jnp.concatenate([dup[0], dup[1]], axis=1), 1)
        ddn = total(jnp.concatenate([ddn[0], ddn[1]], axis=1), 1).T
        dupb = total(small[1:, : hid // d].reshape(2 * hid), 0)
        dqvb = total(dbias[:, 2].reshape(2, 2, half).transpose(1, 0, 2).reshape(2, d), 1)
        vecs = lax.psum(small[0], ("dp", "tensor"))
    return (out, gx, dwq, dqvb, dwo, vecs[0], vecs[1], vecs[2], dup, dupb, ddn, vecs[3], vecs[4], vecs[5])


def solution(mesh):
    comm = mesh.shape["dp"] == 16 and mesh.shape["tensor"] == 2
    rows = P(("dp", "tensor"), None)
    in_specs = (rows, P(None, None, "tensor"), P(None, "tensor"), P("tensor", None), P(), P(), P(), P(None, "tensor"),
                P("tensor"), P("tensor", None), P(), P(), P(), rows, P("dp"))
    out_specs = (rows, rows, P(None, None, "tensor"), P(None, "tensor"), P("tensor", None), P(), P(), P(),
                 P(None, "tensor"), P("tensor"), P("tensor", None), P(), P(), P())
    return jax.shard_map(functools.partial(on_device, comm), mesh=mesh, in_specs=in_specs, out_specs=out_specs,
                         check_vma=False)
```
